32 devices in a mesh: layer: 2 (over x), tile: 16 (over z, y, core).
Axes of the slice: x: 2, y: 2, z: 4, core: 2. Of those that a mesh axis runs over, the one named last changes fastest.
Arguments:
- incident: bfloat16 [2, 32768, 128], P(None, 'tile'), may hold values from -6 to 6
- sources: bfloat16 [2, 2, 32768, 128], P('layer', None, 'tile'), may hold values from -6 to 6
- green_tiles: bfloat16 [2, 192, 2, 256, 256], P('layer', 'tile'), may hold values from -0.1875 to 0.1875
- tile_rows: int32 [2, 192], P('layer', 'tile'), may hold values from 0 to 127, as said below
- tile_cols: int32 [2, 192], P('layer', 'tile'), may hold values from 0 to 7, as said below
- tile_count: int32 [2, 16], P('layer', 'tile'), may hold values from 1 to 12, 144 in all within a row
Outputs:
- traces: bfloat16 [2, 2, 32768, 128], P('layer', None, 'tile')
The draws below stay inside these ranges and needn't reach their ends.
Inputs may be any that keep to these rules, and one draw needn't show every extreme that they name: `tile_rows`: slot i of a layer belongs to tile device d = i // 12; its row block lies among the row blocks held by devices d - 1, d and d + 1, where row block r is held by device r // 8; in every layer some live slot writes to the first row block of the device on its left and some to the last of the device on its right. `tile_cols`: the column block is counted among the 8 row blocks held by the slot's own device. `tile_count`: A device's live slots are its first ones; each layer group has 9 * 16 live slots in all.
All inputs are finite; a program needn't handle non-finite values.
Results may differ from the reference program's by a relative error of at most 0.0095.
Values may be sent and summed in bfloat16 or wider, within the bound.
No kernel may reach another device: no remote copies, remote signals or barrier semaphores. Data moves between devices by JAX's collectives and lax.ppermute only.
A program may use at most 64 MiB of HBM per device.

```python
import math
import jax
import jax.numpy as jnp
import numpy as np
from jax import lax

NI = 32768
TB = 256
TILES_DEV = 12
SRC = 64
FRONTS = 2
LAYERS = 2
BLK_DEV = 8
N_TILE = 16


def slot_pairs(key):
    nblock = NI // TB
    blocks_dev = nblock // N_TILE
    slot_total = N_TILE * TILES_DEV
    choices_all = 3 * blocks_dev * blocks_dev
    inner = jax.random.fold_in(key, 4711)
    keys = jax.random.split(inner, LAYERS * N_TILE)
    orders = jax.vmap(lambda kk: jax.random.permutation(kk, choices_all))(keys)
    picked = orders[:, :TILES_DEV].astype(jnp.int32).reshape(LAYERS, slot_total)
    slots = jnp.arange(slot_total, dtype=jnp.int32)
    owner = slots // TILES_DEV
    window_row = picked // blocks_dev
    columns = picked % blocks_dev
    rows = (owner[None, :] - 1) * blocks_dev + window_row
    rows = jnp.where(rows < 0, rows + blocks_dev, rows)
    rows = jnp.where(rows >= nblock, rows - blocks_dev, rows)
    rows = jnp.where(slots[None, :] == TILES_DEV, 0, rows)
    rows = jnp.where(slots[None, :] == (N_TILE - 2) * TILES_DEV, nblock - 1, rows)
    return (rows.astype(jnp.int32), columns.astype(jnp.int32))


def draw_tile_rows(key, part):
    rows, columns = slot_pairs(key)
    return rows


def draw_tile_cols(key, part):
    rows, columns = slot_pairs(key)
    return columns


def shard_levels(stream_key, dims, cuts, smallest, top_value):
    loudness, own = 1.0, jax.random.fold_in(stream_key, 6)
    for dim, parts in cuts:
        steps = jnp.exp(jax.random.uniform(jax.random.fold_in(own, dim), (parts,), jnp.float32, smallest / len(cuts), top_value / len(cuts)))
        loudness = loudness * jnp.repeat(steps, dims[dim] // parts).reshape([-1 if axis == dim else 1 for axis in range(len(dims))])
    return loudness


def profile(amount, total, bound, lean):
    weights = [(1 << 20) // math.isqrt(standing ** lean) + 1 for standing in range(2, amount + 1)]
    rest, given = total - bound - (amount - 1), [1] * (amount - 1)
    while rest > 0:
        free = [i for i in range(amount - 1) if given[i] < bound]
        whole, left = sum([weights[i] for i in free]), rest
        for i in free:
            addition = min(bound - given[i], max(1, left * weights[i] // whole), rest)
            given[i] = given[i] + addition
            rest = rest - addition
    return np.array([bound] + given)


def uneven(own_key, count, total, limit, skew):
    if count == 2:
        one = jax.random.randint(own_key, (), max(1, total - limit), min(limit, total - 1) + 1)
        return jnp.stack([one, total - one])
    lengths = jnp.asarray(profile(count, total, limit, skew), jnp.int32)
    couples = (count - 1) // 2
    source_of, receiver = lengths[1:1 + 2 * couples:2], lengths[2:2 + 2 * couples:2]
    room = jnp.minimum(source_of - 1, limit - receiver)
    passed = jax.random.randint(jax.random.fold_in(own_key, 1), (couples,), 0, 1 << 20) % (room + 1)
    lengths = lengths.at[1:1 + 2 * couples:2].set(source_of - passed).at[2:2 + 2 * couples:2].set(receiver + passed)
    return lengths[jax.random.permutation(jax.random.fold_in(own_key, 2), count)]


def normal_values(own_key, extent, deviation, limit, cuts=(), kind=jnp.bfloat16):
    drawn = jax.random.normal(own_key, extent, jnp.float32) * deviation
    if len(cuts) > 0:
        drawn = shard_levels(own_key, extent, cuts, -0.22, 0.18) * drawn
    return jnp.clip(drawn, min=-limit, max=limit).astype(kind)


def setup_inputs(seed: int = 0) -> dict:
    splits = jax.random.split(jax.random.key(seed), 7)
    return {
        "incident": normal_values(splits[0], (FRONTS, NI, 2 * SRC), 1.0, 6.0, ((1, 16),)),
        "sources": normal_values(splits[1], (LAYERS, FRONTS, NI, 2 * SRC), 1.0, 6.0, ((0, 2), (2, 16))),
        "green_tiles": normal_values(splits[2], (LAYERS, N_TILE * TILES_DEV, 2, TB, TB), (36 * TB // BLK_DEV) ** -0.5, 0.1875, ((0, 2), (1, 16))),
        "tile_rows": draw_tile_rows(jax.random.fold_in(splits[6], 71), 0),
        "tile_cols": draw_tile_cols(jax.random.fold_in(splits[6], 71), 0),
        "tile_count": jax.vmap(lambda own: uneven(own, N_TILE, 9 * N_TILE, TILES_DEV, 2))(jax.random.split(splits[5], LAYERS)).reshape((LAYERS, N_TILE)).astype(jnp.int32),
    }


def reference(incident, sources, green_tiles, tile_rows, tile_cols, tile_count):
    nblock = NI // TB
    blocks_dev = nblock // N_TILE
    slot_total = N_TILE * TILES_DEV
    owner = jnp.arange(slot_total, dtype=jnp.int32) // TILES_DEV
    within = jnp.arange(slot_total, dtype=jnp.int32) % TILES_DEV
    width = 2 * SRC
    trace = incident
    results = []
    for layer_index in range(LAYERS):
        blocks = trace.astype(jnp.float32).reshape(FRONTS, nblock, TB, width)
        column = (owner * blocks_dev + tile_cols[layer_index]).astype(jnp.int32)
        picked = blocks[:, column]
        swapped = jnp.concatenate([-picked[..., SRC:], picked[..., :SRC]], axis=-1)
        stacked = jnp.stack([picked, swapped], axis=2)
        tiles = green_tiles[layer_index].astype(jnp.float32)
        terms = jnp.einsum("tcab,ftcbs->ftas", tiles, stacked, precision=lax.Precision.HIGHEST)
        active = within < tile_count[layer_index][owner]
        terms = terms * active.astype(jnp.float32)[None, :, None, None]
        row_block = tile_rows[layer_index].astype(jnp.int32)
        offset = row_block // blocks_dev - owner
        total = jnp.zeros((FRONTS, nblock, TB, width), jnp.float32)
        own_terms = jnp.where((offset == 0)[None, :, None, None], terms, jnp.float32(0.0))
        total = total.at[:, row_block].add(own_terms)
        for side in (-1, 1):
            chosen = jnp.where((offset == side)[None, :, None, None], terms, jnp.float32(0.0))
            partial_sum = jnp.zeros((FRONTS, nblock, TB, width), jnp.float32).at[:, row_block].add(chosen)
            rounded = lax.optimization_barrier(partial_sum.astype(jnp.bfloat16))
            total = total + rounded.astype(jnp.float32)
        total = total.reshape(FRONTS, NI, width) + sources[layer_index].astype(jnp.float32)
        trace = total.astype(jnp.bfloat16)
        results.append(trace)
    return jnp.stack(results)
```

```python
import functools

import jax
import jax.numpy as jnp
from jax import lax
from jax.experimental import pallas as pl
from jax.experimental.pallas import tpu as pltpu
from jax.sharding import PartitionSpec as P

MIB = 1 << 20


def exchange_routes(devices):
    inner = [(i, i ^ 1) for i in range(devices)]
    outer = [(i, (i + 1 if i % 2 else i - 1) % devices) for i in range(devices)]
    return inner, outer


def down_route(depth):
    return [(i, (i + 1) % depth) for i in range(depth)]


def product_kernel(wave, pieces, rows_dev, tile_size, *refs):
    row_ref, col_ref, count_ref = refs[:3]
    inbound = refs[3 : 3 + pieces]
    source_ref, tiles_ref, own_ref, inner_ref = refs[3 + pieces : 7 + pieces]
    outer_refs = refs[7 + pieces : 9 + pieces]
    slots, direct, turned, sums, sems = refs[9 + pieces :]
    blocks = rows_dev // tile_size
    width = own_ref.shape[-1]
    half = width // 2
    place = lax.axis_index("tile")

    @pl.when(lax.axis_index("layer") == wave)
    def _():
        count = count_ref[0, 0]

        def fetch(i):
            return pltpu.make_async_copy(tiles_ref.at[0, i], slots.at[i], sems.at[i])

        @pl.loop(0, count)
        def _(i):
            fetch(i).start()

        sums[pl.ds(0, rows_dev), :] = jnp.zeros((rows_dev, width), jnp.float32)
        sums[pl.ds(rows_dev, rows_dev), :] = source_ref[...].reshape(rows_dev, width).astype(jnp.float32)
        sums[pl.ds(2 * rows_dev, rows_dev), :] = jnp.zeros((rows_dev, width), jnp.float32)
        per_piece = rows_dev // pieces
        lane = lax.broadcasted_iota(jnp.int32, (per_piece, width), 1)
        for j, piece in enumerate(inbound):
            value = piece[...].reshape(per_piece, width)
            rows = pl.ds(j * per_piece, per_piece)
            direct[rows, :] = value
            moved = pltpu.roll(value.astype(jnp.float32), half, 1)
            turned[rows, :] = jnp.where(lane < half, -moved, moved).astype(jnp.bfloat16)

        first = (place - 1) * blocks

        @pl.loop(0, count)
        def _(i):
            fetch(i).wait()
            column = pl.ds(pl.multiple_of(col_ref[0, i] * tile_size, tile_size), tile_size)
            target = pl.ds(pl.multiple_of((row_ref[0, i] - first) * tile_size, tile_size), tile_size)
            term = jnp.dot(slots[i, 0], direct[column, :], preferred_element_type=jnp.float32)
            term += jnp.dot(slots[i, 1], turned[column, :], preferred_element_type=jnp.float32)
            sums[target, :] += term

        odd = lax.rem(place, 2)
        inner_start = pl.multiple_of((1 - odd) * 2 * rows_dev, tile_size)
        outer_start = pl.multiple_of(odd * 2 * rows_dev, tile_size)
        portion = rows_dev // 2
        for j, outer_ref in enumerate(outer_refs):
            outer_ref[...] = sums[pl.ds(outer_start + j * portion, portion), :].astype(jnp.bfloat16)
        inner_ref[...] = sums[pl.ds(inner_start, rows_dev), :].astype(jnp.bfloat16)
        own_ref[...] = sums[pl.ds(rows_dev, rows_dev), :]


def products(wave, front, inbound, sources, tiles, tile_rows, tile_cols, tile_count):
    rows_dev, width = sources.shape[-2:]
    slots = tiles.shape[1]
    tile_size = tiles.shape[-1]
    smem = pl.BlockSpec(memory_space=pltpu.SMEM)
    vmem = pl.BlockSpec(memory_space=pltpu.VMEM)
    if wave == 0:
        pieces = [inbound]
        piece_specs = [pl.BlockSpec((1, rows_dev, width), lambda i: (front, 0, 0))]
    else:
        pieces = list(inbound)
        piece_specs = [vmem] * len(pieces)
    portion = jax.ShapeDtypeStruct((rows_dev // 2, width), jnp.bfloat16)
    return pl.pallas_call(
        functools.partial(product_kernel, wave, len(pieces), rows_dev, tile_size),
        grid=(1,),
        out_shape=(
            jax.ShapeDtypeStruct((rows_dev, width), jnp.float32),
            jax.ShapeDtypeStruct((rows_dev, width), jnp.bfloat16),
            portion,
            portion,
        ),
        in_specs=[smem, smem, smem]
        + piece_specs
        + [
            pl.BlockSpec((1, 1, rows_dev, width), lambda i: (0, front, 0, 0)),
            pl.BlockSpec(memory_space=pl.ANY),
        ],
        out_specs=(vmem, vmem, vmem, vmem),
        scratch_shapes=[
            pltpu.VMEM((slots, 2, tile_size, tile_size), jnp.bfloat16),
            pltpu.VMEM((rows_dev, width), jnp.bfloat16),
            pltpu.VMEM((rows_dev, width), jnp.bfloat16),
            pltpu.VMEM((3 * rows_dev, width), jnp.float32),
            pltpu.SemaphoreType.DMA((slots,)),
        ],
        compiler_params=pltpu.CompilerParams(vmem_limit_bytes=24 * MIB),
        cost_estimate=pl.CostEstimate(flops=2 * 10**9, bytes_accessed=6 * 10**6, transcendentals=0),
        name=f"products_{wave}_{front}",
    )(tile_rows, tile_cols, tile_count, *pieces, sources, tiles)


def combine_kernel(wave, own_ref, inner_ref, outer_ref, *refs):
    out_ref = refs[-1]
    total = own_ref[...] + inner_ref[...].astype(jnp.float32) + outer_ref[...].astype(jnp.float32)
    total = total.astype(jnp.bfloat16)
    if wave == 0:
        out_ref[...] = total.reshape(out_ref.shape)
    else:
        active = lax.axis_index("layer") == wave
        earlier = refs[0][...]
        out_ref[...] = jnp.where(active, total, earlier).reshape(out_ref.shape)


def combine(wave, front, part, own, inner, outer, earlier, result, final):
    portion, width = outer.shape
    vmem = pl.BlockSpec(memory_space=pltpu.VMEM)
    half_spec = pl.BlockSpec((portion, width), lambda i: (part, 0))
    args = [own, inner, outer]
    specs = [half_spec, half_spec, vmem]
    if wave > 0:
        args.append(earlier)
        specs.append(vmem)
    aliases = {}
    if final:
        fronts = final
        out_shape = jax.ShapeDtypeStruct((1, fronts, 2 * portion, width), jnp.bfloat16)
        out_spec = pl.BlockSpec((1, 1, portion, width), lambda i: (0, front, part, 0))
        if result is not None:
            aliases = {len(args): 0}
            args.append(result)
            specs.append(pl.BlockSpec(memory_space=pl.ANY))
    else:
        out_shape = jax.ShapeDtypeStruct((portion, width), jnp.bfloat16)
        out_spec = vmem
    return pl.pallas_call(
        functools.partial(combine_kernel, wave),
        grid=(1,),
        out_shape=out_shape,
        in_specs=specs,
        out_specs=out_spec,
        input_output_aliases=aliases,
        compiler_params=pltpu.CompilerParams(vmem_limit_bytes=8 * MIB),
        cost_estimate=pl.CostEstimate(flops=10**6, bytes_accessed=2 * 10**6, transcendentals=0),
        name=f"combine_{wave}_{front}_{part}",
    )(*args)


def shards(incident, sources, green_tiles, tile_rows, tile_cols, tile_count):
    depth = lax.axis_size("layer")
    inner_route, outer_route = exchange_routes(lax.axis_size("tile"))
    layer_route = down_route(depth)
    fronts = incident.shape[0]
    index = (tile_rows, tile_cols, tile_count)
    inbound = [incident] * fronts
    earlier = [[None, None] for _ in range(fronts)]
    result = None
    for wave in range(depth):
        final = wave == depth - 1
        made = []
        for front in range(fronts):
            own, inner, low, high = products(
                wave, front, inbound[front], sources, green_tiles, *index
            )
            low = lax.ppermute(low, "tile", outer_route)
            high = lax.ppermute(high, "tile", outer_route)
            inner = lax.ppermute(inner, "tile", inner_route)
            made.append((own, inner, (low, high)))
        for front, (own, inner, outer) in enumerate(made):
            for part in range(2):
                out = combine(
                    wave, front, part, own, inner, outer[part], earlier[front][part], result, final and fronts
                )
                if final:
                    result = out
                else:
                    earlier[front][part] = out
        if not final:
            inbound = [[lax.ppermute(p, "layer", layer_route) for p in earlier[f]] for f in range(fronts)]
    return result


def solution(mesh):
    return jax.shard_map(
        shards,
        mesh=mesh,
        in_specs=(
            P(None, "tile", None),
            P("layer", None, "tile", None),
            P("layer", "tile", None, None, None),
            P("layer", "tile"),
            P("layer", "tile"),
            P("layer", "tile"),
        ),
        out_specs=P("layer", None, "tile", None),
        check_vma=False,
    )
```

```python
import functools

import jax
import jax.numpy as jnp
from jax import lax
from jax.experimental import pallas as pl
from jax.experimental.pallas import tpu as pltpu
from jax.sharding import PartitionSpec as P

MIB = 1 << 20
VMEM = pl.BlockSpec(memory_space=pltpu.VMEM)
HBM = pl.BlockSpec(memory_space=pltpu.HBM)
SMEM = pl.BlockSpec(memory_space=pltpu.SMEM)


def exchange_routes(devices):
    inner = [(i, i ^ 1) for i in range(devices)]
    outer = [(i, (i + 1 if i % 2 else i - 1) % devices) for i in range(devices)]
    return inner, outer


def down_route(depth):
    return [(i, (i + 1) % depth) for i in range(depth)]


def outer_side():
    return 2 * lax.rem(lax.axis_index("tile"), 2) - 1


def multiply(tiles, pair, i, column, tile_size):
    rows = pl.ds(pl.multiple_of(column * tile_size, tile_size), tile_size)
    term = jnp.dot(tiles[i, 0], pair[0, rows, :], preferred_element_type=jnp.float32)
    return term + jnp.dot(tiles[i, 1], pair[1, rows, :], preferred_element_type=jnp.float32)


def outward_kernel(wave, front, blocks, first, *refs):
    index_refs, inbound_ref = refs[:3], refs[3]
    refs = refs[5:]
    if first:
        stored_tiles, near_ref, far_ref, pair, header_ref, tiles = refs[:6]
        refs = refs[6:]
    else:
        tiles, near_ref, far_ref, pair = refs[:4]
        refs = refs[4:]
    rows_s, cols_s, slot_s, sums, index_sems, inbound_sem, tile_sems = refs
    slots = tiles.shape[0]
    tile_size = tiles.shape[-1]
    rows_dev, width = pair.shape[1:]
    half = width // 2
    index_copies = [
        pltpu.make_async_copy(src, dst, index_sems.at[j])
        for j, (src, dst) in enumerate(zip(index_refs[:2], (rows_s, cols_s)))
    ]
    active = lax.axis_index("layer") == wave

    def tile_copy(i):
        return pltpu.make_async_copy(stored_tiles.at[0, i], tiles.at[i], tile_sems.at[i])

    inbound_copy = pltpu.make_async_copy(
        inbound_ref.at[front] if wave == 0 else inbound_ref, pair.at[0], inbound_sem
    )
    for copy in index_copies:
        copy.start()
    inbound_copy.start()
    if first:
        for i in range(slots):
            tile_copy(i).start()
    for copy in index_copies:
        copy.wait()
    count = index_refs[2][0, 0]
    place = lax.axis_index("tile")
    side = outer_side()
    for r in range(blocks):
        slot_s[r] = -1

    def outward(i):
        return lax.div(rows_s[0, i], blocks) == place + side

    def assign(i, used):
        row = lax.rem(rows_s[0, i], blocks)
        fresh = outward(i) & (slot_s[row] < 0)

        @pl.when(fresh)
        def _():
            slot_s[row] = used

        return used + fresh.astype(jnp.int32)

    used = lax.fori_loop(0, count, assign, jnp.int32(0))
    if first:
        lane = lax.broadcasted_iota(jnp.int32, header_ref.shape, 1)
        header = jnp.where(lane == blocks, used, -1)
        for r in range(blocks):
            header = jnp.where(lane == r, slot_s[r], header)
        header_ref[...] = header
    inbound_copy.wait()

    @pl.when(active)
    def _():
        @pl.loop(0, used)
        def _(j):
            block = pl.ds(pl.multiple_of(j * tile_size, tile_size), tile_size)
            sums[block, :] = jnp.zeros((tile_size, width), jnp.float32)

        moved = pltpu.roll(pair[0].astype(jnp.float32), half, 1)
        lane = lax.broadcasted_iota(jnp.int32, (rows_dev, width), 1)
        pair[1] = jnp.where(lane < half, -moved, moved).astype(jnp.bfloat16)

    @pl.loop(0, slots)
    def _(i):
        if first:
            tile_copy(i).wait()

        @pl.when(active & (i < count) & outward(i))
        def _():
            slot = slot_s[lax.rem(rows_s[0, i], blocks)]
            target = pl.ds(pl.multiple_of(slot * tile_size, tile_size), tile_size)
            sums[target, :] += multiply(tiles, pair, i, cols_s[0, i], tile_size)

    near = near_ref.shape[0] // tile_size

    @pl.when(active)
    def _():
        @pl.loop(0, jnp.minimum(used, near))
        def _(j):
            block = pl.ds(pl.multiple_of(j * tile_size, tile_size), tile_size)
            near_ref[block, :] = sums[block, :].astype(jnp.bfloat16)

        @pl.loop(near, jnp.maximum(used, near))
        def _(j):
            block = pl.ds(pl.multiple_of(j * tile_size, tile_size), tile_size)
            there = pl.ds(pl.multiple_of((j - near) * tile_size, tile_size), tile_size)
            far_ref[there, :] = sums[block, :].astype(jnp.bfloat16)


def in_hbm(array):
    return pltpu.with_memory_space_constraint(array, pltpu.HBM)


def outward(wave, front, inbound, after, tiles, held, blocks, index):
    rows_dev, width = inbound.shape[-2:]
    slots, _, tile_size, _ = tiles.shape[-4:]
    first = held is None
    near = max(1, blocks // 2)
    shape = pltpu.VMEM
    outs = [
        shape((near * tile_size, width), jnp.bfloat16),
        shape(((blocks - near) * tile_size, width), jnp.bfloat16),
        shape((2, rows_dev, width), jnp.bfloat16),
    ]
    if first:
        outs += [shape((8, 128), jnp.int32), shape((slots, 2, tile_size, tile_size), jnp.bfloat16)]
    return pl.pallas_call(
        functools.partial(outward_kernel, wave, front, blocks, first),
        out_shape=outs,
        in_specs=[HBM, HBM, SMEM, HBM if wave == 0 else VMEM]
        + [HBM if wave == 0 and front == 0 else pl.BlockSpec(memory_space=pl.ANY), HBM if first else VMEM],
        out_specs=[VMEM] * len(outs),
        scratch_shapes=[
            pltpu.SMEM((1, slots), jnp.int32),
            pltpu.SMEM((1, slots), jnp.int32),
            pltpu.SMEM((blocks,), jnp.int32),
            pltpu.VMEM((rows_dev, width), jnp.float32),
            pltpu.SemaphoreType.DMA((2,)),
            pltpu.SemaphoreType.DMA(()),
            pltpu.SemaphoreType.DMA((slots,)),
        ],
        compiler_params=pltpu.CompilerParams(vmem_limit_bytes=16 * MIB),
        cost_estimate=pl.CostEstimate(flops=5 * 10**8, bytes_accessed=4 * 10**6, transcendentals=0),
        name=f"outward_{wave}_{front}",
    )(*index, inbound, after, tiles if first else held)


def inward_kernel(wave, front, blocks, *refs):
    index_refs, (source_ref, tiles, pair, own_ref, inner_ref) = refs[:3], refs[3:8]
    rows_s, cols_s, source_v, sums, index_sems, source_sem = refs[8:]
    tile_size = tiles.shape[-1]
    rows_dev, width = pair.shape[1:]

    @pl.when(lax.axis_index("layer") == wave)
    def _():
        source_copy = pltpu.make_async_copy(source_ref.at[0, front], source_v, source_sem)
        index_copies = [
            pltpu.make_async_copy(src, dst, index_sems.at[j])
            for j, (src, dst) in enumerate(zip(index_refs[:2], (rows_s, cols_s)))
        ]
        for copy in index_copies:
            copy.start()
        source_copy.start()
        sums[...] = jnp.zeros(sums.shape, jnp.float32)
        for copy in index_copies:
            copy.wait()
        place = lax.axis_index("tile")
        side = outer_side()

        @pl.loop(0, index_refs[2][0, 0])
        def _(i):
            row = rows_s[0, i]
            offset = lax.div(row, blocks) - place

            @pl.when(offset != side)
            def _():
                start = jnp.where(offset == 0, 0, rows_dev) + lax.rem(row, blocks) * tile_size
                target = pl.ds(pl.multiple_of(start, tile_size), tile_size)
                sums[target, :] += multiply(tiles, pair, i, cols_s[0, i], tile_size)

        inner_ref[...] = sums[pl.ds(rows_dev, rows_dev), :].astype(jnp.bfloat16)
        source_copy.wait()
        own_ref[...] = sums[pl.ds(0, rows_dev), :] + source_v[...].astype(jnp.float32)


def inward(wave, front, pair, sources, held, blocks, index):
    rows_dev, width = pair.shape[1:]
    slots = held.shape[0]
    return pl.pallas_call(
        functools.partial(inward_kernel, wave, front, blocks),
        out_shape=(
            pltpu.VMEM((rows_dev, width), jnp.float32),
            pltpu.VMEM((rows_dev, width), jnp.bfloat16),
        ),
        in_specs=[HBM, HBM, SMEM, HBM, VMEM, VMEM],
        out_specs=(VMEM, VMEM),
        scratch_shapes=[
            pltpu.SMEM((1, slots), jnp.int32),
            pltpu.SMEM((1, slots), jnp.int32),
            pltpu.VMEM((rows_dev, width), jnp.bfloat16),
            pltpu.VMEM((2 * rows_dev, width), jnp.float32),
            pltpu.SemaphoreType.DMA((2,)),
            pltpu.SemaphoreType.DMA(()),
        ],
        compiler_params=pltpu.CompilerParams(vmem_limit_bytes=16 * MIB),
        cost_estimate=pl.CostEstimate(flops=10**9, bytes_accessed=4 * 10**6, transcendentals=0),
        name=f"inward_{wave}_{front}",
    )(*index, sources, held, pair)


def combine_kernel(wave, blocks, header_ref, own_ref, inner_ref, near_ref, far_ref, *refs):
    out_ref = refs[-1]
    rows_dev, width = own_ref.shape
    tile_size = rows_dev // blocks
    near = near_ref.shape[0] // tile_size

    def store(rows, value):
        if len(out_ref.shape) == 2:
            out_ref[rows, :] = value
        else:
            out_ref[0, 0, rows, :] = value

    def work():
        for r in range(blocks):
            rows = pl.ds(r * tile_size, tile_size)
            total = own_ref[rows, :] + inner_ref[rows, :].astype(jnp.float32)
            slot = header_ref[0, r]
            store(rows, total.astype(jnp.bfloat16))
            for low, ref in ((0, near_ref), (near, far_ref)):
                here = slot - low

                @pl.when((here >= 0) & (here < ref.shape[0] // tile_size))
                def _():
                    block = pl.ds(pl.multiple_of(here * tile_size, tile_size), tile_size)
                    store(rows, (total + ref[block, :].astype(jnp.float32)).astype(jnp.bfloat16))

    if wave == 0:
        work()
    else:
        active = lax.axis_index("layer") == wave
        pl.when(active)(work)

        @pl.when(jnp.logical_not(active))
        def _():
            store(pl.ds(0, rows_dev), refs[0][...])


def combine(wave, front, blocks, header, own, inner, near, far, earlier, result, fronts):
    rows_dev, width = own.shape
    args = [header, own, inner, near, far]
    specs = [SMEM] + [VMEM] * 4
    aliases, grid = {}, None
    if wave > 0:
        args.append(earlier)
        specs.append(VMEM)
    if fronts:
        grid = (1,)
        out_shape = jax.ShapeDtypeStruct((1, fronts, rows_dev, width), jnp.bfloat16)
        out_spec = pl.BlockSpec((1, 1, rows_dev, width), lambda i: (0, front, 0, 0))
        if result is not None:
            aliases = {len(args): 0}
            args.append(result)
            specs.append(pl.BlockSpec(memory_space=pl.ANY))
    else:
        out_shape = pltpu.VMEM((rows_dev, width), jnp.bfloat16)
        out_spec = VMEM
    return pl.pallas_call(
        functools.partial(combine_kernel, wave, blocks),
        **({"grid": grid} if grid else {}),
        out_shape=out_shape,
        in_specs=specs,
        out_specs=out_spec,
        input_output_aliases=aliases,
        compiler_params=pltpu.CompilerParams(vmem_limit_bytes=8 * MIB),
        cost_estimate=pl.CostEstimate(flops=10**6, bytes_accessed=2 * 10**6, transcendentals=0),
        name=f"combine_{wave}_{front}",
    )(*args)


def shards(incident, sources, green_tiles, tile_rows, tile_cols, tile_count):
    depth = lax.axis_size("layer")
    inner_route, outer_route = exchange_routes(lax.axis_size("tile"))
    layer_route = down_route(depth)
    fronts, rows_dev, _ = incident.shape
    blocks = rows_dev // green_tiles.shape[-1]
    near_blocks = max(1, blocks // 2)
    index = (in_hbm(tile_rows), in_hbm(tile_cols), tile_count)
    incident, sources, green_tiles = map(in_hbm, (incident, sources, green_tiles))
    inbound = [incident] * fronts
    earlier = [None] * fronts
    held = header = result = None
    after = index[0]
    for wave in range(depth):
        final = wave == depth - 1
        passed = []
        for front in range(fronts):
            made = outward(wave, front, inbound[front], after, green_tiles, held, blocks, index)
            near, far, pair = made[:3]
            near = lax.ppermute(near, "tile", outer_route)
            if held is None:
                sent, held = made[3:]
                header = lax.ppermute(sent, "tile", outer_route)
                wide = jnp.maximum(sent[0, blocks], header[0, blocks]) > near_blocks
            own, inner = inward(wave, front, pair, sources, held, blocks, index)
            inner = lax.ppermute(inner, "tile", inner_route)
            far = lax.cond(
                wide, lambda part: lax.ppermute(part, "tile", outer_route), lambda part: part, far
            )
            out = combine(
                wave, front, blocks, header, own, inner, near, far, earlier[front], result, final and fronts
            )
            if final:
                result = out
            else:
                earlier[front] = out
                after = out
                passed.append(lax.ppermute(out, "layer", layer_route))
        inbound = passed
    return result


def solution(mesh):
    return jax.shard_map(
        shards,
        mesh=mesh,
        in_specs=(
            P(None, "tile", None),
            P("layer", None, "tile", None),
            P("layer", "tile", None, None, None),
            P("layer", "tile"),
            P("layer", "tile"),
            P("layer", "tile"),
        ),
        out_specs=P("layer", None, "tile", None),
        check_vma=False,
    )
```

```python
import functools

import jax
import jax.numpy as jnp
from jax import lax
from jax.experimental import pallas as pl
from jax.experimental.pallas import tpu as pltpu
from jax.sharding import PartitionSpec as P

MIB = 1 << 20
VMEM = pl.BlockSpec(memory_space=pltpu.VMEM)
HBM = pl.BlockSpec(memory_space=pltpu.HBM)
SMEM = pl.BlockSpec(memory_space=pltpu.SMEM)
PARTS = 2


def exchange_routes(devices):
    inner = [(i, i ^ 1) for i in range(devices)]
    outer = [(i, (i + 1 if i % 2 else i - 1) % devices) for i in range(devices)]
    return inner, outer


def down_route(depth):
    return [(i, (i + 1) % depth) for i in range(depth)]


def in_hbm(array):
    return pltpu.with_memory_space_constraint(array, pltpu.HBM)


def quarters(shape):
    return lax.rem(lax.broadcasted_iota(jnp.int32, shape, 1), shape[1] // 2) < shape[1] // 4


def pack(block, part):
    rows, width = block.shape
    upper, lower = block[: rows // 2], block[rows // 2 :]
    if part == 0:
        lower = pltpu.roll(lower, width // 4, 1)
    else:
        upper = pltpu.roll(upper, width - width // 4, 1)
    return jnp.where(quarters(upper.shape), upper, lower)


def turn(value):
    half = value.shape[1] // 2
    moved = pltpu.roll(value, half, 1)
    lane = lax.broadcasted_iota(jnp.int32, value.shape, 1)
    return jnp.where(lane < half, -moved, moved)


def accumulate(index_refs, rows_s, cols_s, tiles, pair, sums, blocks, ready):
    tile_size = tiles.shape[-1]
    first = (lax.axis_index("tile") - 1) * blocks
    count = index_refs[2][0, 0]
    for i in range(tiles.shape[0]):
        ready(i)
        live = i < count
        row = jnp.where(live, rows_s[0, i] - first, 3 * blocks)
        column = jnp.where(live, cols_s[0, i], 0)
        rows = pl.ds(pl.multiple_of(column * tile_size, tile_size), tile_size)
        target = pl.ds(pl.multiple_of(row * tile_size, tile_size), tile_size)
        term = jnp.dot(tiles[i, 0], pair[0, rows, :], preferred_element_type=jnp.float32)
        term += jnp.dot(tiles[i, 1], pair[1, rows, :], preferred_element_type=jnp.float32)
        sums[target, :] += term


def side_starts(rows_dev):
    odd = lax.rem(lax.axis_index("tile"), 2)
    return (1 - odd) * 2 * rows_dev, odd * 2 * rows_dev


def read_block(sums, start, r, tile_size):
    return sums[pl.ds(pl.multiple_of(start + r * tile_size, tile_size), tile_size), :]


def front_kernel(front, blocks, *refs):
    index_refs, incident, sources = refs[:3], refs[3], refs[4]
    if front == 0:
        stored, outer_refs, inner_ref, own_refs, tiles = refs[5], refs[6:8], refs[8], refs[9:11], refs[11]
        rest = refs[12:]
    else:
        tiles, outer_refs, inner_ref, own_refs = refs[5], refs[7:9], refs[9], refs[10:12]
        rest = refs[13:]
    rows_s, cols_s, source_v, pair, sums, sems, tile_sems = rest
    slots, tile_size = tiles.shape[0], tiles.shape[-1]
    rows_dev = pair.shape[1]
    packed = rows_dev // 2

    def tile_copy(i):
        return pltpu.make_async_copy(stored.at[0, i], tiles.at[i], tile_sems.at[i])

    if front == 0:
        for i in range(slots):
            tile_copy(i).start()

    active = lax.axis_index("layer") == 0

    @pl.when(active)
    def _():
        copies = [
            pltpu.make_async_copy(index_refs[0], rows_s, sems.at[0]),
            pltpu.make_async_copy(index_refs[1], cols_s, sems.at[1]),
            pltpu.make_async_copy(incident.at[front], pair.at[0], sems.at[2]),
            pltpu.make_async_copy(sources.at[0, front], source_v, sems.at[3]),
        ]
        for copy in copies:
            copy.start()
        sums[...] = jnp.zeros(sums.shape, jnp.float32)
        for copy in copies[:3]:
            copy.wait()
        for r in range(blocks):
            rows = pl.ds(r * tile_size, tile_size)
            pair[1, rows, :] = turn(pair[0, rows, :].astype(jnp.float32)).astype(jnp.bfloat16)
        ready = (lambda i: tile_copy(i).wait()) if front == 0 else (lambda i: None)
        accumulate(index_refs, rows_s, cols_s, tiles, pair, sums, blocks, ready)
        inner_start, outer_start = side_starts(rows_dev)
        copies[3].wait()
        half = tile_size // 2
        for r in range(blocks):
            own = sums[pl.ds(rows_dev + r * tile_size, tile_size), :]
            own = own + source_v[pl.ds(r * tile_size, tile_size), :].astype(jnp.float32)
            inner = read_block(sums, inner_start, r, tile_size)
            outer = read_block(sums, outer_start, r, tile_size)
            for part in range(PARTS):
                rows = pl.ds(r * half, half)
                own_refs[part][rows, :] = pack(own, part)
                outer_refs[part][rows, :] = pack(outer, part).astype(jnp.bfloat16)
                inner_ref[pl.ds(part * packed + r * half, half), :] = pack(inner, part).astype(jnp.bfloat16)

    if front == 0:

        @pl.when(jnp.logical_not(active))
        def _():
            for i in range(slots):
                tile_copy(i).wait()


def scratch(slots, rows_dev, width, tile_size):
    return [
        pltpu.SMEM((1, slots), jnp.int32),
        pltpu.SMEM((1, slots), jnp.int32),
        pltpu.VMEM((rows_dev, width), jnp.bfloat16),
        pltpu.VMEM((2, rows_dev, width), jnp.bfloat16),
        pltpu.VMEM((3 * rows_dev + tile_size, width), jnp.float32),
        pltpu.SemaphoreType.DMA((4,)),
        pltpu.SemaphoreType.DMA((slots,)),
    ]


def kernel_options(name, flops, moved, limit=20):
    return dict(
        compiler_params=pltpu.CompilerParams(vmem_limit_bytes=limit * MIB),
        cost_estimate=pl.CostEstimate(flops=flops, bytes_accessed=moved, transcendentals=0),
        name=name,
    )


def front_products(front, incident, sources, tiles, index, blocks, through=None):
    rows_dev, width = incident.shape[-2:]
    slots, _, tile_size, _ = tiles.shape[-4:]
    packed = rows_dev // 2
    outer = pltpu.VMEM((packed, width), jnp.bfloat16)
    own = pltpu.VMEM((packed, width), jnp.float32)
    outs = [outer, outer, pltpu.VMEM((rows_dev, width), jnp.bfloat16), own, own]
    args, specs, aliases = [*index, incident, sources, tiles], [HBM, HBM, SMEM, HBM, HBM], {}
    if front == 0:
        specs.append(HBM)
        outs.append(pltpu.VMEM((slots, 2, tile_size, tile_size), jnp.bfloat16))
    else:
        specs += [VMEM, VMEM]
        aliases = {len(args): len(outs)}
        args.append(through)
        outs.append(outer)
    return pl.pallas_call(
        functools.partial(front_kernel, front, blocks),
        out_shape=outs,
        in_specs=specs,
        out_specs=[VMEM] * len(outs),
        scratch_shapes=scratch(slots, rows_dev, width, tile_size),
        input_output_aliases=aliases,
        **kernel_options(f"front_{front}", 10**9, 5 * 10**6),
    )(*args)


def chunk_kernel(wave, front, part, blocks, *refs):
    index_refs, (inbound, sources, tiles, outer_ref, inner_ref, own_ref) = refs[:3], refs[3:9]
    rows_s, cols_s, source_v, pair, sums, sems, tile_sems = refs[9:]
    tile_size = tiles.shape[-1]
    rows_dev, width = pair.shape[1:]
    half = tile_size // 2

    @pl.when(lax.axis_index("layer") == wave)
    def _():
        copies = [
            pltpu.make_async_copy(index_refs[0], rows_s, sems.at[0]),
            pltpu.make_async_copy(index_refs[1], cols_s, sems.at[1]),
            pltpu.make_async_copy(sources.at[0, front], source_v, sems.at[3]),
        ]
        for copy in copies:
            copy.start()
        sums[...] = jnp.zeros(sums.shape, jnp.float32)
        for r in range(blocks):
            upper = inbound[pl.ds(r * half, half), :].astype(jnp.float32)
            lower = pltpu.roll(upper, width - width // 4, 1)
            for j, value in enumerate((upper, lower)):
                rows = pl.ds(r * tile_size + j * half, half)
                pair[0, rows, :] = value.astype(jnp.bfloat16)
                pair[1, rows, :] = turn(value).astype(jnp.bfloat16)
        for copy in copies[:2]:
            copy.wait()
        accumulate(index_refs, rows_s, cols_s, tiles, pair, sums, blocks, lambda i: None)
        inner_start, outer_start = side_starts(rows_dev)
        copies[2].wait()
        for r in range(blocks):
            rows = pl.ds(r * half, half)
            outer_ref[rows, :] = pack(read_block(sums, outer_start, r, tile_size), 0).astype(jnp.bfloat16)
            inner_ref[rows, :] = pack(read_block(sums, inner_start, r, tile_size), 0).astype(jnp.bfloat16)
            source = source_v[pl.ds(r * tile_size, tile_size), :].astype(jnp.float32)
            own = sums[pl.ds(rows_dev + r * tile_size, tile_size), :]
            own_ref[rows, :] = pack(own, 0) + pack(source, part)


def chunk_products(wave, front, part, inbound, sources, tiles, index, blocks):
    rows_dev, width = sources.shape[-2:]
    slots, _, tile_size, _ = tiles.shape
    payload = pltpu.VMEM((rows_dev // 2, width), jnp.bfloat16)
    return pl.pallas_call(
        functools.partial(chunk_kernel, wave, front, part, blocks),
        out_shape=[payload, payload, pltpu.VMEM((rows_dev // 2, width), jnp.float32)],
        in_specs=[HBM, HBM, SMEM, VMEM, HBM, VMEM],
        out_specs=[VMEM] * 3,
        scratch_shapes=scratch(slots, rows_dev, width, tile_size),
        **kernel_options(f"chunk_{wave}_{front}_{part}", 10**9, 5 * 10**6),
    )(*index, inbound, sources, tiles)


def combine_kernel(wave, part, has_through, final, *refs):
    own_ref, inner_ref, outer_ref = refs[:3]
    packed, width = own_ref.shape
    out_ref = refs[-1] if not has_through else refs[-2]
    rows = pl.ds(part * packed if inner_ref.shape[0] > packed else 0, packed)
    total = own_ref[...] + inner_ref[rows, :].astype(jnp.float32) + outer_ref[...].astype(jnp.float32)
    if wave > 0:
        active = lax.axis_index("layer") == wave
        total = jnp.where(active, total, refs[3][...].astype(jnp.float32))
    if not (final and part == PARTS - 1):
        out_ref[...] = total.astype(jnp.bfloat16)
        return
    blocks, half = final
    low, high = refs[4][...].astype(jnp.float32), total
    first = quarters((half, width))
    for r in range(blocks):
        a, b = low[r * half : (r + 1) * half], high[r * half : (r + 1) * half]
        upper = jnp.where(first, a, pltpu.roll(b, width // 4, 1))
        lower = jnp.where(first, pltpu.roll(a, width - width // 4, 1), b)
        out_ref[0, 0, pl.ds(2 * r * half, half), :] = upper.astype(jnp.bfloat16)
        out_ref[0, 0, pl.ds((2 * r + 1) * half, half), :] = lower.astype(jnp.bfloat16)


def combine(wave, front, part, own, inner, outer, earlier=None, through=None, final=None, partner=None, result=None, fronts=0):
    packed, width = own.shape
    args, specs, aliases = [own, inner, outer], [VMEM] * 3, {}
    grid = {}
    if wave > 0:
        args.append(earlier)
        specs.append(VMEM)
    outs, out_specs = [pltpu.VMEM((packed, width), jnp.bfloat16)], [VMEM]
    if through is not None:
        aliases = {len(args): 1}
        args.append(through)
        specs.append(VMEM)
        outs.append(pltpu.VMEM(through.shape, through.dtype))
        out_specs.append(VMEM)
    if final and part == PARTS - 1:
        grid = {"grid": (1,)}
        args.append(partner)
        specs.append(VMEM)
        outs = [jax.ShapeDtypeStruct((1, fronts, 2 * packed, width), jnp.bfloat16)]
        out_specs = [pl.BlockSpec((1, 1, 2 * packed, width), lambda i: (0, front, 0, 0))]
        if result is not None:
            aliases = {len(args): 0}
            args.append(result)
            specs.append(pl.BlockSpec(memory_space=pl.ANY))
    return pl.pallas_call(
        functools.partial(combine_kernel, wave, part, through is not None, final),
        out_shape=outs,
        in_specs=specs,
        out_specs=out_specs,
        input_output_aliases=aliases,
        **grid,
        **kernel_options(f"combine_{wave}_{front}_{part}", 10**6, 10**6, 12),
    )(*args)


def shards(incident, sources, green_tiles, tile_rows, tile_cols, tile_count):
    depth = lax.axis_size("layer")
    inner_route, outer_route = exchange_routes(lax.axis_size("tile"))
    layer_route = down_route(depth)
    fronts, rows_dev, _ = incident.shape
    tile_size = green_tiles.shape[-1]
    blocks = rows_dev // tile_size
    index = (in_hbm(tile_rows), in_hbm(tile_cols), tile_count)
    incident, sources, green_tiles = map(in_hbm, (incident, sources, green_tiles))

    def across(payload, route=outer_route):
        return lax.ppermute(payload, "tile", route)

    def down(payload):
        return lax.ppermute(payload, "layer", layer_route)

    def finish(wave, chunks, earlier):
        result = None
        for front in range(fronts):
            partner = None
            for part in range(PARTS):
                own, inner, outer = chunks[front * PARTS + part]
                (out,) = combine(
                    wave, front, part, own, inner, outer, earlier[front * PARTS + part],
                    final=(blocks, tile_size // 2), partner=partner, result=result, fronts=fronts,
                )
                partner = out
            result = out
        return result

    queue, chunks, held = [], [], green_tiles
    waiting = None
    for front in range(fronts):
        made = front_products(front, incident, sources, held, index, blocks, waiting)
        if front == 0:
            held = made[5]
            waiting = made[1]
            outers = [across(made[0]), None]
        else:
            chunks[-1][2] = across(made[5])
            outers = [None, None]
            queue += [(len(chunks), made[0]), (len(chunks) + 1, made[1])]
        inner = across(made[2], inner_route)
        for part in range(PARTS):
            chunks.append([made[3 + part], inner, outers[part]])
        if front > 0 and front < fronts - 1:
            waiting = queue.pop()[1]
    if fronts == 1:
        chunks[-1][2] = across(waiting)
    passed, leaving = [], []
    for c, (own, inner, outer) in enumerate(chunks):
        through = queue[0][1] if queue else None
        made = combine(0, c // PARTS, c % PARTS, own, inner, outer, through=through)
        if queue:
            place, _ = queue.pop(0)
            chunks[place][2] = across(made[1])
        leaving.append(made[0])
        if depth > 1:
            passed.append(down(made[0]))
    for wave in range(1, depth):
        final = wave == depth - 1
        chunks = []
        for c, inbound in enumerate(passed):
            outer, inner, own = chunk_products(
                wave, c // PARTS, c % PARTS, inbound, sources, held, index, blocks
            )
            chunks.append((own, across(inner, inner_route), across(outer)))
        if final:
            return finish(wave, chunks, leaving)
        later = []
        for c, (own, inner, outer) in enumerate(chunks):
            later += combine(wave, c // PARTS, c % PARTS, own, inner, outer, leaving[c])
        leaving = later
        passed = [down(chunk) for chunk in leaving]


def solution(mesh):
    return jax.shard_map(
        shards,
        mesh=mesh,
        in_specs=(
            P(None, "tile", None),
            P("layer", None, "tile", None),
            P("layer", "tile", None, None, None),
            P("layer", "tile"),
            P("layer", "tile"),
            P("layer", "tile"),
        ),
        out_specs=P("layer", None, "tile", None),
        check_vma=False,
    )
```

```python
import functools

import jax
import jax.numpy as jnp
from jax import lax
from jax.experimental import pallas as pl
from jax.experimental.pallas import tpu as pltpu
from jax.sharding import PartitionSpec as P


MIB = 1 << 20
VMEM = pl.BlockSpec(memory_space=pltpu.VMEM)
HBM = pl.BlockSpec(memory_space=pltpu.HBM)
SMEM = pl.BlockSpec(memory_space=pltpu.SMEM)
PARTS = 2


def inner_route(devices):
    return [(i, i ^ 1) for i in range(devices)]


def outer_route(wave, devices):
    pairs = [(wave * devices + i, wave * devices + i + 1) for i in range(1, devices - 1, 2)]
    return pairs + [(b, a) for a, b in pairs]


def down_route(depth):
    return [(i, (i + 1) % depth) for i in range(depth)]


def in_hbm(array):
    return pltpu.with_memory_space_constraint(array, pltpu.HBM)


def quarters(shape):
    return lax.rem(lax.broadcasted_iota(jnp.int32, shape, 1), shape[1] // 2) < shape[1] // 4


def pack(block, part):
    rows, width = block.shape
    upper, lower = block[: rows // 2], block[rows // 2 :]
    if part == 0:
        lower = pltpu.roll(lower, width // 4, 1)
    else:
        upper = pltpu.roll(upper, width - width // 4, 1)
    return jnp.where(quarters(upper.shape), upper, lower)


def turn(value):
    half = value.shape[1] // 2
    moved = pltpu.roll(value, half, 1)
    lane = lax.broadcasted_iota(jnp.int32, value.shape, 1)
    return jnp.where(lane < half, -moved, moved)


def accumulate(index_refs, rows_s, cols_s, tiles, pair, sums, blocks, ready):
    tile_size = tiles.shape[-1]
    first = (lax.axis_index("tile") - 1) * blocks
    count = index_refs[2][0, 0]
    for i in range(tiles.shape[0]):
        ready(i)
        live = i < count
        row = jnp.where(live, rows_s[0, i] - first, 3 * blocks)
        column = jnp.where(live, cols_s[0, i], 0)
        rows = pl.ds(pl.multiple_of(column * tile_size, tile_size), tile_size)
        target = pl.ds(pl.multiple_of(row * tile_size, tile_size), tile_size)
        term = jnp.dot(tiles[i, 0], pair[0, rows, :], preferred_element_type=jnp.float32)
        term += jnp.dot(tiles[i, 1], pair[1, rows, :], preferred_element_type=jnp.float32)
        sums[target, :] += term


def side_starts(rows_dev):
    odd = lax.rem(lax.axis_index("tile"), 2)
    return (1 - odd) * 2 * rows_dev, odd * 2 * rows_dev


def read_block(sums, start, r, tile_size):
    return sums[pl.ds(pl.multiple_of(start + r * tile_size, tile_size), tile_size), :]


def front_kernel(front, blocks, *refs):
    index_refs, incident, sources = refs[:3], refs[3], refs[4]
    if front == 0:
        stored, outer_refs, inner_ref, own_refs, tiles = refs[5], refs[6:8], refs[8], refs[9:11], refs[11]
        rest = refs[12:]
    else:
        tiles, outer_refs, inner_ref, own_refs = refs[5], refs[7:9], refs[9], refs[10:12]
        rest = refs[13:]
    rows_s, cols_s, source_v, pair, sums, sems, tile_sems = rest
    slots, tile_size = tiles.shape[0], tiles.shape[-1]
    rows_dev = pair.shape[1]
    packed = rows_dev // 2

    def tile_copy(i):
        return pltpu.make_async_copy(stored.at[0, i], tiles.at[i], tile_sems.at[i])

    active = lax.axis_index("layer") == 0
    copies = [
        pltpu.make_async_copy(index_refs[0], rows_s, sems.at[0]),
        pltpu.make_async_copy(index_refs[1], cols_s, sems.at[1]),
        pltpu.make_async_copy(incident.at[front], pair.at[0], sems.at[2]),
        pltpu.make_async_copy(sources.at[0, front], source_v, sems.at[3]),
    ]

    @pl.when(active)
    def _():
        for copy in copies[:3]:
            copy.start()

    if front == 0:
        for i in range(slots):
            tile_copy(i).start()

    @pl.when(active)
    def _():
        copies[3].start()
        sums[...] = jnp.zeros(sums.shape, jnp.float32)
        for copy in copies[:3]:
            copy.wait()
        for r in range(blocks):
            rows = pl.ds(r * tile_size, tile_size)
            pair[1, rows, :] = turn(pair[0, rows, :].astype(jnp.float32)).astype(jnp.bfloat16)
        ready = (lambda i: tile_copy(i).wait()) if front == 0 else (lambda i: None)
        accumulate(index_refs, rows_s, cols_s, tiles, pair, sums, blocks, ready)
        inner_start, outer_start = side_starts(rows_dev)
        copies[3].wait()
        half = tile_size // 2
        for r in range(blocks):
            own = sums[pl.ds(rows_dev + r * tile_size, tile_size), :]
            own = own + source_v[pl.ds(r * tile_size, tile_size), :].astype(jnp.float32)
            inner = read_block(sums, inner_start, r, tile_size)
            outer = read_block(sums, outer_start, r, tile_size)
            for part in range(PARTS):
                rows = pl.ds(r * half, half)
                own_refs[part][rows, :] = pack(own, part)
                outer_refs[part][rows, :] = pack(outer, part).astype(jnp.bfloat16)
                inner_ref[pl.ds(part * packed + r * half, half), :] = pack(inner, part).astype(jnp.bfloat16)

    if front == 0:

        @pl.when(jnp.logical_not(active))
        def _():
            for i in range(slots):
                tile_copy(i).wait()


def scratch(slots, rows_dev, width, tile_size):
    return [
        pltpu.SMEM((1, slots), jnp.int32),
        pltpu.SMEM((1, slots), jnp.int32),
        pltpu.VMEM((rows_dev, width), jnp.bfloat16),
        pltpu.VMEM((2, rows_dev, width), jnp.bfloat16),
        pltpu.VMEM((3 * rows_dev + tile_size, width), jnp.float32),
        pltpu.SemaphoreType.DMA((4,)),
        pltpu.SemaphoreType.DMA((slots,)),
    ]


def kernel_options(name, flops, moved, limit=20):
    return dict(
        compiler_params=pltpu.CompilerParams(vmem_limit_bytes=limit * MIB),
        cost_estimate=pl.CostEstimate(flops=flops, bytes_accessed=moved, transcendentals=0),
        name=name,
    )


def front_products(front, incident, sources, tiles, index, blocks, through=None):
    rows_dev, width = incident.shape[-2:]
    slots, _, tile_size, _ = tiles.shape[-4:]
    packed = rows_dev // 2
    outer = pltpu.VMEM((packed, width), jnp.bfloat16)
    own = pltpu.VMEM((packed, width), jnp.float32)
    outs = [outer, outer, pltpu.VMEM((rows_dev, width), jnp.bfloat16), own, own]
    args, specs, aliases = [*index, incident, sources, tiles], [HBM, HBM, SMEM, HBM, HBM], {}
    if front == 0:
        specs.append(HBM)
        outs.append(pltpu.VMEM((slots, 2, tile_size, tile_size), jnp.bfloat16))
    else:
        specs += [VMEM, VMEM]
        aliases = {len(args): len(outs)}
        args.append(through)
        outs.append(outer)
    return pl.pallas_call(
        functools.partial(front_kernel, front, blocks),
        out_shape=outs,
        in_specs=specs,
        out_specs=[VMEM] * len(outs),
        scratch_shapes=scratch(slots, rows_dev, width, tile_size),
        input_output_aliases=aliases,
        **kernel_options(f"front_{front}", 10**9, 5 * 10**6),
    )(*args)


def chunk_kernel(wave, front, part, blocks, *refs):
    index_refs, (inbound, sources, tiles, outer_ref, inner_ref, own_ref) = refs[:3], refs[3:9]
    rows_s, cols_s, source_v, pair, sums, sems, _ = refs[9:]
    tile_size = tiles.shape[-1]
    rows_dev, width = pair.shape[1:]
    half = tile_size // 2

    @pl.when(lax.axis_index("layer") == wave)
    def _():
        copies = [
            pltpu.make_async_copy(index_refs[0], rows_s, sems.at[0]),
            pltpu.make_async_copy(index_refs[1], cols_s, sems.at[1]),
            pltpu.make_async_copy(sources.at[0, front], source_v, sems.at[3]),
        ]
        for copy in copies:
            copy.start()
        sums[...] = jnp.zeros(sums.shape, jnp.float32)
        for r in range(blocks):
            upper = inbound[pl.ds(r * half, half), :].astype(jnp.float32)
            lower = pltpu.roll(upper, width - width // 4, 1)
            for j, value in enumerate((upper, lower)):
                rows = pl.ds(r * tile_size + j * half, half)
                pair[0, rows, :] = value.astype(jnp.bfloat16)
                pair[1, rows, :] = turn(value).astype(jnp.bfloat16)
        for copy in copies[:2]:
            copy.wait()
        accumulate(index_refs, rows_s, cols_s, tiles, pair, sums, blocks, lambda i: None)
        inner_start, outer_start = side_starts(rows_dev)
        copies[2].wait()
        for r in range(blocks):
            rows = pl.ds(r * half, half)
            outer_ref[rows, :] = pack(read_block(sums, outer_start, r, tile_size), 0).astype(jnp.bfloat16)
            inner_ref[rows, :] = pack(read_block(sums, inner_start, r, tile_size), 0).astype(jnp.bfloat16)
            source = source_v[pl.ds(r * tile_size, tile_size), :].astype(jnp.float32)
            own = sums[pl.ds(rows_dev + r * tile_size, tile_size), :]
            own_ref[rows, :] = pack(own, 0) + pack(source, part)


def chunk_products(wave, front, part, inbound, sources, tiles, index, blocks):
    rows_dev, width = sources.shape[-2:]
    slots, _, tile_size, _ = tiles.shape
    payload = pltpu.VMEM((rows_dev // 2, width), jnp.bfloat16)
    return pl.pallas_call(
        functools.partial(chunk_kernel, wave, front, part, blocks),
        out_shape=[payload, payload, pltpu.VMEM((rows_dev // 2, width), jnp.float32)],
        in_specs=[HBM, HBM, SMEM, VMEM, HBM, VMEM],
        out_specs=[VMEM] * 3,
        scratch_shapes=scratch(slots, rows_dev, width, tile_size),
        **kernel_options(f"chunk_{wave}_{front}_{part}", 10**9, 5 * 10**6),
    )(*index, inbound, sources, tiles)


def combine_kernel(wave, part, has_through, final, *refs):
    own_ref, inner_ref, outer_ref = refs[:3]
    packed, width = own_ref.shape
    out_ref = refs[-1] if not has_through else refs[-2]
    rows = pl.ds(part * packed if inner_ref.shape[0] > packed else 0, packed)
    total = own_ref[...] + inner_ref[rows, :].astype(jnp.float32) + outer_ref[...].astype(jnp.float32)
    if wave > 0:
        active = lax.axis_index("layer") == wave
        total = jnp.where(active, total, refs[3][...].astype(jnp.float32))
    if not (final and part == PARTS - 1):
        out_ref[...] = total.astype(jnp.bfloat16)
        return
    blocks, half = final
    low, high = refs[4][...].astype(jnp.float32), total
    first = quarters((half, width))
    for r in range(blocks):
        a, b = low[r * half : (r + 1) * half], high[r * half : (r + 1) * half]
        upper = jnp.where(first, a, pltpu.roll(b, width // 4, 1))
        lower = jnp.where(first, pltpu.roll(a, width - width // 4, 1), b)
        out_ref[0, 0, pl.ds(2 * r * half, half), :] = upper.astype(jnp.bfloat16)
        out_ref[0, 0, pl.ds((2 * r + 1) * half, half), :] = lower.astype(jnp.bfloat16)


def combine(wave, front, part, own, inner, outer, earlier=None, through=None, final=None, partner=None, result=None, fronts=0):
    packed, width = own.shape
    args, specs, aliases = [own, inner, outer], [VMEM] * 3, {}
    grid = {}
    if wave > 0:
        args.append(earlier)
        specs.append(VMEM)
    outs, out_specs = [pltpu.VMEM((packed, width), jnp.bfloat16)], [VMEM]
    if through is not None:
        aliases = {len(args): 1}
        args.append(through)
        specs.append(VMEM)
        outs.append(pltpu.VMEM(through.shape, through.dtype))
        out_specs.append(VMEM)
    if final and part == PARTS - 1:
        grid = {"grid": (1,)}
        args.append(partner)
        specs.append(VMEM)
        outs = [jax.ShapeDtypeStruct((1, fronts, 2 * packed, width), jnp.bfloat16)]
        out_specs = [pl.BlockSpec((1, 1, 2 * packed, width), lambda i: (0, front, 0, 0))]
        if result is not None:
            aliases = {len(args): 0}
            args.append(result)
            specs.append(pl.BlockSpec(memory_space=pl.ANY))
    return pl.pallas_call(
        functools.partial(combine_kernel, wave, part, through is not None, final),
        out_shape=outs,
        in_specs=specs,
        out_specs=out_specs,
        input_output_aliases=aliases,
        **grid,
        **kernel_options(f"combine_{wave}_{front}_{part}", 10**6, 10**6, 12),
    )(*args)


def shards(incident, sources, green_tiles, tile_rows, tile_cols, tile_count):
    depth, devices = lax.axis_size("layer"), lax.axis_size("tile")
    layer_route = down_route(depth)
    fronts, rows_dev, _ = incident.shape
    tile_size = green_tiles.shape[-1]
    blocks = rows_dev // tile_size
    index = (in_hbm(tile_rows), in_hbm(tile_cols), tile_count)
    incident, sources, green_tiles = map(in_hbm, (incident, sources, green_tiles))

    def across(payload, wave):
        return lax.ppermute(payload, ("layer", "tile"), outer_route(wave, devices))

    def beside(payload):
        return lax.ppermute(payload, "tile", inner_route(devices))

    def down(payload):
        return lax.ppermute(payload, "layer", layer_route)

    def total(wave, chunk, *args, **kwargs):
        return combine(wave, chunk // PARTS, chunk % PARTS, *args, **kwargs)

    chunks, payloads, held, waiting = [], [], green_tiles, None
    for front in range(fronts):
        made = front_products(front, incident, sources, held, index, blocks, waiting)
        if front == 0:
            held, waiting = made[5], made[1]
            payloads = [None] * PARTS
            outers = [across(made[0], 0), None]
        else:
            if front == 1:
                chunks[1][2] = across(made[5], 0)
            payloads += made[:2]
            outers = [None, None]
            waiting = made[1]
        inner = beside(made[2])
        chunks += [[made[3 + part], inner, outers[part]] for part in range(PARTS)]
    if fronts == 1:
        chunks[1][2] = across(waiting, 0)
    passed, leaving = [], []
    for c in range(len(chunks)):
        behind = c + PARTS
        through = payloads[behind] if behind < len(chunks) else None
        made = total(0, c, *chunks[c], through=through)
        if through is not None:
            chunks[behind][2] = across(made[1], 0)
        leaving.append(made[0])
        if depth > 1:
            passed.append(down(made[0]))
    for wave in range(1, depth):
        final = wave == depth - 1
        chunks = []
        for c, inbound in enumerate(passed):
            outer, inner, own = chunk_products(
                wave, c // PARTS, c % PARTS, inbound, sources, held, index, blocks
            )
            chunks.append((own, beside(inner), across(outer, wave)))
        if final:
            break
        leaving = [total(wave, c, *chunk, leaving[c])[0] for c, chunk in enumerate(chunks)]
        passed = [down(chunk) for chunk in leaving]
    result = partner = None
    for c, chunk in enumerate(chunks):
        (out,) = total(
            depth - 1, c, *chunk, leaving[c],
            final=(blocks, tile_size // 2), partner=partner, result=result, fronts=fronts,
        )
        partner = out
        if c % PARTS == PARTS - 1:
            result = out
    return result


def solution(mesh):
    return jax.shard_map(
        shards,
        mesh=mesh,
        in_specs=(
            P(None, "tile", None),
            P("layer", None, "tile", None),
            P("layer", "tile", None, None, None),
            P("layer", "tile"),
            P("layer", "tile"),
            P("layer", "tile"),
        ),
        out_specs=P("layer", None, "tile", None),
        check_vma=False,
    )
```

```python
import functools

import jax
import jax.numpy as jnp
from jax import lax
from jax.experimental import pallas as pl
from jax.experimental.pallas import tpu as pltpu
from jax.sharding import PartitionSpec as P


MIB = 1 << 20
VMEM = pl.BlockSpec(memory_space=pltpu.VMEM)
HBM = pl.BlockSpec(memory_space=pltpu.HBM)
SMEM = pl.BlockSpec(memory_space=pltpu.SMEM)
PARTS = 2


def inner_route(devices):
    return [(i, i ^ 1) for i in range(devices)]


def outer_route(wave, devices):
    pairs = [(wave * devices + i, wave * devices + i + 1) for i in range(1, devices - 1, 2)]
    return pairs + [(b, a) for a, b in pairs]


def down_route(depth):
    return [(i, (i + 1) % depth) for i in range(depth)]


def in_hbm(array):
    return pltpu.with_memory_space_constraint(array, pltpu.HBM)


def quarters(shape):
    return lax.rem(lax.broadcasted_iota(jnp.int32, shape, 1), shape[1] // 2) < shape[1] // 4


def pack(block, part):
    rows, width = block.shape
    upper, lower = block[: rows // 2], block[rows // 2 :]
    if part == 0:
        lower = pltpu.roll(lower, width // 4, 1)
    else:
        upper = pltpu.roll(upper, width - width // 4, 1)
    return jnp.where(quarters(upper.shape), upper, lower)


def turn(value):
    half = value.shape[1] // 2
    moved = pltpu.roll(value, half, 1)
    lane = lax.broadcasted_iota(jnp.int32, value.shape, 1)
    return jnp.where(lane < half, -moved, moved)


def accumulate(index_refs, rows_s, cols_s, tiles, pair, sums, blocks, ready):
    tile_size = tiles.shape[-1]
    first = (lax.axis_index("tile") - 1) * blocks
    count = index_refs[2][0, 0]
    for i in range(tiles.shape[0]):
        ready(i)
        live = i < count
        row = jnp.where(live, rows_s[0, i] - first, 3 * blocks)
        column = jnp.where(live, cols_s[0, i], 0)
        rows = pl.ds(pl.multiple_of(column * tile_size, tile_size), tile_size)
        target = pl.ds(pl.multiple_of(row * tile_size, tile_size), tile_size)
        term = jnp.dot(tiles[i, 0], pair[0, rows, :], preferred_element_type=jnp.float32)
        term += jnp.dot(tiles[i, 1], pair[1, rows, :], preferred_element_type=jnp.float32)
        sums[target, :] += term


def side_starts(rows_dev):
    odd = lax.rem(lax.axis_index("tile"), 2)
    return (1 - odd) * 2 * rows_dev, odd * 2 * rows_dev


def read_block(sums, start, r, tile_size):
    return sums[pl.ds(pl.multiple_of(start + r * tile_size, tile_size), tile_size), :]


def front_kernel(front, blocks, *refs):
    index_refs, incident, sources = refs[:3], refs[3], refs[4]
    if front == 0:
        stored, outer_refs, inner_ref, own_refs, tiles = refs[5], refs[6:8], refs[8], refs[9:11], refs[11]
        rest = refs[12:]
    else:
        tiles, outer_refs, inner_ref, own_refs = refs[5], refs[7:9], refs[9], refs[10:12]
        rest = refs[13:]
    rows_s, cols_s, source_v, pair, sums, sems, tile_sems = rest
    slots, tile_size = tiles.shape[0], tiles.shape[-1]
    rows_dev = pair.shape[1]
    packed = rows_dev // 2

    def tile_copy(i):
        return pltpu.make_async_copy(stored.at[0, i], tiles.at[i], tile_sems.at[i])

    active = lax.axis_index("layer") == 0
    copies = [
        pltpu.make_async_copy(index_refs[0], rows_s, sems.at[0]),
        pltpu.make_async_copy(index_refs[1], cols_s, sems.at[1]),
        pltpu.make_async_copy(incident.at[front], pair.at[0], sems.at[2]),
        pltpu.make_async_copy(sources.at[0, front], source_v, sems.at[3]),
    ]

    @pl.when(active)
    def _():
        for copy in copies[:3]:
            copy.start()

    early = slots // 4 if front == 0 else 0
    for i in range(early):
        tile_copy(i).start()

    @pl.when(active)
    def _():
        sums[...] = jnp.zeros(sums.shape, jnp.float32)
        for copy in copies[:3]:
            copy.wait()
        if front == 0:
            for i in range(early, slots):
                tile_copy(i).start()
        for r in range(blocks):
            rows = pl.ds(r * tile_size, tile_size)
            pair[1, rows, :] = turn(pair[0, rows, :].astype(jnp.float32)).astype(jnp.bfloat16)
        copies[3].start()
        ready = (lambda i: tile_copy(i).wait()) if front == 0 else (lambda i: None)
        accumulate(index_refs, rows_s, cols_s, tiles, pair, sums, blocks, ready)
        inner_start, outer_start = side_starts(rows_dev)
        copies[3].wait()
        half = tile_size // 2
        for r in range(blocks):
            own = sums[pl.ds(rows_dev + r * tile_size, tile_size), :]
            own = own + source_v[pl.ds(r * tile_size, tile_size), :].astype(jnp.float32)
            inner = read_block(sums, inner_start, r, tile_size)
            outer = read_block(sums, outer_start, r, tile_size)
            for part in range(PARTS):
                rows = pl.ds(r * half, half)
                own_refs[part][rows, :] = pack(own, part)
                outer_refs[part][rows, :] = pack(outer, part).astype(jnp.bfloat16)
                inner_ref[pl.ds(part * packed + r * half, half), :] = pack(inner, part).astype(jnp.bfloat16)

    if front == 0:

        @pl.when(jnp.logical_not(active))
        def _():
            for i in range(early, slots):
                tile_copy(i).start()
            for i in range(slots):
                tile_copy(i).wait()


def scratch(slots, rows_dev, width, tile_size):
    return [
        pltpu.SMEM((1, slots), jnp.int32),
        pltpu.SMEM((1, slots), jnp.int32),
        pltpu.VMEM((rows_dev, width), jnp.bfloat16),
        pltpu.VMEM((2, rows_dev, width), jnp.bfloat16),
        pltpu.VMEM((3 * rows_dev + tile_size, width), jnp.float32),
        pltpu.SemaphoreType.DMA((4,)),
        pltpu.SemaphoreType.DMA((slots,)),
    ]


def kernel_options(name, flops, moved, limit=20):
    return dict(
        compiler_params=pltpu.CompilerParams(vmem_limit_bytes=limit * MIB),
        cost_estimate=pl.CostEstimate(flops=flops, bytes_accessed=moved, transcendentals=0),
        name=name,
    )


def front_products(front, incident, sources, tiles, index, blocks, through=None):
    rows_dev, width = incident.shape[-2:]
    slots, _, tile_size, _ = tiles.shape[-4:]
    packed = rows_dev // 2
    outer = pltpu.VMEM((packed, width), jnp.bfloat16)
    own = pltpu.VMEM((packed, width), jnp.float32)
    outs = [outer, outer, pltpu.VMEM((rows_dev, width), jnp.bfloat16), own, own]
    args, specs, aliases = [*index, incident, sources, tiles], [HBM, HBM, SMEM, HBM, HBM], {}
    if front == 0:
        specs.append(HBM)
        outs.append(pltpu.VMEM((slots, 2, tile_size, tile_size), jnp.bfloat16))
    else:
        specs += [VMEM, VMEM]
        aliases = {len(args): len(outs)}
        args.append(through)
        outs.append(outer)
    return pl.pallas_call(
        functools.partial(front_kernel, front, blocks),
        out_shape=outs,
        in_specs=specs,
        out_specs=[VMEM] * len(outs),
        scratch_shapes=scratch(slots, rows_dev, width, tile_size),
        input_output_aliases=aliases,
        **kernel_options(f"front_{front}", 10**9, 5 * 10**6),
    )(*args)


def prepare_kernel(wave, front, part, sources, sums, source_v, sem):
    rows_dev, width = source_v.shape

    @pl.when(lax.axis_index("layer") == wave)
    def _():
        copy = pltpu.make_async_copy(sources.at[0, front], source_v, sem)
        copy.start()
        side = jnp.zeros((rows_dev, width), jnp.float32)
        sums[pl.ds(0, rows_dev), :] = side
        sums[pl.ds(2 * rows_dev, sums.shape[0] - 2 * rows_dev), :] = jnp.zeros(
            (sums.shape[0] - 2 * rows_dev, width), jnp.float32
        )
        copy.wait()
        source = source_v[...].astype(jnp.float32)
        if part > 0:
            source = pltpu.roll(source, width - width // 4, 1)
        sums[pl.ds(rows_dev, rows_dev), :] = source


def prepare(wave, front, part, sources, tile_size):
    rows_dev, width = sources.shape[-2:]
    return pl.pallas_call(
        functools.partial(prepare_kernel, wave, front, part),
        out_shape=pltpu.VMEM((3 * rows_dev + tile_size, width), jnp.float32),
        in_specs=[HBM],
        out_specs=VMEM,
        scratch_shapes=[pltpu.VMEM((rows_dev, width), jnp.bfloat16), pltpu.SemaphoreType.DMA(())],
        **kernel_options(f"prepare_{wave}_{front}_{part}", 10**6, 10**6, 4),
    )(sources)


def chunk_kernel(wave, blocks, *refs):
    index_refs, (inbound, tiles, _, outer_ref, inner_ref, own_ref, sums) = refs[:3], refs[3:10]
    rows_s, cols_s, pair, sems = refs[10:]
    tile_size = tiles.shape[-1]
    rows_dev, width = pair.shape[1:]
    half = tile_size // 2

    @pl.when(lax.axis_index("layer") == wave)
    def _():
        copies = [
            pltpu.make_async_copy(index_refs[0], rows_s, sems.at[0]),
            pltpu.make_async_copy(index_refs[1], cols_s, sems.at[1]),
        ]
        for copy in copies:
            copy.start()
        for r in range(blocks):
            upper = inbound[pl.ds(r * half, half), :].astype(jnp.float32)
            lower = pltpu.roll(upper, width - width // 4, 1)
            for j, value in enumerate((upper, lower)):
                rows = pl.ds(r * tile_size + j * half, half)
                pair[0, rows, :] = value.astype(jnp.bfloat16)
                pair[1, rows, :] = turn(value).astype(jnp.bfloat16)
        for copy in copies:
            copy.wait()
        accumulate(index_refs, rows_s, cols_s, tiles, pair, sums, blocks, lambda i: None)
        inner_start, outer_start = side_starts(rows_dev)
        for r in range(blocks):
            rows = pl.ds(r * half, half)
            outer_ref[rows, :] = pack(read_block(sums, outer_start, r, tile_size), 0).astype(jnp.bfloat16)
            inner_ref[rows, :] = pack(read_block(sums, inner_start, r, tile_size), 0).astype(jnp.bfloat16)
            own_ref[rows, :] = pack(read_block(sums, rows_dev, r, tile_size), 0)


def chunk_products(wave, front, part, inbound, tiles, sums, index, blocks):
    slots, _, tile_size, _ = tiles.shape
    rows_dev, width = blocks * tile_size, sums.shape[-1]
    payload = pltpu.VMEM((rows_dev // 2, width), jnp.bfloat16)
    return pl.pallas_call(
        functools.partial(chunk_kernel, wave, blocks),
        out_shape=[payload, payload, pltpu.VMEM((rows_dev // 2, width), jnp.float32), pltpu.VMEM(sums.shape, sums.dtype)],
        in_specs=[HBM, HBM, SMEM, VMEM, VMEM, VMEM],
        out_specs=[VMEM] * 4,
        scratch_shapes=[
            pltpu.SMEM((1, slots), jnp.int32),
            pltpu.SMEM((1, slots), jnp.int32),
            pltpu.VMEM((2, rows_dev, width), jnp.bfloat16),
            pltpu.SemaphoreType.DMA((2,)),
        ],
        input_output_aliases={5: 3},
        **kernel_options(f"chunk_{wave}_{front}_{part}", 10**9, 5 * 10**6, 4),
    )(*index, inbound, tiles, sums)


def combine_kernel(wave, part, has_through, final, *refs):
    own_ref, inner_ref, outer_ref = refs[:3]
    packed, width = own_ref.shape
    out_ref = refs[-1] if not has_through else refs[-2]
    rows = pl.ds(part * packed if inner_ref.shape[0] > packed else 0, packed)
    total = own_ref[...] + inner_ref[rows, :].astype(jnp.float32) + outer_ref[...].astype(jnp.float32)
    if wave > 0:
        active = lax.axis_index("layer") == wave
        total = jnp.where(active, total, refs[3][...].astype(jnp.float32))
    if not (final and part == PARTS - 1):
        out_ref[...] = total.astype(jnp.bfloat16)
        return
    blocks, half = final
    low, high = refs[4][...].astype(jnp.float32), total
    first = quarters((half, width))
    for r in range(blocks):
        a, b = low[r * half : (r + 1) * half], high[r * half : (r + 1) * half]
        upper = jnp.where(first, a, pltpu.roll(b, width // 4, 1))
        lower = jnp.where(first, pltpu.roll(a, width - width // 4, 1), b)
        out_ref[0, 0, pl.ds(2 * r * half, half), :] = upper.astype(jnp.bfloat16)
        out_ref[0, 0, pl.ds((2 * r + 1) * half, half), :] = lower.astype(jnp.bfloat16)


def combine(wave, front, part, own, inner, outer, earlier=None, through=None, final=None, partner=None, result=None, fronts=0):
    packed, width = own.shape
    args, specs, aliases = [own, inner, outer], [VMEM] * 3, {}
    grid = {}
    if wave > 0:
        args.append(earlier)
        specs.append(VMEM)
    outs, out_specs = [pltpu.VMEM((packed, width), jnp.bfloat16)], [VMEM]
    if through is not None:
        aliases = {len(args): 1}
        args.append(through)
        specs.append(VMEM)
        outs.append(pltpu.VMEM(through.shape, through.dtype))
        out_specs.append(VMEM)
    if final and part == PARTS - 1:
        grid = {"grid": (1,)}
        args.append(partner)
        specs.append(VMEM)
        outs = [jax.ShapeDtypeStruct((1, fronts, 2 * packed, width), jnp.bfloat16)]
        out_specs = [pl.BlockSpec((1, 1, 2 * packed, width), lambda i: (0, front, 0, 0))]
        if result is not None:
            aliases = {len(args): 0}
            args.append(result)
            specs.append(pl.BlockSpec(memory_space=pl.ANY))
    return pl.pallas_call(
        functools.partial(combine_kernel, wave, part, through is not None, final),
        out_shape=outs,
        in_specs=specs,
        out_specs=out_specs,
        input_output_aliases=aliases,
        **grid,
        **kernel_options(f"combine_{wave}_{front}_{part}", 10**6, 10**6, 12),
    )(*args)


def shards(incident, sources, green_tiles, tile_rows, tile_cols, tile_count):
    depth, devices = lax.axis_size("layer"), lax.axis_size("tile")
    layer_route = down_route(depth)
    fronts, rows_dev, _ = incident.shape
    tile_size = green_tiles.shape[-1]
    blocks = rows_dev // tile_size
    index = (in_hbm(tile_rows), in_hbm(tile_cols), tile_count)
    incident, sources, green_tiles = map(in_hbm, (incident, sources, green_tiles))

    def across(payload, wave):
        return lax.ppermute(payload, ("layer", "tile"), outer_route(wave, devices))

    def beside(payload):
        return lax.ppermute(payload, "tile", inner_route(devices))

    def down(payload):
        return lax.ppermute(payload, "layer", layer_route)

    def total(wave, chunk, *args, **kwargs):
        return combine(wave, chunk // PARTS, chunk % PARTS, *args, **kwargs)

    chunks, payloads, held, waiting = [], [], green_tiles, None
    for front in range(fronts):
        made = front_products(front, incident, sources, held, index, blocks, waiting)
        if front == 0:
            held, waiting = made[5], made[1]
            payloads = [None] * PARTS
            outers = [across(made[0], 0), None]
        else:
            if front == 1:
                chunks[1][2] = across(made[5], 0)
            payloads += made[:2]
            outers = [None, None]
            waiting = made[1]
        inner = beside(made[2])
        chunks += [[made[3 + part], inner, outers[part]] for part in range(PARTS)]
    if fronts == 1:
        chunks[1][2] = across(waiting, 0)
    passed, leaving = [], []
    for c in range(len(chunks)):
        behind = c + PARTS
        through = payloads[behind] if behind < len(chunks) else None
        made = total(0, c, *chunks[c], through=through)
        if through is not None:
            chunks[behind][2] = across(made[1], 0)
        leaving.append(made[0])
        if depth > 1:
            passed.append(down(made[0]))
    for wave in range(1, depth):
        final = wave == depth - 1
        chunks = []
        for c, inbound in enumerate(passed):
            sums = prepare(wave, c // PARTS, c % PARTS, sources, tile_size)
            outer, inner, own, _ = chunk_products(
                wave, c // PARTS, c % PARTS, inbound, held, sums, index, blocks
            )
            chunks.append((own, beside(inner), across(outer, wave)))
        if final:
            break
        leaving = [total(wave, c, *chunk, leaving[c])[0] for c, chunk in enumerate(chunks)]
        passed = [down(chunk) for chunk in leaving]
    result = partner = None
    for c, chunk in enumerate(chunks):
        (out,) = total(
            depth - 1, c, *chunk, leaving[c],
            final=(blocks, tile_size // 2), partner=partner, result=result, fronts=fronts,
        )
        partner = out
        if c % PARTS == PARTS - 1:
            result = out
    return result


def solution(mesh):
    return jax.shard_map(
        shards,
        mesh=mesh,
        in_specs=(
            P(None, "tile", None),
            P("layer", None, "tile", None),
            P("layer", "tile", None, None, None),
            P("layer", "tile"),
            P("layer", "tile"),
            P("layer", "tile"),
        ),
        out_specs=P("layer", None, "tile", None),
        check_vma=False,
    )
```

```python
import functools

import jax
import jax.numpy as jnp
from jax import lax
from jax.experimental import pallas as pl
from jax.experimental.pallas import tpu as pltpu
from jax.sharding import PartitionSpec as P


MIB = 1 << 20
VMEM = pl.BlockSpec(memory_space=pltpu.VMEM)
HBM = pl.BlockSpec(memory_space=pltpu.HBM)
SMEM = pl.BlockSpec(memory_space=pltpu.SMEM)
PARTS = 2


def inner_route(devices):
    return [(i, i ^ 1) for i in range(devices)]


def outer_route(wave, devices):
    pairs = [(wave * devices + i, wave * devices + i + 1) for i in range(1, devices - 1, 2)]
    return pairs + [(b, a) for a, b in pairs]


def down_route(depth):
    return [(i, (i + 1) % depth) for i in range(depth)]


def in_hbm(array):
    return pltpu.with_memory_space_constraint(array, pltpu.HBM)


def quarters(shape):
    return lax.rem(lax.broadcasted_iota(jnp.int32, shape, 1), shape[1] // 2) < shape[1] // 4


def pack(block, part):
    rows, width = block.shape
    upper, lower = block[: rows // 2], block[rows // 2 :]
    if part == 0:
        lower = pltpu.roll(lower, width // 4, 1)
    else:
        upper = pltpu.roll(upper, width - width // 4, 1)
    return jnp.where(quarters(upper.shape), upper, lower)


def turn(value):
    half = value.shape[1] // 2
    moved = pltpu.roll(value, half, 1)
    lane = lax.broadcasted_iota(jnp.int32, value.shape, 1)
    return jnp.where(lane < half, -moved, moved)


def accumulate(index_refs, rows_s, cols_s, tiles, pair, sums, blocks, skipped=None):
    tile_size = tiles.shape[-1]
    first = (lax.axis_index("tile") - 1) * blocks
    count = index_refs[2][0, 0]
    for i in range(tiles.shape[0]):
        live = i < count
        window = rows_s[0, i] - first
        if skipped is not None:
            live = live & (lax.div(window, blocks) != skipped)
        row = jnp.where(live, window, 3 * blocks)
        column = jnp.where(live, cols_s[0, i], 0)
        rows = pl.ds(pl.multiple_of(column * tile_size, tile_size), tile_size)
        target = pl.ds(pl.multiple_of(row * tile_size, tile_size), tile_size)
        term = jnp.dot(tiles[i, 0], pair[0, rows, :], preferred_element_type=jnp.float32)
        term += jnp.dot(tiles[i, 1], pair[1, rows, :], preferred_element_type=jnp.float32)
        sums[target, :] += term


def side_starts(rows_dev):
    odd = lax.rem(lax.axis_index("tile"), 2)
    return (1 - odd) * 2 * rows_dev, odd * 2 * rows_dev


def read_block(sums, start, r, tile_size):
    return sums[pl.ds(pl.multiple_of(start + r * tile_size, tile_size), tile_size), :]


def outer_window():
    return 2 * lax.rem(lax.axis_index("tile"), 2)


def open_kernel(blocks, *refs):
    index_refs, (incident, stored, *outer_refs), (pair, tiles) = refs[:3], refs[3:7], refs[7:9]
    rows_s, cols_s, sums, sems, tile_sems = refs[9:]
    slots, tile_size = tiles.shape[0], tiles.shape[-1]
    half = tile_size // 2
    active = lax.axis_index("layer") == 0
    copies = [
        pltpu.make_async_copy(index_refs[0], rows_s, sems.at[0]),
        pltpu.make_async_copy(index_refs[1], cols_s, sems.at[1]),
        pltpu.make_async_copy(incident.at[0], pair.at[0], sems.at[2]),
    ]

    def tile_copy(i):
        return pltpu.make_async_copy(stored.at[0, i], tiles.at[i], tile_sems.at[i])

    for copy in copies:
        copy.start()
    early = slots // 4
    for i in range(early):
        tile_copy(i).start()

    @pl.when(active)
    def _():
        sums[...] = jnp.zeros(sums.shape, jnp.float32)

    for copy in copies:
        copy.wait()
    for i in range(early, slots):
        tile_copy(i).start()

    @pl.when(active)
    def _():
        for r in range(blocks):
            rows = pl.ds(r * tile_size, tile_size)
            pair[1, rows, :] = turn(pair[0, rows, :].astype(jnp.float32)).astype(jnp.bfloat16)

    count = index_refs[2][0, 0]
    first = (lax.axis_index("tile") - 1) * blocks

    @pl.loop(0, slots)
    def _(i):
        tile_copy(i).wait()
        window = rows_s[0, i] - first

        @pl.when(active & (i < count) & (lax.div(window, blocks) == outer_window()))
        def _():
            rows = pl.ds(pl.multiple_of(cols_s[0, i] * tile_size, tile_size), tile_size)
            target = pl.ds(pl.multiple_of(lax.rem(window, blocks) * tile_size, tile_size), tile_size)
            term = jnp.dot(tiles[i, 0], pair[0, rows, :], preferred_element_type=jnp.float32)
            term += jnp.dot(tiles[i, 1], pair[1, rows, :], preferred_element_type=jnp.float32)
            sums[target, :] += term

    @pl.when(active)
    def _():
        for r in range(blocks):
            block = sums[pl.ds(r * tile_size, tile_size), :]
            for part in range(PARTS):
                outer_refs[part][pl.ds(r * half, half), :] = pack(block, part).astype(jnp.bfloat16)


def open_products(incident, tiles, index, blocks):
    rows_dev, width = incident.shape[-2:]
    slots, _, tile_size, _ = tiles.shape[-4:]
    outer = pltpu.VMEM((rows_dev // 2, width), jnp.bfloat16)
    return pl.pallas_call(
        functools.partial(open_kernel, blocks),
        out_shape=[
            outer,
            outer,
            pltpu.VMEM((2, rows_dev, width), jnp.bfloat16),
            pltpu.VMEM((slots, 2, tile_size, tile_size), jnp.bfloat16),
        ],
        in_specs=[HBM, HBM, SMEM, HBM, HBM],
        out_specs=[VMEM] * 4,
        scratch_shapes=[
            pltpu.SMEM((1, slots), jnp.int32),
            pltpu.SMEM((1, slots), jnp.int32),
            pltpu.VMEM((rows_dev, width), jnp.float32),
            pltpu.SemaphoreType.DMA((3,)),
            pltpu.SemaphoreType.DMA((slots,)),
        ],
        **kernel_options("open", 5 * 10**8, 4 * 10**6, 4),
    )(*index, incident, tiles)


def front_kernel(front, blocks, *refs):
    index_refs, sources, tiles, operand = refs[:3], refs[3], refs[4], refs[5]
    outs, (rows_s, cols_s, source_v, sums, sems, *rest) = refs[6 : len(refs) - (5 if front == 0 else 6)], refs[
        len(refs) - (5 if front == 0 else 6) :
    ]
    inner_ref, own_refs, outer_refs = outs[0], outs[1:3], outs[3:]
    pair = operand if front == 0 else rest[0]
    tile_size = tiles.shape[-1]
    rows_dev = pair.shape[1]
    packed = rows_dev // 2

    @pl.when(lax.axis_index("layer") == 0)
    def _():
        copies = [
            pltpu.make_async_copy(index_refs[0], rows_s, sems.at[0]),
            pltpu.make_async_copy(index_refs[1], cols_s, sems.at[1]),
            pltpu.make_async_copy(sources.at[0, front], source_v, sems.at[2]),
        ]
        if front > 0:
            copies.append(pltpu.make_async_copy(operand.at[front], pair.at[0], sems.at[3]))
        for copy in copies:
            copy.start()
        sums[...] = jnp.zeros(sums.shape, jnp.float32)
        for copy in copies:
            copy.wait()
        if front > 0:
            for r in range(blocks):
                rows = pl.ds(r * tile_size, tile_size)
                pair[1, rows, :] = turn(pair[0, rows, :].astype(jnp.float32)).astype(jnp.bfloat16)
        accumulate(
            index_refs, rows_s, cols_s, tiles, pair, sums, blocks, outer_window() if front == 0 else None
        )
        inner_start, outer_start = side_starts(rows_dev)
        half = tile_size // 2
        for r in range(blocks):
            own = sums[pl.ds(rows_dev + r * tile_size, tile_size), :]
            own = own + source_v[pl.ds(r * tile_size, tile_size), :].astype(jnp.float32)
            inner = read_block(sums, inner_start, r, tile_size)
            for part in range(PARTS):
                rows = pl.ds(r * half, half)
                own_refs[part][rows, :] = pack(own, part)
                inner_ref[pl.ds(part * packed + r * half, half), :] = pack(inner, part).astype(jnp.bfloat16)
            if front > 0:
                outer = read_block(sums, outer_start, r, tile_size)
                for part in range(PARTS):
                    outer_refs[part][pl.ds(r * half, half), :] = pack(outer, part).astype(jnp.bfloat16)


def kernel_options(name, flops, moved, limit=20):
    return dict(
        compiler_params=pltpu.CompilerParams(vmem_limit_bytes=limit * MIB),
        cost_estimate=pl.CostEstimate(flops=flops, bytes_accessed=moved, transcendentals=0),
        name=name,
    )


def front_products(front, operand, sources, tiles, index, blocks):
    rows_dev, width = sources.shape[-2:]
    slots, _, tile_size, _ = tiles.shape
    outer = pltpu.VMEM((rows_dev // 2, width), jnp.bfloat16)
    own = pltpu.VMEM((rows_dev // 2, width), jnp.float32)
    outs = [pltpu.VMEM((rows_dev, width), jnp.bfloat16), own, own] + ([outer, outer] if front else [])
    scratch = [
        pltpu.SMEM((1, slots), jnp.int32),
        pltpu.SMEM((1, slots), jnp.int32),
        pltpu.VMEM((rows_dev, width), jnp.bfloat16),
        pltpu.VMEM((3 * rows_dev + tile_size, width), jnp.float32),
        pltpu.SemaphoreType.DMA((4,)),
    ]
    if front:
        scratch.append(pltpu.VMEM((2, rows_dev, width), jnp.bfloat16))
    return pl.pallas_call(
        functools.partial(front_kernel, front, blocks),
        out_shape=outs,
        in_specs=[HBM, HBM, SMEM, HBM, VMEM, HBM if front else VMEM],
        out_specs=[VMEM] * len(outs),
        scratch_shapes=scratch,
        **kernel_options(f"front_{front}", 10**9, 5 * 10**6, 6),
    )(*index, sources, tiles, operand)


def prepare_kernel(wave, front, part, sources, sums, source_v, sem):
    rows_dev, width = source_v.shape

    @pl.when(lax.axis_index("layer") == wave)
    def _():
        copy = pltpu.make_async_copy(sources.at[0, front], source_v, sem)
        copy.start()
        side = jnp.zeros((rows_dev, width), jnp.float32)
        sums[pl.ds(0, rows_dev), :] = side
        sums[pl.ds(2 * rows_dev, sums.shape[0] - 2 * rows_dev), :] = jnp.zeros(
            (sums.shape[0] - 2 * rows_dev, width), jnp.float32
        )
        copy.wait()
        source = source_v[...].astype(jnp.float32)
        if part > 0:
            source = pltpu.roll(source, width - width // 4, 1)
        sums[pl.ds(rows_dev, rows_dev), :] = source


def prepare(wave, front, part, sources, tile_size):
    rows_dev, width = sources.shape[-2:]
    return pl.pallas_call(
        functools.partial(prepare_kernel, wave, front, part),
        out_shape=pltpu.VMEM((3 * rows_dev + tile_size, width), jnp.float32),
        in_specs=[HBM],
        out_specs=VMEM,
        scratch_shapes=[pltpu.VMEM((rows_dev, width), jnp.bfloat16), pltpu.SemaphoreType.DMA(())],
        **kernel_options(f"prepare_{wave}_{front}_{part}", 10**6, 10**6, 4),
    )(sources)


def chunk_kernel(wave, blocks, *refs):
    index_refs, (inbound, tiles, _, outer_ref, inner_ref, own_ref, sums) = refs[:3], refs[3:10]
    rows_s, cols_s, pair, sems = refs[10:]
    tile_size = tiles.shape[-1]
    rows_dev, width = pair.shape[1:]
    half = tile_size // 2

    @pl.when(lax.axis_index("layer") == wave)
    def _():
        copies = [
            pltpu.make_async_copy(index_refs[0], rows_s, sems.at[0]),
            pltpu.make_async_copy(index_refs[1], cols_s, sems.at[1]),
        ]
        for copy in copies:
            copy.start()
        for r in range(blocks):
            upper = inbound[pl.ds(r * half, half), :].astype(jnp.float32)
            lower = pltpu.roll(upper, width - width // 4, 1)
            for j, value in enumerate((upper, lower)):
                rows = pl.ds(r * tile_size + j * half, half)
                pair[0, rows, :] = value.astype(jnp.bfloat16)
                pair[1, rows, :] = turn(value).astype(jnp.bfloat16)
        for copy in copies:
            copy.wait()
        accumulate(index_refs, rows_s, cols_s, tiles, pair, sums, blocks)
        inner_start, outer_start = side_starts(rows_dev)
        for r in range(blocks):
            rows = pl.ds(r * half, half)
            outer_ref[rows, :] = pack(read_block(sums, outer_start, r, tile_size), 0).astype(jnp.bfloat16)
            inner_ref[rows, :] = pack(read_block(sums, inner_start, r, tile_size), 0).astype(jnp.bfloat16)
            own_ref[rows, :] = pack(read_block(sums, rows_dev, r, tile_size), 0)


def chunk_products(wave, front, part, inbound, tiles, sums, index, blocks):
    slots, _, tile_size, _ = tiles.shape
    rows_dev, width = blocks * tile_size, sums.shape[-1]
    payload = pltpu.VMEM((rows_dev // 2, width), jnp.bfloat16)
    return pl.pallas_call(
        functools.partial(chunk_kernel, wave, blocks),
        out_shape=[payload, payload, pltpu.VMEM((rows_dev // 2, width), jnp.float32), pltpu.VMEM(sums.shape, sums.dtype)],
        in_specs=[HBM, HBM, SMEM, VMEM, VMEM, VMEM],
        out_specs=[VMEM] * 4,
        scratch_shapes=[
            pltpu.SMEM((1, slots), jnp.int32),
            pltpu.SMEM((1, slots), jnp.int32),
            pltpu.VMEM((2, rows_dev, width), jnp.bfloat16),
            pltpu.SemaphoreType.DMA((2,)),
        ],
        input_output_aliases={5: 3},
        **kernel_options(f"chunk_{wave}_{front}_{part}", 10**9, 5 * 10**6, 4),
    )(*index, inbound, tiles, sums)


def combine_kernel(wave, part, has_through, final, *refs):
    own_ref, inner_ref, outer_ref = refs[:3]
    packed, width = own_ref.shape
    out_ref = refs[-1] if not has_through else refs[-2]
    rows = pl.ds(part * packed if inner_ref.shape[0] > packed else 0, packed)
    total = own_ref[...] + inner_ref[rows, :].astype(jnp.float32) + outer_ref[...].astype(jnp.float32)
    if wave > 0:
        active = lax.axis_index("layer") == wave
        total = jnp.where(active, total, refs[3][...].astype(jnp.float32))
    if not (final and part == PARTS - 1):
        out_ref[...] = total.astype(jnp.bfloat16)
        return
    blocks, half = final
    low, high = refs[4][...].astype(jnp.float32), total
    first = quarters((half, width))
    for r in range(blocks):
        a, b = low[r * half : (r + 1) * half], high[r * half : (r + 1) * half]
        upper = jnp.where(first, a, pltpu.roll(b, width // 4, 1))
        lower = jnp.where(first, pltpu.roll(a, width - width // 4, 1), b)
        out_ref[0, 0, pl.ds(2 * r * half, half), :] = upper.astype(jnp.bfloat16)
        out_ref[0, 0, pl.ds((2 * r + 1) * half, half), :] = lower.astype(jnp.bfloat16)


def combine(wave, front, part, own, inner, outer, earlier=None, through=None, final=None, partner=None, result=None, fronts=0):
    packed, width = own.shape
    args, specs, aliases = [own, inner, outer], [VMEM] * 3, {}
    grid = {}
    if wave > 0:
        args.append(earlier)
        specs.append(VMEM)
    outs, out_specs = [pltpu.VMEM((packed, width), jnp.bfloat16)], [VMEM]
    if through is not None:
        aliases = {len(args): 1}
        args.append(through)
        specs.append(VMEM)
        outs.append(pltpu.VMEM(through.shape, through.dtype))
        out_specs.append(VMEM)
    if final and part == PARTS - 1:
        grid = {"grid": (1,)}
        args.append(partner)
        specs.append(VMEM)
        outs = [jax.ShapeDtypeStruct((1, fronts, 2 * packed, width), jnp.bfloat16)]
        out_specs = [pl.BlockSpec((1, 1, 2 * packed, width), lambda i: (0, front, 0, 0))]
        if result is not None:
            aliases = {len(args): 0}
            args.append(result)
            specs.append(pl.BlockSpec(memory_space=pl.ANY))
    return pl.pallas_call(
        functools.partial(combine_kernel, wave, part, through is not None, final),
        out_shape=outs,
        in_specs=specs,
        out_specs=out_specs,
        input_output_aliases=aliases,
        **grid,
        **kernel_options(f"combine_{wave}_{front}_{part}", 10**6, 10**6, 12),
    )(*args)


def shards(incident, sources, green_tiles, tile_rows, tile_cols, tile_count):
    depth, devices = lax.axis_size("layer"), lax.axis_size("tile")
    layer_route = down_route(depth)
    fronts, rows_dev, _ = incident.shape
    tile_size = green_tiles.shape[-1]
    blocks = rows_dev // tile_size
    index = (in_hbm(tile_rows), in_hbm(tile_cols), tile_count)
    incident, sources, green_tiles = map(in_hbm, (incident, sources, green_tiles))

    def across(payload, wave):
        return lax.ppermute(payload, ("layer", "tile"), outer_route(wave, devices))

    def beside(payload):
        return lax.ppermute(payload, "tile", inner_route(devices))

    def down(payload):
        return lax.ppermute(payload, "layer", layer_route)

    def total(wave, chunk, *args, **kwargs):
        return combine(wave, chunk // PARTS, chunk % PARTS, *args, **kwargs)

    first = open_products(incident, green_tiles, index, blocks)
    payloads, held = list(first[:PARTS]), first[3]
    chunks = []
    for front in range(fronts):
        made = front_products(front, incident if front else first[2], sources, held, index, blocks)
        inner = beside(made[0])
        payloads += made[3:]
        chunks += [[made[1 + part], inner, None] for part in range(PARTS)]
    for c in range(min(PARTS + 1, len(chunks))):
        chunks[c][2] = across(payloads[c], 0)
    passed, leaving = [], []
    for c in range(len(chunks)):
        behind = c + PARTS
        through = payloads[behind] if PARTS < behind < len(chunks) else None
        made = total(0, c, *chunks[c], through=through)
        if through is not None:
            chunks[behind][2] = across(made[1], 0)
        leaving.append(made[0])
        if depth > 1:
            passed.append(down(made[0]))
    for wave in range(1, depth):
        final = wave == depth - 1
        chunks = []
        for c, inbound in enumerate(passed):
            sums = prepare(wave, c // PARTS, c % PARTS, sources, tile_size)
            outer, inner, own, _ = chunk_products(
                wave, c // PARTS, c % PARTS, inbound, held, sums, index, blocks
            )
            chunks.append((own, beside(inner), across(outer, wave)))
        if final:
            break
        leaving = [total(wave, c, *chunk, leaving[c])[0] for c, chunk in enumerate(chunks)]
        passed = [down(chunk) for chunk in leaving]
    result = partner = None
    for c, chunk in enumerate(chunks):
        (out,) = total(
            depth - 1, c, *chunk, leaving[c],
            final=(blocks, tile_size // 2), partner=partner, result=result, fronts=fronts,
        )
        partner = out
        if c % PARTS == PARTS - 1:
            result = out
    return result


def solution(mesh):
    return jax.shard_map(
        shards,
        mesh=mesh,
        in_specs=(
            P(None, "tile", None),
            P("layer", None, "tile", None),
            P("layer", "tile", None, None, None),
            P("layer", "tile"),
            P("layer", "tile"),
            P("layer", "tile"),
        ),
        out_specs=P("layer", None, "tile", None),
        check_vma=False,
    )
```

```python
import functools

import jax
import jax.numpy as jnp
from jax import lax
from jax.experimental import pallas as pl
from jax.experimental.pallas import tpu as pltpu
from jax.sharding import PartitionSpec as P


MIB = 1 << 20
VMEM = pl.BlockSpec(memory_space=pltpu.VMEM)
HBM = pl.BlockSpec(memory_space=pltpu.HBM)
SMEM = pl.BlockSpec(memory_space=pltpu.SMEM)
PARTS = 2


def inner_route(devices):
    return [(i, i ^ 1) for i in range(devices)]


def outer_route(wave, devices):
    pairs = [(wave * devices + i, wave * devices + i + 1) for i in range(1, devices - 1, 2)]
    return pairs + [(b, a) for a, b in pairs]


def down_route(depth):
    return [(i, (i + 1) % depth) for i in range(depth)]


def in_hbm(array):
    return pltpu.with_memory_space_constraint(array, pltpu.HBM)


def quarters(shape):
    return lax.rem(lax.broadcasted_iota(jnp.int32, shape, 1), shape[1] // 2) < shape[1] // 4


def pack(block, part):
    rows, width = block.shape
    upper, lower = block[: rows // 2], block[rows // 2 :]
    if part == 0:
        lower = pltpu.roll(lower, width // 4, 1)
    else:
        upper = pltpu.roll(upper, width - width // 4, 1)
    return jnp.where(quarters(upper.shape), upper, lower)


def turn(value):
    half = value.shape[1] // 2
    moved = pltpu.roll(value, half, 1)
    lane = lax.broadcasted_iota(jnp.int32, value.shape, 1)
    return jnp.where(lane < half, -moved, moved)


def accumulate(index_refs, rows_s, cols_s, tiles, pair, sums, blocks, skipped=None):
    tile_size = tiles.shape[-1]
    first = (lax.axis_index("tile") - 1) * blocks
    count = index_refs[2][0, 0]
    for i in range(tiles.shape[0]):
        live = i < count
        window = rows_s[0, i] - first
        if skipped is not None:
            live = live & (lax.div(window, blocks) != skipped)
        row = jnp.where(live, window, 3 * blocks)
        column = jnp.where(live, cols_s[0, i], 0)
        rows = pl.ds(pl.multiple_of(column * tile_size, tile_size), tile_size)
        target = pl.ds(pl.multiple_of(row * tile_size, tile_size), tile_size)
        term = jnp.dot(tiles[i, 0], pair[0, rows, :], preferred_element_type=jnp.float32)
        term += jnp.dot(tiles[i, 1], pair[1, rows, :], preferred_element_type=jnp.float32)
        sums[target, :] += term


def side_starts(rows_dev):
    odd = lax.rem(lax.axis_index("tile"), 2)
    return (1 - odd) * 2 * rows_dev, odd * 2 * rows_dev


def read_block(sums, start, r, tile_size):
    return sums[pl.ds(pl.multiple_of(start + r * tile_size, tile_size), tile_size), :]


def outer_window():
    return 2 * lax.rem(lax.axis_index("tile"), 2)


def open_kernel(blocks, *refs):
    index_refs, (incident, stored, *outer_refs), (pair, tiles) = refs[:3], refs[3:7], refs[7:9]
    rows_s, cols_s, sums, sems, tile_sems = refs[9:]
    slots, tile_size = tiles.shape[0], tiles.shape[-1]
    half = tile_size // 2
    active = lax.axis_index("layer") == 0
    copies = [
        pltpu.make_async_copy(index_refs[0], rows_s, sems.at[0]),
        pltpu.make_async_copy(index_refs[1], cols_s, sems.at[1]),
        pltpu.make_async_copy(incident.at[0], pair.at[0], sems.at[2]),
    ]

    def tile_copy(i):
        return pltpu.make_async_copy(stored.at[0, i], tiles.at[i], tile_sems.at[i])

    for copy in copies:
        copy.start()
    early = slots // 4
    for i in range(early):
        tile_copy(i).start()

    @pl.when(active)
    def _():
        sums[...] = jnp.zeros(sums.shape, jnp.float32)

    for copy in copies:
        copy.wait()
    for i in range(early, slots):
        tile_copy(i).start()

    @pl.when(active)
    def _():
        for r in range(blocks):
            rows = pl.ds(r * tile_size, tile_size)
            pair[1, rows, :] = turn(pair[0, rows, :].astype(jnp.float32)).astype(jnp.bfloat16)

    count = index_refs[2][0, 0]
    first = (lax.axis_index("tile") - 1) * blocks

    @pl.loop(0, slots)
    def _(i):
        tile_copy(i).wait()
        window = rows_s[0, i] - first

        @pl.when(active & (i < count) & (lax.div(window, blocks) == outer_window()))
        def _():
            rows = pl.ds(pl.multiple_of(cols_s[0, i] * tile_size, tile_size), tile_size)
            target = pl.ds(pl.multiple_of(lax.rem(window, blocks) * tile_size, tile_size), tile_size)
            term = jnp.dot(tiles[i, 0], pair[0, rows, :], preferred_element_type=jnp.float32)
            term += jnp.dot(tiles[i, 1], pair[1, rows, :], preferred_element_type=jnp.float32)
            sums[target, :] += term

    @pl.when(active)
    def _():
        for r in range(blocks):
            block = sums[pl.ds(r * tile_size, tile_size), :]
            for part in range(PARTS):
                outer_refs[part][pl.ds(r * half, half), :] = pack(block, part).astype(jnp.bfloat16)


def open_products(incident, tiles, index, blocks):
    rows_dev, width = incident.shape[-2:]
    slots, _, tile_size, _ = tiles.shape[-4:]
    outer = pltpu.VMEM((rows_dev // 2, width), jnp.bfloat16)
    return pl.pallas_call(
        functools.partial(open_kernel, blocks),
        out_shape=[
            outer,
            outer,
            pltpu.VMEM((2, rows_dev, width), jnp.bfloat16),
            pltpu.VMEM((slots, 2, tile_size, tile_size), jnp.bfloat16),
        ],
        in_specs=[HBM, HBM, SMEM, HBM, HBM],
        out_specs=[VMEM] * 4,
        scratch_shapes=[
            pltpu.SMEM((1, slots), jnp.int32),
            pltpu.SMEM((1, slots), jnp.int32),
            pltpu.VMEM((rows_dev, width), jnp.float32),
            pltpu.SemaphoreType.DMA((3,)),
            pltpu.SemaphoreType.DMA((slots,)),
        ],
        **kernel_options("open", 5 * 10**8, 4 * 10**6, 4),
    )(*index, incident, tiles)


def front_kernel(front, blocks, *refs):
    index_refs, sources, tiles, operand = refs[:3], refs[3], refs[4], refs[5]
    outs, (rows_s, cols_s, source_v, sums, sems, *rest) = refs[6 : len(refs) - (5 if front == 0 else 6)], refs[
        len(refs) - (5 if front == 0 else 6) :
    ]
    inner_ref, own_refs, outer_refs = outs[0], outs[1:3], outs[3:]
    pair = operand if front == 0 else rest[0]
    tile_size = tiles.shape[-1]
    rows_dev = pair.shape[1]
    packed = rows_dev // 2

    @pl.when(lax.axis_index("layer") == 0)
    def _():
        copies = [
            pltpu.make_async_copy(index_refs[0], rows_s, sems.at[0]),
            pltpu.make_async_copy(index_refs[1], cols_s, sems.at[1]),
            pltpu.make_async_copy(sources.at[0, front], source_v, sems.at[2]),
        ]
        if front > 0:
            copies.append(pltpu.make_async_copy(operand.at[front], pair.at[0], sems.at[3]))
        for copy in copies:
            copy.start()
        sums[...] = jnp.zeros(sums.shape, jnp.float32)
        for copy in copies:
            copy.wait()
        if front > 0:
            for r in range(blocks):
                rows = pl.ds(r * tile_size, tile_size)
                pair[1, rows, :] = turn(pair[0, rows, :].astype(jnp.float32)).astype(jnp.bfloat16)
        accumulate(
            index_refs, rows_s, cols_s, tiles, pair, sums, blocks, outer_window() if front == 0 else None
        )
        inner_start, outer_start = side_starts(rows_dev)
        half = tile_size // 2
        for r in range(blocks):
            own = sums[pl.ds(rows_dev + r * tile_size, tile_size), :]
            own = own + source_v[pl.ds(r * tile_size, tile_size), :].astype(jnp.float32)
            inner = read_block(sums, inner_start, r, tile_size)
            for part in range(PARTS):
                rows = pl.ds(r * half, half)
                own_refs[part][rows, :] = pack(own, part)
                inner_ref[pl.ds(part * packed + r * half, half), :] = pack(inner, part).astype(jnp.bfloat16)
            if front > 0:
                outer = read_block(sums, outer_start, r, tile_size)
                for part in range(PARTS):
                    outer_refs[part][pl.ds(r * half, half), :] = pack(outer, part).astype(jnp.bfloat16)


def kernel_options(name, flops, moved, limit=20):
    return dict(
        compiler_params=pltpu.CompilerParams(vmem_limit_bytes=limit * MIB),
        cost_estimate=pl.CostEstimate(flops=flops, bytes_accessed=moved, transcendentals=0),
        name=name,
    )


def front_products(front, operand, sources, tiles, index, blocks):
    rows_dev, width = sources.shape[-2:]
    slots, _, tile_size, _ = tiles.shape
    outer = pltpu.VMEM((rows_dev // 2, width), jnp.bfloat16)
    own = pltpu.VMEM((rows_dev // 2, width), jnp.float32)
    outs = [pltpu.VMEM((rows_dev, width), jnp.bfloat16), own, own] + ([outer, outer] if front else [])
    scratch = [
        pltpu.SMEM((1, slots), jnp.int32),
        pltpu.SMEM((1, slots), jnp.int32),
        pltpu.VMEM((rows_dev, width), jnp.bfloat16),
        pltpu.VMEM((3 * rows_dev + tile_size, width), jnp.float32),
        pltpu.SemaphoreType.DMA((4,)),
    ]
    if front:
        scratch.append(pltpu.VMEM((2, rows_dev, width), jnp.bfloat16))
    return pl.pallas_call(
        functools.partial(front_kernel, front, blocks),
        out_shape=outs,
        in_specs=[HBM, HBM, SMEM, HBM, VMEM, HBM if front else VMEM],
        out_specs=[VMEM] * len(outs),
        scratch_shapes=scratch,
        **kernel_options(f"front_{front}", 10**9, 5 * 10**6, 6),
    )(*index, sources, tiles, operand)


def prepare_kernel(wave, front, part, blocks, sources, sums, source_v, sem):
    rows_dev, width = source_v.shape
    tile_size, packed = rows_dev // blocks, rows_dev // 2
    half = tile_size // 2

    @pl.when(lax.axis_index("layer") == wave)
    def _():
        copy = pltpu.make_async_copy(sources.at[0, front], source_v, sem)
        copy.start()
        rest = sums.shape[0] - 2 * packed
        sums[pl.ds(0, packed), :] = jnp.zeros((packed, width), jnp.float32)
        sums[pl.ds(2 * packed, rest), :] = jnp.zeros((rest, width), jnp.float32)
        copy.wait()
        for r in range(blocks):
            source = source_v[pl.ds(r * tile_size, tile_size), :].astype(jnp.float32)
            sums[pl.ds(packed + r * half, half), :] = pack(source, part)


def prepare(wave, front, part, sources, tile_size):
    rows_dev, width = sources.shape[-2:]
    return pl.pallas_call(
        functools.partial(prepare_kernel, wave, front, part, rows_dev // tile_size),
        out_shape=pltpu.VMEM(((3 * rows_dev + tile_size) // 2, width), jnp.float32),
        in_specs=[HBM],
        out_specs=VMEM,
        scratch_shapes=[pltpu.VMEM((rows_dev, width), jnp.bfloat16), pltpu.SemaphoreType.DMA(())],
        **kernel_options(f"prepare_{wave}_{front}_{part}", 10**6, 10**6, 4),
    )(sources)


def chunk_kernel(wave, blocks, *refs):
    rows_s, cols_s, count_s, inbound, tiles, _, outer_ref, inner_ref, sums, operand = refs
    tile_size = tiles.shape[-1]
    packed, width = inbound.shape
    half = tile_size // 2
    first = quarters((half, width))

    @pl.when(lax.axis_index("layer") == wave)
    def _():
        for r in range(blocks):
            value = inbound[pl.ds(r * half, half), :].astype(jnp.float32)
            for j, given in enumerate((value, turn(value))):
                upper = jnp.where(first, given, 0.0)
                lower = jnp.where(first, 0.0, given)
                parts = (
                    upper,
                    pltpu.roll(lower, width - width // 4, 1),
                    pltpu.roll(upper, width // 4, 1),
                    lower,
                )
                for k, part in enumerate(parts):
                    rows = pl.ds((8 * r + 4 * j + k) * half, half)
                    operand[rows, :] = part.astype(jnp.bfloat16)
        start = (lax.axis_index("tile") - 1) * blocks
        count = count_s[0, 0]
        for i in range(tiles.shape[0]):
            live = i < count
            row = jnp.where(live, rows_s[0, i] - start, 3 * blocks)
            column = jnp.where(live, cols_s[0, i], 0)
            rows = pl.ds(pl.multiple_of(column * 4 * tile_size, tile_size), 4 * tile_size)
            target = pl.ds(pl.multiple_of(row * half, half), half)
            left = jnp.concatenate(
                [tiles[i, j, pl.ds(k * half, half), :] for j in range(2) for k in range(2)], axis=1
            )
            sums[target, :] += jnp.dot(left, operand[rows, :], preferred_element_type=jnp.float32)
        inner_start, outer_start = side_starts(packed)
        for ref, begin in ((outer_ref, outer_start), (inner_ref, inner_start)):
            for r in range(blocks):
                ref[pl.ds(r * half, half), :] = read_block(sums, begin, r, half).astype(jnp.bfloat16)


def chunk_products(wave, front, part, inbound, tiles, sums, index, blocks):
    tile_size = tiles.shape[-1]
    packed, width = inbound.shape
    payload = pltpu.VMEM((packed, width), jnp.bfloat16)
    return pl.pallas_call(
        functools.partial(chunk_kernel, wave, blocks),
        out_shape=[payload, payload, pltpu.VMEM(sums.shape, sums.dtype)],
        in_specs=[SMEM, SMEM, SMEM, VMEM, VMEM, VMEM],
        out_specs=[VMEM] * 3,
        scratch_shapes=[pltpu.VMEM((4 * blocks * tile_size, width), jnp.bfloat16)],
        input_output_aliases={5: 2},
        **kernel_options(f"chunk_{wave}_{front}_{part}", 10**9, 5 * 10**6, 4),
    )(*index, inbound, tiles, sums)


def combine_kernel(wave, part, has_through, final, *refs):
    own_ref, inner_ref, outer_ref = refs[:3]
    packed, width = outer_ref.shape
    own_rows = pl.ds(packed if own_ref.shape[0] > packed else 0, packed)
    inner_rows = pl.ds(part * packed if inner_ref.shape[0] > packed else 0, packed)
    total = own_ref[own_rows, :] + inner_ref[inner_rows, :].astype(jnp.float32) + outer_ref[...].astype(jnp.float32)
    if wave > 0:
        active = lax.axis_index("layer") == wave
        total = jnp.where(active, total, refs[3][...].astype(jnp.float32))
    if not (final and part == PARTS - 1):
        out_ref = refs[-2] if has_through else refs[-1]
        out_ref[...] = total.astype(jnp.bfloat16)
        return
    front, blocks, half = final
    out_ref, staged, sems = refs[-3:]
    low, high = refs[4][...].astype(jnp.float32), total
    first = quarters((half, width))
    copies = []
    for r in range(blocks):
        a, b = low[r * half : (r + 1) * half], high[r * half : (r + 1) * half]
        upper = jnp.where(first, a, pltpu.roll(b, width // 4, 1))
        lower = jnp.where(first, pltpu.roll(a, width - width // 4, 1), b)
        staged[pl.ds(2 * r * half, half), :] = upper.astype(jnp.bfloat16)
        staged[pl.ds((2 * r + 1) * half, half), :] = lower.astype(jnp.bfloat16)
        rows = pl.ds(2 * r * half, 2 * half)
        copies.append(pltpu.make_async_copy(staged.at[rows, :], out_ref.at[0, front, rows, :], sems.at[r]))
        copies[-1].start()
    for copy in copies:
        copy.wait()


def combine(wave, front, part, own, inner, outer, earlier=None, through=None, final=None, partner=None, result=None, fronts=0):
    packed, width = outer.shape
    args, specs, aliases, scratch = [own, inner, outer], [VMEM] * 3, {}, []
    if wave > 0:
        args.append(earlier)
        specs.append(VMEM)
    outs, out_specs = [pltpu.VMEM((packed, width), jnp.bfloat16)], [VMEM]
    if through is not None:
        aliases = {len(args): 1}
        args.append(through)
        specs.append(VMEM)
        outs.append(pltpu.VMEM(through.shape, through.dtype))
        out_specs.append(VMEM)
    if final and part == PARTS - 1:
        final = (front, *final)
        args.append(partner)
        specs.append(VMEM)
        outs = [jax.ShapeDtypeStruct((1, fronts, 2 * packed, width), jnp.bfloat16)]
        out_specs = [HBM]
        scratch = [pltpu.VMEM((2 * packed, width), jnp.bfloat16), pltpu.SemaphoreType.DMA((final[1],))]
        if result is not None:
            aliases = {len(args): 0}
            args.append(result)
            specs.append(HBM)
    return pl.pallas_call(
        functools.partial(combine_kernel, wave, part, through is not None, final),
        out_shape=outs,
        in_specs=specs,
        out_specs=out_specs,
        scratch_shapes=scratch,
        input_output_aliases=aliases,
        **kernel_options(f"combine_{wave}_{front}_{part}", 10**6, 10**6, 8),
    )(*args)


def shards(incident, sources, green_tiles, tile_rows, tile_cols, tile_count):
    depth, devices = lax.axis_size("layer"), lax.axis_size("tile")
    layer_route = down_route(depth)
    fronts, rows_dev, _ = incident.shape
    tile_size = green_tiles.shape[-1]
    blocks = rows_dev // tile_size
    index = (in_hbm(tile_rows), in_hbm(tile_cols), tile_count)
    resident = tuple(pltpu.with_memory_space_constraint(a, pltpu.SMEM) for a in (tile_rows, tile_cols))
    resident = (*resident, tile_count)
    incident, sources, green_tiles = map(in_hbm, (incident, sources, green_tiles))

    def across(payload, wave):
        return lax.ppermute(payload, ("layer", "tile"), outer_route(wave, devices))

    def beside(payload):
        return lax.ppermute(payload, "tile", inner_route(devices))

    def down(payload):
        return lax.ppermute(payload, "layer", layer_route)

    def total(wave, chunk, *args, **kwargs):
        return combine(wave, chunk // PARTS, chunk % PARTS, *args, **kwargs)

    first = open_products(incident, green_tiles, index, blocks)
    payloads, held = list(first[:PARTS]), first[3]
    chunks = []
    for front in range(fronts):
        made = front_products(front, incident if front else first[2], sources, held, index, blocks)
        inner = beside(made[0])
        payloads += made[3:]
        chunks += [[made[1 + part], inner, None] for part in range(PARTS)]
    for c in range(min(PARTS + 1, len(chunks))):
        chunks[c][2] = across(payloads[c], 0)
    passed, leaving = [], []
    for c in range(len(chunks)):
        behind = c + PARTS
        through = payloads[behind] if PARTS < behind < len(chunks) else None
        made = total(0, c, *chunks[c], through=through)
        if through is not None:
            chunks[behind][2] = across(made[1], 0)
        leaving.append(made[0])
        if depth > 1:
            passed.append(down(made[0]))
    for wave in range(1, depth):
        final = wave == depth - 1
        chunks = []
        for c, inbound in enumerate(passed):
            sums = prepare(wave, c // PARTS, c % PARTS, sources, tile_size)
            outer, inner, own = chunk_products(
                wave, c // PARTS, c % PARTS, inbound, held, sums, resident, blocks
            )
            chunks.append((own, beside(inner), across(outer, wave)))
        if final:
            break
        leaving = [total(wave, c, *chunk, leaving[c])[0] for c, chunk in enumerate(chunks)]
        passed = [down(chunk) for chunk in leaving]
    result = partner = None
    for c, chunk in enumerate(chunks):
        (out,) = total(
            depth - 1, c, *chunk, leaving[c],
            final=(blocks, tile_size // 2), partner=partner, result=result, fronts=fronts,
        )
        partner = out
        if c % PARTS == PARTS - 1:
            result = out
    return result


def solution(mesh):
    return jax.shard_map(
        shards,
        mesh=mesh,
        in_specs=(
            P(None, "tile", None),
            P("layer", None, "tile", None),
            P("layer", "tile", None, None, None),
            P("layer", "tile"),
            P("layer", "tile"),
            P("layer", "tile"),
        ),
        out_specs=P("layer", None, "tile", None),
        check_vma=False,
    )
```

```python
import functools

import jax
import jax.numpy as jnp
from jax import lax
from jax.experimental import pallas as pl
from jax.experimental.pallas import tpu as pltpu
from jax.sharding import PartitionSpec as P


MIB = 1 << 20
VMEM = pl.BlockSpec(memory_space=pltpu.VMEM)
HBM = pl.BlockSpec(memory_space=pltpu.HBM)
SMEM = pl.BlockSpec(memory_space=pltpu.SMEM)
PARTS = 2


def inner_route(devices):
    return [(i, i ^ 1) for i in range(devices)]


def outer_route(wave, depth, devices):
    pairs = []
    for layer in range(depth):
        for i in range(devices):
            other = (i + 1 if i % 2 else i - 1) % devices if layer == wave else i ^ 1
            pairs.append((layer * devices + i, layer * devices + other))
    return pairs


def down_route(depth):
    return [(i, (i + 1) % depth) for i in range(depth)]


def in_hbm(array):
    return pltpu.with_memory_space_constraint(array, pltpu.HBM)


def quarters(shape):
    return lax.rem(lax.broadcasted_iota(jnp.int32, shape, 1), shape[1] // 2) < shape[1] // 4


def pack(block, part):
    rows, width = block.shape
    upper, lower = block[: rows // 2], block[rows // 2 :]
    if part == 0:
        lower = pltpu.roll(lower, width // 4, 1)
    else:
        upper = pltpu.roll(upper, width - width // 4, 1)
    return jnp.where(quarters(upper.shape), upper, lower)


def turn(value):
    half = value.shape[1] // 2
    moved = pltpu.roll(value, half, 1)
    lane = lax.broadcasted_iota(jnp.int32, value.shape, 1)
    return jnp.where(lane < half, -moved, moved)


def accumulate(index_refs, rows_s, cols_s, tiles, pair, sums, blocks, skipped=None):
    tile_size = tiles.shape[-1]
    first = (lax.axis_index("tile") - 1) * blocks
    count = index_refs[2][0, 0]
    for i in range(tiles.shape[0]):
        live = i < count
        window = rows_s[0, i] - first
        if skipped is not None:
            live = live & (lax.div(window, blocks) != skipped)
        row = jnp.where(live, window, 3 * blocks)
        column = jnp.where(live, cols_s[0, i], 0)
        rows = pl.ds(pl.multiple_of(column * tile_size, tile_size), tile_size)
        target = pl.ds(pl.multiple_of(row * tile_size, tile_size), tile_size)
        term = jnp.dot(tiles[i, 0], pair[0, rows, :], preferred_element_type=jnp.float32)
        term += jnp.dot(tiles[i, 1], pair[1, rows, :], preferred_element_type=jnp.float32)
        sums[target, :] += term


def side_starts(rows_dev):
    odd = lax.rem(lax.axis_index("tile"), 2)
    return (1 - odd) * 2 * rows_dev, odd * 2 * rows_dev


def read_block(sums, start, r, tile_size):
    return sums[pl.ds(pl.multiple_of(start + r * tile_size, tile_size), tile_size), :]


def outer_window():
    return 2 * lax.rem(lax.axis_index("tile"), 2)


def open_kernel(blocks, *refs):
    index_refs, (incident, stored, *outer_refs), (pair, tiles) = refs[:3], refs[3:7], refs[7:9]
    rows_s, cols_s, sums, sems, tile_sems = refs[9:]
    slots, tile_size = tiles.shape[0], tiles.shape[-1]
    half = tile_size // 2
    active = lax.axis_index("layer") == 0
    copies = [
        pltpu.make_async_copy(index_refs[0], rows_s, sems.at[0]),
        pltpu.make_async_copy(index_refs[1], cols_s, sems.at[1]),
        pltpu.make_async_copy(incident.at[0], pair.at[0], sems.at[2]),
    ]

    def tile_copy(i):
        return pltpu.make_async_copy(stored.at[0, i], tiles.at[i], tile_sems.at[i])

    for copy in copies:
        copy.start()
    early = slots // 4
    for i in range(early):
        tile_copy(i).start()

    @pl.when(active)
    def _():
        sums[...] = jnp.zeros(sums.shape, jnp.float32)

    for copy in copies:
        copy.wait()
    for i in range(early, slots):
        tile_copy(i).start()

    @pl.when(active)
    def _():
        for r in range(blocks):
            rows = pl.ds(r * tile_size, tile_size)
            pair[1, rows, :] = turn(pair[0, rows, :].astype(jnp.float32)).astype(jnp.bfloat16)

    count = index_refs[2][0, 0]
    first = (lax.axis_index("tile") - 1) * blocks

    @pl.loop(0, slots)
    def _(i):
        tile_copy(i).wait()
        window = rows_s[0, i] - first

        @pl.when(active & (i < count) & (lax.div(window, blocks) == outer_window()))
        def _():
            rows = pl.ds(pl.multiple_of(cols_s[0, i] * tile_size, tile_size), tile_size)
            target = pl.ds(pl.multiple_of(lax.rem(window, blocks) * tile_size, tile_size), tile_size)
            term = jnp.dot(tiles[i, 0], pair[0, rows, :], preferred_element_type=jnp.float32)
            term += jnp.dot(tiles[i, 1], pair[1, rows, :], preferred_element_type=jnp.float32)
            sums[target, :] += term

    @pl.when(active)
    def _():
        for r in range(blocks):
            block = sums[pl.ds(r * tile_size, tile_size), :]
            for part in range(PARTS):
                outer_refs[part][pl.ds(r * half, half), :] = pack(block, part).astype(jnp.bfloat16)


def open_products(incident, tiles, index, blocks):
    rows_dev, width = incident.shape[-2:]
    slots, _, tile_size, _ = tiles.shape[-4:]
    outer = pltpu.VMEM((rows_dev // 2, width), jnp.bfloat16)
    return pl.pallas_call(
        functools.partial(open_kernel, blocks),
        out_shape=[
            outer,
            outer,
            pltpu.VMEM((2, rows_dev, width), jnp.bfloat16),
            pltpu.VMEM((slots, 2, tile_size, tile_size), jnp.bfloat16),
        ],
        in_specs=[HBM, HBM, SMEM, HBM, HBM],
        out_specs=[VMEM] * 4,
        scratch_shapes=[
            pltpu.SMEM((1, slots), jnp.int32),
            pltpu.SMEM((1, slots), jnp.int32),
            pltpu.VMEM((rows_dev, width), jnp.float32),
            pltpu.SemaphoreType.DMA((3,)),
            pltpu.SemaphoreType.DMA((slots,)),
        ],
        **kernel_options("open", 5 * 10**8, 4 * 10**6, 4),
    )(*index, incident, tiles)


def front_kernel(front, blocks, *refs):
    index_refs, sources, tiles, operand = refs[:3], refs[3], refs[4], refs[5]
    outs, (rows_s, cols_s, source_v, sums, sems, *rest) = refs[6 : len(refs) - (5 if front == 0 else 6)], refs[
        len(refs) - (5 if front == 0 else 6) :
    ]
    inner_ref, own_refs, outer_refs = outs[0], outs[1:3], outs[3:]
    pair = operand if front == 0 else rest[0]
    tile_size = tiles.shape[-1]
    rows_dev = pair.shape[1]
    packed = rows_dev // 2

    @pl.when(lax.axis_index("layer") == 0)
    def _():
        copies = [
            pltpu.make_async_copy(index_refs[0], rows_s, sems.at[0]),
            pltpu.make_async_copy(index_refs[1], cols_s, sems.at[1]),
            pltpu.make_async_copy(sources.at[0, front], source_v, sems.at[2]),
        ]
        if front > 0:
            copies.append(pltpu.make_async_copy(operand.at[front], pair.at[0], sems.at[3]))
        for copy in copies:
            copy.start()
        sums[...] = jnp.zeros(sums.shape, jnp.float32)
        for copy in copies:
            copy.wait()
        if front > 0:
            for r in range(blocks):
                rows = pl.ds(r * tile_size, tile_size)
                pair[1, rows, :] = turn(pair[0, rows, :].astype(jnp.float32)).astype(jnp.bfloat16)
        accumulate(
            index_refs, rows_s, cols_s, tiles, pair, sums, blocks, outer_window() if front == 0 else None
        )
        inner_start, outer_start = side_starts(rows_dev)
        half = tile_size // 2
        for r in range(blocks):
            own = sums[pl.ds(rows_dev + r * tile_size, tile_size), :]
            own = own + source_v[pl.ds(r * tile_size, tile_size), :].astype(jnp.float32)
            inner = read_block(sums, inner_start, r, tile_size)
            for part in range(PARTS):
                rows = pl.ds(r * half, half)
                own_refs[part][rows, :] = pack(own, part)
                inner_ref[pl.ds(part * packed + r * half, half), :] = pack(inner, part).astype(jnp.bfloat16)
            if front > 0:
                outer = read_block(sums, outer_start, r, tile_size)
                for part in range(PARTS):
                    outer_refs[part][pl.ds(r * half, half), :] = pack(outer, part).astype(jnp.bfloat16)


def kernel_options(name, flops, moved, limit=20):
    return dict(
        compiler_params=pltpu.CompilerParams(vmem_limit_bytes=limit * MIB),
        cost_estimate=pl.CostEstimate(flops=flops, bytes_accessed=moved, transcendentals=0),
        name=name,
    )


def front_products(front, operand, sources, tiles, index, blocks):
    rows_dev, width = sources.shape[-2:]
    slots, _, tile_size, _ = tiles.shape
    outer = pltpu.VMEM((rows_dev // 2, width), jnp.bfloat16)
    own = pltpu.VMEM((rows_dev // 2, width), jnp.float32)
    outs = [pltpu.VMEM((rows_dev, width), jnp.bfloat16), own, own] + ([outer, outer] if front else [])
    scratch = [
        pltpu.SMEM((1, slots), jnp.int32),
        pltpu.SMEM((1, slots), jnp.int32),
        pltpu.VMEM((rows_dev, width), jnp.bfloat16),
        pltpu.VMEM((3 * rows_dev + tile_size, width), jnp.float32),
        pltpu.SemaphoreType.DMA((4,)),
    ]
    if front:
        scratch.append(pltpu.VMEM((2, rows_dev, width), jnp.bfloat16))
    return pl.pallas_call(
        functools.partial(front_kernel, front, blocks),
        out_shape=outs,
        in_specs=[HBM, HBM, SMEM, HBM, VMEM, HBM if front else VMEM],
        out_specs=[VMEM] * len(outs),
        scratch_shapes=scratch,
        **kernel_options(f"front_{front}", 10**9, 5 * 10**6, 6),
    )(*index, sources, tiles, operand)


def prepare_kernel(wave, front, part, blocks, sources, sums, source_v, sem):
    rows_dev, width = source_v.shape
    tile_size, packed = rows_dev // blocks, rows_dev // 2
    half = tile_size // 2

    @pl.when(lax.axis_index("layer") == wave)
    def _():
        copy = pltpu.make_async_copy(sources.at[0, front], source_v, sem)
        copy.start()
        rest = sums.shape[0] - 2 * packed
        sums[pl.ds(0, packed), :] = jnp.zeros((packed, width), jnp.float32)
        sums[pl.ds(2 * packed, rest), :] = jnp.zeros((rest, width), jnp.float32)
        copy.wait()
        for r in range(blocks):
            source = source_v[pl.ds(r * tile_size, tile_size), :].astype(jnp.float32)
            sums[pl.ds(packed + r * half, half), :] = pack(source, part)


def prepare(wave, front, part, sources, tile_size):
    rows_dev, width = sources.shape[-2:]
    return pl.pallas_call(
        functools.partial(prepare_kernel, wave, front, part, rows_dev // tile_size),
        out_shape=pltpu.VMEM(((3 * rows_dev + tile_size) // 2, width), jnp.float32),
        in_specs=[HBM],
        out_specs=VMEM,
        scratch_shapes=[pltpu.VMEM((rows_dev, width), jnp.bfloat16), pltpu.SemaphoreType.DMA(())],
        **kernel_options(f"prepare_{wave}_{front}_{part}", 10**6, 10**6, 4),
    )(sources)


def chunk_kernel(wave, blocks, *refs):
    rows_ref, cols_ref, count_s, inbound, tiles, _, outer_ref, inner_ref, sums, operand, rows_s, cols_s, sems = refs
    tile_size = tiles.shape[-1]
    packed, width = inbound.shape
    half = tile_size // 2
    first = quarters((half, width))

    @pl.when(lax.axis_index("layer") == wave)
    def _():
        copies = [
            pltpu.make_async_copy(rows_ref, rows_s, sems.at[0]),
            pltpu.make_async_copy(cols_ref, cols_s, sems.at[1]),
        ]
        for copy in copies:
            copy.start()
        for r in range(blocks):
            value = inbound[pl.ds(r * half, half), :].astype(jnp.float32)
            for j, given in enumerate((value, turn(value))):
                upper = jnp.where(first, given, 0.0)
                lower = jnp.where(first, 0.0, given)
                parts = (
                    upper,
                    pltpu.roll(lower, width - width // 4, 1),
                    pltpu.roll(upper, width // 4, 1),
                    lower,
                )
                for k, part in enumerate(parts):
                    rows = pl.ds((8 * r + 4 * j + k) * half, half)
                    operand[rows, :] = part.astype(jnp.bfloat16)
        for copy in copies:
            copy.wait()
        start = (lax.axis_index("tile") - 1) * blocks
        count = count_s[0, 0]
        for i in range(tiles.shape[0]):
            live = i < count
            row = jnp.where(live, rows_s[0, i] - start, 3 * blocks)
            column = jnp.where(live, cols_s[0, i], 0)
            rows = pl.ds(pl.multiple_of(column * 4 * tile_size, tile_size), 4 * tile_size)
            target = pl.ds(pl.multiple_of(row * half, half), half)
            left = jnp.concatenate(
                [tiles[i, j, pl.ds(k * half, half), :] for j in range(2) for k in range(2)], axis=1
            )
            sums[target, :] += jnp.dot(left, operand[rows, :], preferred_element_type=jnp.float32)
        inner_start, outer_start = side_starts(packed)
        for ref, begin in ((outer_ref, outer_start), (inner_ref, inner_start)):
            for r in range(blocks):
                ref[pl.ds(r * half, half), :] = read_block(sums, begin, r, half).astype(jnp.bfloat16)


def chunk_products(wave, front, part, inbound, tiles, sums, index, blocks):
    tile_size = tiles.shape[-1]
    packed, width = inbound.shape
    payload = pltpu.VMEM((packed, width), jnp.bfloat16)
    return pl.pallas_call(
        functools.partial(chunk_kernel, wave, blocks),
        out_shape=[payload, payload, pltpu.VMEM(sums.shape, sums.dtype)],
        in_specs=[HBM, HBM, SMEM, VMEM, VMEM, VMEM],
        out_specs=[VMEM] * 3,
        scratch_shapes=[
            pltpu.VMEM((4 * blocks * tile_size, width), jnp.bfloat16),
            pltpu.SMEM((1, tiles.shape[0]), jnp.int32),
            pltpu.SMEM((1, tiles.shape[0]), jnp.int32),
            pltpu.SemaphoreType.DMA((2,)),
        ],
        input_output_aliases={5: 2},
        **kernel_options(f"chunk_{wave}_{front}_{part}", 10**9, 5 * 10**6, 4),
    )(*index, inbound, tiles, sums)


def combine_kernel(wave, part, has_through, final, *refs):
    own_ref, inner_ref, outer_ref = refs[:3]
    packed, width = outer_ref.shape
    own_rows = pl.ds(packed if own_ref.shape[0] > packed else 0, packed)
    inner_rows = pl.ds(part * packed if inner_ref.shape[0] > packed else 0, packed)
    total = own_ref[own_rows, :] + inner_ref[inner_rows, :].astype(jnp.float32) + outer_ref[...].astype(jnp.float32)
    if wave > 0:
        active = lax.axis_index("layer") == wave
        total = jnp.where(active, total, refs[3][...].astype(jnp.float32))
    if not (final and part == PARTS - 1):
        out_ref = refs[-2] if has_through else refs[-1]
        out_ref[...] = total.astype(jnp.bfloat16)
        return
    front, blocks, half = final
    out_ref, staged, sems = refs[-3:]
    low, high = refs[4][...].astype(jnp.float32), total
    first = quarters((half, width))
    copies = []
    for r in range(blocks):
        a, b = low[r * half : (r + 1) * half], high[r * half : (r + 1) * half]
        upper = jnp.where(first, a, pltpu.roll(b, width // 4, 1))
        lower = jnp.where(first, pltpu.roll(a, width - width // 4, 1), b)
        staged[pl.ds(2 * r * half, half), :] = upper.astype(jnp.bfloat16)
        staged[pl.ds((2 * r + 1) * half, half), :] = lower.astype(jnp.bfloat16)
        rows = pl.ds(2 * r * half, 2 * half)
        copies.append(pltpu.make_async_copy(staged.at[rows, :], out_ref.at[0, front, rows, :], sems.at[r]))
        copies[-1].start()
    for copy in copies:
        copy.wait()


def combine(wave, front, part, own, inner, outer, earlier=None, through=None, final=None, partner=None, result=None, fronts=0):
    packed, width = outer.shape
    args, specs, aliases, scratch = [own, inner, outer], [VMEM] * 3, {}, []
    if wave > 0:
        args.append(earlier)
        specs.append(VMEM)
    outs, out_specs = [pltpu.VMEM((packed, width), jnp.bfloat16)], [VMEM]
    if through is not None:
        aliases = {len(args): 1}
        args.append(through)
        specs.append(VMEM)
        outs.append(pltpu.VMEM(through.shape, through.dtype))
        out_specs.append(VMEM)
    if final and part == PARTS - 1:
        final = (front, *final)
        args.append(partner)
        specs.append(VMEM)
        outs = [jax.ShapeDtypeStruct((1, fronts, 2 * packed, width), jnp.bfloat16)]
        out_specs = [HBM]
        scratch = [pltpu.VMEM((2 * packed, width), jnp.bfloat16), pltpu.SemaphoreType.DMA((final[1],))]
        if result is not None:
            aliases = {len(args): 0}
            args.append(result)
            specs.append(HBM)
    return pl.pallas_call(
        functools.partial(combine_kernel, wave, part, through is not None, final),
        out_shape=outs,
        in_specs=specs,
        out_specs=out_specs,
        scratch_shapes=scratch,
        input_output_aliases=aliases,
        **kernel_options(f"combine_{wave}_{front}_{part}", 10**6, 10**6, 8),
    )(*args)


def shards(incident, sources, green_tiles, tile_rows, tile_cols, tile_count):
    depth, devices = lax.axis_size("layer"), lax.axis_size("tile")
    layer_route = down_route(depth)
    fronts, rows_dev, _ = incident.shape
    tile_size = green_tiles.shape[-1]
    blocks = rows_dev // tile_size
    index = (in_hbm(tile_rows), in_hbm(tile_cols), tile_count)
    incident, sources, green_tiles = map(in_hbm, (incident, sources, green_tiles))

    def across(payload, wave):
        return lax.ppermute(payload, ("layer", "tile"), outer_route(wave, depth, devices))

    def beside(payload):
        return lax.ppermute(payload, "tile", inner_route(devices))

    def down(payload):
        return lax.ppermute(payload, "layer", layer_route)

    def total(wave, chunk, *args, **kwargs):
        return combine(wave, chunk // PARTS, chunk % PARTS, *args, **kwargs)

    first = open_products(incident, green_tiles, index, blocks)
    payloads, held = list(first[:PARTS]), first[3]
    chunks = []
    for front in range(fronts):
        made = front_products(front, incident if front else first[2], sources, held, index, blocks)
        inner = beside(made[0])
        payloads += made[3:]
        chunks += [[made[1 + part], inner, None] for part in range(PARTS)]
    for c in range(min(PARTS + 1, len(chunks))):
        chunks[c][2] = across(payloads[c], 0)
    passed, leaving = [], []
    for c in range(len(chunks)):
        behind = c + PARTS
        through = payloads[behind] if PARTS < behind < len(chunks) else None
        made = total(0, c, *chunks[c], through=through)
        if through is not None:
            chunks[behind][2] = across(made[1], 0)
        leaving.append(made[0])
        if depth > 1:
            passed.append(down(made[0]))
    for wave in range(1, depth):
        final = wave == depth - 1
        chunks = []
        for c, inbound in enumerate(passed):
            sums = prepare(wave, c // PARTS, c % PARTS, sources, tile_size)
            outer, inner, own = chunk_products(
                wave, c // PARTS, c % PARTS, inbound, held, sums, index, blocks
            )
            chunks.append((own, beside(inner), across(outer, wave)))
        if final:
            break
        leaving = [total(wave, c, *chunk, leaving[c])[0] for c, chunk in enumerate(chunks)]
        passed = [down(chunk) for chunk in leaving]
    result = partner = None
    for c, chunk in enumerate(chunks):
        (out,) = total(
            depth - 1, c, *chunk, leaving[c],
            final=(blocks, tile_size // 2), partner=partner, result=result, fronts=fronts,
        )
        partner = out
        if c % PARTS == PARTS - 1:
            result = out
    return result


def solution(mesh):
    return jax.shard_map(
        shards,
        mesh=mesh,
        in_specs=(
            P(None, "tile", None),
            P("layer", None, "tile", None),
            P("layer", "tile", None, None, None),
            P("layer", "tile"),
            P("layer", "tile"),
            P("layer", "tile"),
        ),
        out_specs=P("layer", None, "tile", None),
        check_vma=False,
    )
```

```python
import functools

import jax
import jax.numpy as jnp
from jax import lax
from jax.experimental import pallas as pl
from jax.experimental.pallas import tpu as pltpu
from jax.sharding import PartitionSpec as P


MIB = 1 << 20
VMEM = pl.BlockSpec(memory_space=pltpu.VMEM)
HBM = pl.BlockSpec(memory_space=pltpu.HBM)
SMEM = pl.BlockSpec(memory_space=pltpu.SMEM)
PARTS = 2


def inner_route(devices):
    return [(i, i ^ 1) for i in range(devices)]


def outer_route(wave, depth, devices):
    pairs = []
    for layer in range(depth):
        for i in range(devices):
            other = (i + 1 if i % 2 else i - 1) % devices if layer == wave else i ^ 1
            pairs.append((layer * devices + i, layer * devices + other))
    return pairs


def down_route(depth):
    return [(i, (i + 1) % depth) for i in range(depth)]


def in_hbm(array):
    return pltpu.with_memory_space_constraint(array, pltpu.HBM)


def quarters(shape):
    return lax.rem(lax.broadcasted_iota(jnp.int32, shape, 1), shape[1] // 2) < shape[1] // 4


def pack(block, part):
    rows, width = block.shape
    upper, lower = block[: rows // 2], block[rows // 2 :]
    if part == 0:
        lower = pltpu.roll(lower, width // 4, 1)
    else:
        upper = pltpu.roll(upper, width - width // 4, 1)
    return jnp.where(quarters(upper.shape), upper, lower)


def turn(value):
    half = value.shape[1] // 2
    moved = pltpu.roll(value, half, 1)
    lane = lax.broadcasted_iota(jnp.int32, value.shape, 1)
    return jnp.where(lane < half, -moved, moved)


def accumulate(index_refs, tiles, pair, sums, blocks, skipped=None):
    rows_s, cols_s, count_s = index_refs
    tile_size = tiles.shape[-1]
    first = (lax.axis_index("tile") - 1) * blocks
    count = count_s[0, 0]
    for i in range(tiles.shape[0]):
        live = i < count
        window = rows_s[0, i] - first
        if skipped is not None:
            live = live & (lax.div(window, blocks) != skipped)
        row = jnp.where(live, window, 3 * blocks)
        column = jnp.where(live, cols_s[0, i], 0)
        rows = pl.ds(pl.multiple_of(column * tile_size, tile_size), tile_size)
        target = pl.ds(pl.multiple_of(row * tile_size, tile_size), tile_size)
        term = jnp.dot(tiles[i, 0], pair[0, rows, :], preferred_element_type=jnp.float32)
        term += jnp.dot(tiles[i, 1], pair[1, rows, :], preferred_element_type=jnp.float32)
        sums[target, :] += term


def side_starts(rows_dev):
    odd = lax.rem(lax.axis_index("tile"), 2)
    return (1 - odd) * 2 * rows_dev, odd * 2 * rows_dev


def read_block(sums, start, r, tile_size):
    return sums[pl.ds(pl.multiple_of(start + r * tile_size, tile_size), tile_size), :]


def outer_window():
    return 2 * lax.rem(lax.axis_index("tile"), 2)


def open_kernel(blocks, *refs):
    index_refs, (incident, stored, *outer_refs), (pair, tiles) = refs[:3], refs[3:7], refs[7:9]
    rows_s, cols_s, sums, sems, tile_sems = refs[9:]
    slots, tile_size = tiles.shape[0], tiles.shape[-1]
    half = tile_size // 2
    active = lax.axis_index("layer") == 0
    copies = [
        pltpu.make_async_copy(index_refs[0], rows_s, sems.at[0]),
        pltpu.make_async_copy(index_refs[1], cols_s, sems.at[1]),
        pltpu.make_async_copy(incident.at[0], pair.at[0], sems.at[2]),
    ]

    def tile_copy(i):
        return pltpu.make_async_copy(stored.at[0, i], tiles.at[i], tile_sems.at[i])

    for copy in copies:
        copy.start()
    early = slots // 4
    for i in range(early):
        tile_copy(i).start()

    @pl.when(active)
    def _():
        sums[...] = jnp.zeros(sums.shape, jnp.float32)

    for copy in copies:
        copy.wait()
    for i in range(early, slots):
        tile_copy(i).start()

    @pl.when(active)
    def _():
        for r in range(blocks):
            rows = pl.ds(r * tile_size, tile_size)
            pair[1, rows, :] = turn(pair[0, rows, :].astype(jnp.float32)).astype(jnp.bfloat16)

    count = index_refs[2][0, 0]
    first = (lax.axis_index("tile") - 1) * blocks

    @pl.loop(0, slots)
    def _(i):
        tile_copy(i).wait()
        window = rows_s[0, i] - first

        @pl.when(active & (i < count) & (lax.div(window, blocks) == outer_window()))
        def _():
            rows = pl.ds(pl.multiple_of(cols_s[0, i] * tile_size, tile_size), tile_size)
            target = pl.ds(pl.multiple_of(lax.rem(window, blocks) * tile_size, tile_size), tile_size)
            term = jnp.dot(tiles[i, 0], pair[0, rows, :], preferred_element_type=jnp.float32)
            term += jnp.dot(tiles[i, 1], pair[1, rows, :], preferred_element_type=jnp.float32)
            sums[target, :] += term

    @pl.when(active)
    def _():
        for r in range(blocks):
            block = sums[pl.ds(r * tile_size, tile_size), :]
            for part in range(PARTS):
                outer_refs[part][pl.ds(r * half, half), :] = pack(block, part).astype(jnp.bfloat16)


def open_products(incident, tiles, index, blocks):
    rows_dev, width = incident.shape[-2:]
    slots, _, tile_size, _ = tiles.shape[-4:]
    outer = pltpu.VMEM((rows_dev // 2, width), jnp.bfloat16)
    return pl.pallas_call(
        functools.partial(open_kernel, blocks),
        out_shape=[
            outer,
            outer,
            pltpu.VMEM((2, rows_dev, width), jnp.bfloat16),
            pltpu.VMEM((slots, 2, tile_size, tile_size), jnp.bfloat16),
            pltpu.SMEM((1, slots), jnp.int32),
            pltpu.SMEM((1, slots), jnp.int32),
        ],
        in_specs=[HBM, HBM, SMEM, HBM, HBM],
        out_specs=[VMEM] * 4 + [SMEM] * 2,
        scratch_shapes=[
            pltpu.VMEM((rows_dev, width), jnp.float32),
            pltpu.SemaphoreType.DMA((3,)),
            pltpu.SemaphoreType.DMA((slots,)),
        ],
        **kernel_options("open", 5 * 10**8, 4 * 10**6, 4),
    )(*index, incident, tiles)


def front_kernel(front, blocks, *refs):
    index_refs, sources, tiles, operand = refs[:3], refs[3], refs[4], refs[5]
    own = 3 if front == 0 else 4
    outs, (source_v, sums, sems, *rest) = refs[6:-own], refs[-own:]
    inner_ref, own_refs, outer_refs = outs[0], outs[1:3], outs[3:]
    pair = operand if front == 0 else rest[0]
    tile_size = tiles.shape[-1]
    rows_dev = pair.shape[1]
    packed = rows_dev // 2

    @pl.when(lax.axis_index("layer") == 0)
    def _():
        copies = [pltpu.make_async_copy(sources.at[0, front], source_v, sems.at[0])]
        if front > 0:
            copies.insert(0, pltpu.make_async_copy(operand.at[front], pair.at[0], sems.at[1]))
        for copy in copies:
            copy.start()
        sums[...] = jnp.zeros(sums.shape, jnp.float32)
        if front > 0:
            copies[0].wait()
            for r in range(blocks):
                rows = pl.ds(r * tile_size, tile_size)
                pair[1, rows, :] = turn(pair[0, rows, :].astype(jnp.float32)).astype(jnp.bfloat16)
        accumulate(index_refs, tiles, pair, sums, blocks, outer_window() if front == 0 else None)
        copies[-1].wait()
        inner_start, outer_start = side_starts(rows_dev)
        half = tile_size // 2
        for r in range(blocks):
            own = sums[pl.ds(rows_dev + r * tile_size, tile_size), :]
            own = own + source_v[pl.ds(r * tile_size, tile_size), :].astype(jnp.float32)
            inner = read_block(sums, inner_start, r, tile_size)
            for part in range(PARTS):
                rows = pl.ds(r * half, half)
                own_refs[part][rows, :] = pack(own, part)
                inner_ref[pl.ds(part * packed + r * half, half), :] = pack(inner, part).astype(jnp.bfloat16)
            if front > 0:
                outer = read_block(sums, outer_start, r, tile_size)
                for part in range(PARTS):
                    outer_refs[part][pl.ds(r * half, half), :] = pack(outer, part).astype(jnp.bfloat16)


def kernel_options(name, flops, moved, limit=20):
    return dict(
        compiler_params=pltpu.CompilerParams(vmem_limit_bytes=limit * MIB),
        cost_estimate=pl.CostEstimate(flops=flops, bytes_accessed=moved, transcendentals=0),
        name=name,
    )


def front_products(front, operand, sources, tiles, index, blocks):
    rows_dev, width = sources.shape[-2:]
    tile_size = tiles.shape[-1]
    outer = pltpu.VMEM((rows_dev // 2, width), jnp.bfloat16)
    own = pltpu.VMEM((rows_dev // 2, width), jnp.float32)
    outs = [pltpu.VMEM((rows_dev, width), jnp.bfloat16), own, own] + ([outer, outer] if front else [])
    scratch = [
        pltpu.VMEM((rows_dev, width), jnp.bfloat16),
        pltpu.VMEM((3 * rows_dev + tile_size, width), jnp.float32),
        pltpu.SemaphoreType.DMA((2,)),
    ]
    if front:
        scratch.append(pltpu.VMEM((2, rows_dev, width), jnp.bfloat16))
    return pl.pallas_call(
        functools.partial(front_kernel, front, blocks),
        out_shape=outs,
        in_specs=[SMEM, SMEM, SMEM, HBM, VMEM, HBM if front else VMEM],
        out_specs=[VMEM] * len(outs),
        scratch_shapes=scratch,
        **kernel_options(f"front_{front}", 10**9, 5 * 10**6, 6),
    )(*index, sources, tiles, operand)


def prepare_kernel(wave, front, part, blocks, sources, sums, source_v, sem):
    rows_dev, width = source_v.shape
    tile_size, packed = rows_dev // blocks, rows_dev // 2
    half = tile_size // 2

    @pl.when(lax.axis_index("layer") == wave)
    def _():
        copy = pltpu.make_async_copy(sources.at[0, front], source_v, sem)
        copy.start()
        rest = sums.shape[0] - 2 * packed
        sums[pl.ds(0, packed), :] = jnp.zeros((packed, width), jnp.float32)
        sums[pl.ds(2 * packed, rest), :] = jnp.zeros((rest, width), jnp.float32)
        copy.wait()
        for r in range(blocks):
            source = source_v[pl.ds(r * tile_size, tile_size), :].astype(jnp.float32)
            sums[pl.ds(packed + r * half, half), :] = pack(source, part)


def prepare(wave, front, part, sources, tile_size):
    rows_dev, width = sources.shape[-2:]
    return pl.pallas_call(
        functools.partial(prepare_kernel, wave, front, part, rows_dev // tile_size),
        out_shape=pltpu.VMEM(((3 * rows_dev + tile_size) // 2, width), jnp.float32),
        in_specs=[HBM],
        out_specs=VMEM,
        scratch_shapes=[pltpu.VMEM((rows_dev, width), jnp.bfloat16), pltpu.SemaphoreType.DMA(())],
        **kernel_options(f"prepare_{wave}_{front}_{part}", 10**6, 10**6, 4),
    )(sources)


def chunk_kernel(wave, blocks, *refs):
    rows_s, cols_s, count_s, inbound, tiles, _, outer_ref, inner_ref, sums, operand = refs
    tile_size = tiles.shape[-1]
    packed, width = inbound.shape
    half = tile_size // 2
    first = quarters((half, width))

    @pl.when(lax.axis_index("layer") == wave)
    def _():
        for r in range(blocks):
            value = inbound[pl.ds(r * half, half), :].astype(jnp.float32)
            for j, given in enumerate((value, turn(value))):
                upper = jnp.where(first, given, 0.0)
                lower = jnp.where(first, 0.0, given)
                parts = (
                    upper,
                    pltpu.roll(lower, width - width // 4, 1),
                    pltpu.roll(upper, width // 4, 1),
                    lower,
                )
                for k, part in enumerate(parts):
                    rows = pl.ds((8 * r + 4 * j + k) * half, half)
                    operand[rows, :] = part.astype(jnp.bfloat16)
        start = (lax.axis_index("tile") - 1) * blocks
        count = count_s[0, 0]
        for i in range(tiles.shape[0]):
            live = i < count
            row = jnp.where(live, rows_s[0, i] - start, 3 * blocks)
            column = jnp.where(live, cols_s[0, i], 0)
            rows = pl.ds(pl.multiple_of(column * 4 * tile_size, tile_size), 4 * tile_size)
            target = pl.ds(pl.multiple_of(row * half, half), half)
            left = jnp.concatenate(
                [tiles[i, j, pl.ds(k * half, half), :] for j in range(2) for k in range(2)], axis=1
            )
            sums[target, :] += jnp.dot(left, operand[rows, :], preferred_element_type=jnp.float32)
        inner_start, outer_start = side_starts(packed)
        for ref, begin in ((outer_ref, outer_start), (inner_ref, inner_start)):
            for r in range(blocks):
                ref[pl.ds(r * half, half), :] = read_block(sums, begin, r, half).astype(jnp.bfloat16)


def chunk_products(wave, front, part, inbound, tiles, sums, index, blocks):
    tile_size = tiles.shape[-1]
    packed, width = inbound.shape
    payload = pltpu.VMEM((packed, width), jnp.bfloat16)
    return pl.pallas_call(
        functools.partial(chunk_kernel, wave, blocks),
        out_shape=[payload, payload, pltpu.VMEM(sums.shape, sums.dtype)],
        in_specs=[SMEM, SMEM, SMEM, VMEM, VMEM, VMEM],
        out_specs=[VMEM] * 3,
        scratch_shapes=[pltpu.VMEM((4 * blocks * tile_size, width), jnp.bfloat16)],
        input_output_aliases={5: 2},
        **kernel_options(f"chunk_{wave}_{front}_{part}", 10**9, 5 * 10**6, 4),
    )(*index, inbound, tiles, sums)


def combine_kernel(wave, part, has_through, final, *refs):
    own_ref, inner_ref, outer_ref = refs[:3]
    packed, width = outer_ref.shape
    own_rows = pl.ds(packed if own_ref.shape[0] > packed else 0, packed)
    inner_rows = pl.ds(part * packed if inner_ref.shape[0] > packed else 0, packed)
    total = own_ref[own_rows, :] + inner_ref[inner_rows, :].astype(jnp.float32) + outer_ref[...].astype(jnp.float32)
    if wave > 0:
        active = lax.axis_index("layer") == wave
        total = jnp.where(active, total, refs[3][...].astype(jnp.float32))
    if not (final and part == PARTS - 1):
        out_ref = refs[-2] if has_through else refs[-1]
        out_ref[...] = total.astype(jnp.bfloat16)
        return
    front, blocks, half = final
    out_ref, staged, sems = refs[-3:]
    low, high = refs[4][...].astype(jnp.float32), total
    first = quarters((half, width))
    copies = []
    for r in range(blocks):
        a, b = low[r * half : (r + 1) * half], high[r * half : (r + 1) * half]
        upper = jnp.where(first, a, pltpu.roll(b, width // 4, 1))
        lower = jnp.where(first, pltpu.roll(a, width - width // 4, 1), b)
        staged[pl.ds(2 * r * half, half), :] = upper.astype(jnp.bfloat16)
        staged[pl.ds((2 * r + 1) * half, half), :] = lower.astype(jnp.bfloat16)
        rows = pl.ds(2 * r * half, 2 * half)
        copies.append(pltpu.make_async_copy(staged.at[rows, :], out_ref.at[0, front, rows, :], sems.at[r]))
        copies[-1].start()
    for copy in copies:
        copy.wait()


def combine(wave, front, part, own, inner, outer, earlier=None, through=None, final=None, partner=None, result=None, fronts=0):
    packed, width = outer.shape
    args, specs, aliases, scratch = [own, inner, outer], [VMEM] * 3, {}, []
    if wave > 0:
        args.append(earlier)
        specs.append(VMEM)
    outs, out_specs = [pltpu.VMEM((packed, width), jnp.bfloat16)], [VMEM]
    if through is not None:
        aliases = {len(args): 1}
        args.append(through)
        specs.append(VMEM)
        outs.append(pltpu.VMEM(through.shape, through.dtype))
        out_specs.append(VMEM)
    if final and part == PARTS - 1:
        final = (front, *final)
        args.append(partner)
        specs.append(VMEM)
        outs = [jax.ShapeDtypeStruct((1, fronts, 2 * packed, width), jnp.bfloat16)]
        out_specs = [HBM]
        scratch = [pltpu.VMEM((2 * packed, width), jnp.bfloat16), pltpu.SemaphoreType.DMA((final[1],))]
        if result is not None:
            aliases = {len(args): 0}
            args.append(result)
            specs.append(HBM)
    return pl.pallas_call(
        functools.partial(combine_kernel, wave, part, through is not None, final),
        out_shape=outs,
        in_specs=specs,
        out_specs=out_specs,
        scratch_shapes=scratch,
        input_output_aliases=aliases,
        **kernel_options(f"combine_{wave}_{front}_{part}", 10**6, 10**6, 8),
    )(*args)


def shards(incident, sources, green_tiles, tile_rows, tile_cols, tile_count):
    depth, devices = lax.axis_size("layer"), lax.axis_size("tile")
    layer_route = down_route(depth)
    fronts, rows_dev, _ = incident.shape
    tile_size = green_tiles.shape[-1]
    blocks = rows_dev // tile_size
    index = (in_hbm(tile_rows), in_hbm(tile_cols), tile_count)
    incident, sources, green_tiles = map(in_hbm, (incident, sources, green_tiles))

    def across(payload, wave):
        return lax.ppermute(payload, ("layer", "tile"), outer_route(wave, depth, devices))

    def beside(payload):
        return lax.ppermute(payload, "tile", inner_route(devices))

    def down(payload):
        return lax.ppermute(payload, "layer", layer_route)

    def total(wave, chunk, *args, **kwargs):
        return combine(wave, chunk // PARTS, chunk % PARTS, *args, **kwargs)

    first = open_products(incident, green_tiles, index, blocks)
    payloads, held = list(first[:PARTS]), first[3]
    index = (*first[4:], tile_count)
    chunks = []
    for front in range(fronts):
        made = front_products(front, incident if front else first[2], sources, held, index, blocks)
        inner = beside(made[0])
        payloads += made[3:]
        chunks += [[made[1 + part], inner, None] for part in range(PARTS)]
    for c in range(min(PARTS + 1, len(chunks))):
        chunks[c][2] = across(payloads[c], 0)
    passed, leaving = [], []
    for c in range(len(chunks)):
        behind = c + PARTS
        through = payloads[behind] if PARTS < behind < len(chunks) else None
        made = total(0, c, *chunks[c], through=through)
        if through is not None:
            chunks[behind][2] = across(made[1], 0)
        leaving.append(made[0])
        if depth > 1:
            passed.append(down(made[0]))
    for wave in range(1, depth):
        final = wave == depth - 1
        chunks = []
        for c, inbound in enumerate(passed):
            sums = prepare(wave, c // PARTS, c % PARTS, sources, tile_size)
            outer, inner, own = chunk_products(
                wave, c // PARTS, c % PARTS, inbound, held, sums, index, blocks
            )
            chunks.append((own, beside(inner), across(outer, wave)))
        if final:
            break
        leaving = [total(wave, c, *chunk, leaving[c])[0] for c, chunk in enumerate(chunks)]
        passed = [down(chunk) for chunk in leaving]
    result = partner = None
    for c, chunk in enumerate(chunks):
        (out,) = total(
            depth - 1, c, *chunk, leaving[c],
            final=(blocks, tile_size // 2), partner=partner, result=result, fronts=fronts,
        )
        partner = out
        if c % PARTS == PARTS - 1:
            result = out
    return result


def solution(mesh):
    return jax.shard_map(
        shards,
        mesh=mesh,
        in_specs=(
            P(None, "tile", None),
            P("layer", None, "tile", None),
            P("layer", "tile", None, None, None),
            P("layer", "tile"),
            P("layer", "tile"),
            P("layer", "tile"),
        ),
        out_specs=P("layer", None, "tile", None),
        check_vma=False,
    )
```

```python
import functools

import jax
import jax.numpy as jnp
from jax import lax
from jax.experimental import pallas as pl
from jax.experimental.pallas import tpu as pltpu
from jax.sharding import PartitionSpec as P


MIB = 1 << 20
VMEM = pl.BlockSpec(memory_space=pltpu.VMEM)
HBM = pl.BlockSpec(memory_space=pltpu.HBM)
SMEM = pl.BlockSpec(memory_space=pltpu.SMEM)
PARTS = 2


def inner_route(devices):
    return [(i, i ^ 1) for i in range(devices)]


def outer_route(wave, depth, devices, near):
    twin = (wave + 1) % depth
    near = near and depth > 1
    pairs = []
    for layer in range(depth):
        for i in range(devices):
            to, other = layer, (i + 1 if i % 2 else i - 1)
            if layer != wave and not (near and layer == twin):
                other = i ^ 1
            elif not 0 <= other < devices:
                if near:
                    to, other = (twin if layer == wave else wave), i
                else:
                    other %= devices
            pairs.append((layer * devices + i, to * devices + other))
    return pairs


def down_route(depth):
    return [(i, (i + 1) % depth) for i in range(depth)]


def in_hbm(array):
    return pltpu.with_memory_space_constraint(array, pltpu.HBM)


def quarters(shape):
    return lax.rem(lax.broadcasted_iota(jnp.int32, shape, 1), shape[1] // 2) < shape[1] // 4


def pack(block, part):
    rows, width = block.shape
    upper, lower = block[: rows // 2], block[rows // 2 :]
    if part == 0:
        lower = pltpu.roll(lower, width // 4, 1)
    else:
        upper = pltpu.roll(upper, width - width // 4, 1)
    return jnp.where(quarters(upper.shape), upper, lower)


def turn(value):
    half = value.shape[1] // 2
    moved = pltpu.roll(value, half, 1)
    lane = lax.broadcasted_iota(jnp.int32, value.shape, 1)
    return jnp.where(lane < half, -moved, moved)


def accumulate(index_refs, tiles, pair, sums, blocks, skipped=None):
    rows_s, cols_s, count_s = index_refs
    tile_size = tiles.shape[-1]
    first = (lax.axis_index("tile") - 1) * blocks
    count = count_s[0, 0]
    for i in range(tiles.shape[0]):
        live = i < count
        window = rows_s[0, i] - first
        if skipped is not None:
            live = live & (lax.div(window, blocks) != skipped)
        row = jnp.where(live, window, 3 * blocks)
        column = jnp.where(live, cols_s[0, i], 0)
        rows = pl.ds(pl.multiple_of(column * tile_size, tile_size), tile_size)
        target = pl.ds(pl.multiple_of(row * tile_size, tile_size), tile_size)
        term = jnp.dot(tiles[i, 0], pair[0, rows, :], preferred_element_type=jnp.float32)
        term += jnp.dot(tiles[i, 1], pair[1, rows, :], preferred_element_type=jnp.float32)
        sums[target, :] += term


def side_starts(rows_dev):
    odd = lax.rem(lax.axis_index("tile"), 2)
    return (1 - odd) * 2 * rows_dev, odd * 2 * rows_dev


def read_block(sums, start, r, tile_size):
    return sums[pl.ds(pl.multiple_of(start + r * tile_size, tile_size), tile_size), :]


def outer_window():
    return 2 * lax.rem(lax.axis_index("tile"), 2)


def open_kernel(blocks, *refs):
    index_refs, (incident, stored, *outer_refs), (pair, tiles) = refs[:3], refs[3:7], refs[7:9]
    rows_s, cols_s, sums, sems, tile_sems = refs[9:]
    slots, tile_size = tiles.shape[0], tiles.shape[-1]
    half = tile_size // 2
    active = lax.axis_index("layer") == 0
    copies = [
        pltpu.make_async_copy(index_refs[0], rows_s, sems.at[0]),
        pltpu.make_async_copy(index_refs[1], cols_s, sems.at[1]),
        pltpu.make_async_copy(incident.at[0], pair.at[0], sems.at[2]),
    ]

    def tile_copy(i):
        return pltpu.make_async_copy(stored.at[0, i], tiles.at[i], tile_sems.at[i])

    for copy in copies:
        copy.start()
    early = slots // 4
    for i in range(early):
        tile_copy(i).start()

    @pl.when(active)
    def _():
        sums[...] = jnp.zeros(sums.shape, jnp.float32)

    for copy in copies:
        copy.wait()
    for i in range(early, slots):
        tile_copy(i).start()

    @pl.when(active)
    def _():
        for r in range(blocks):
            rows = pl.ds(r * tile_size, tile_size)
            pair[1, rows, :] = turn(pair[0, rows, :].astype(jnp.float32)).astype(jnp.bfloat16)

    count = index_refs[2][0, 0]
    first = (lax.axis_index("tile") - 1) * blocks

    @pl.loop(0, slots)
    def _(i):
        tile_copy(i).wait()
        window = rows_s[0, i] - first

        @pl.when(active & (i < count) & (lax.div(window, blocks) == outer_window()))
        def _():
            rows = pl.ds(pl.multiple_of(cols_s[0, i] * tile_size, tile_size), tile_size)
            target = pl.ds(pl.multiple_of(lax.rem(window, blocks) * tile_size, tile_size), tile_size)
            term = jnp.dot(tiles[i, 0], pair[0, rows, :], preferred_element_type=jnp.float32)
            term += jnp.dot(tiles[i, 1], pair[1, rows, :], preferred_element_type=jnp.float32)
            sums[target, :] += term

    @pl.when(active)
    def _():
        for r in range(blocks):
            block = sums[pl.ds(r * tile_size, tile_size), :]
            for part in range(PARTS):
                outer_refs[part][pl.ds(r * half, half), :] = pack(block, part).astype(jnp.bfloat16)


def open_products(incident, tiles, index, blocks):
    rows_dev, width = incident.shape[-2:]
    slots, _, tile_size, _ = tiles.shape[-4:]
    outer = pltpu.VMEM((rows_dev // 2, width), jnp.bfloat16)
    return pl.pallas_call(
        functools.partial(open_kernel, blocks),
        out_shape=[
            outer,
            outer,
            pltpu.VMEM((2, rows_dev, width), jnp.bfloat16),
            pltpu.VMEM((slots, 2, tile_size, tile_size), jnp.bfloat16),
            pltpu.SMEM((1, slots), jnp.int32),
            pltpu.SMEM((1, slots), jnp.int32),
        ],
        in_specs=[HBM, HBM, SMEM, HBM, HBM],
        out_specs=[VMEM] * 4 + [SMEM] * 2,
        scratch_shapes=[
            pltpu.VMEM((rows_dev, width), jnp.float32),
            pltpu.SemaphoreType.DMA((3,)),
            pltpu.SemaphoreType.DMA((slots,)),
        ],
        **kernel_options("open", 5 * 10**8, 4 * 10**6, 4),
    )(*index, incident, tiles)


def front_kernel(front, blocks, *refs):
    index_refs, sources, tiles, operand = refs[:3], refs[3], refs[4], refs[5]
    own = 3 if front == 0 else 4
    outs, (source_v, sums, sems, *rest) = refs[6:-own], refs[-own:]
    inner_ref, own_refs, outer_refs = outs[0], outs[1:3], outs[3:]
    pair = operand if front == 0 else rest[0]
    tile_size = tiles.shape[-1]
    rows_dev = pair.shape[1]
    packed = rows_dev // 2

    @pl.when(lax.axis_index("layer") == 0)
    def _():
        copies = [pltpu.make_async_copy(sources.at[0, front], source_v, sems.at[0])]
        if front > 0:
            copies.insert(0, pltpu.make_async_copy(operand.at[front], pair.at[0], sems.at[1]))
        for copy in copies:
            copy.start()
        sums[...] = jnp.zeros(sums.shape, jnp.float32)
        if front > 0:
            copies[0].wait()
            for r in range(blocks):
                rows = pl.ds(r * tile_size, tile_size)
                pair[1, rows, :] = turn(pair[0, rows, :].astype(jnp.float32)).astype(jnp.bfloat16)
        accumulate(index_refs, tiles, pair, sums, blocks, outer_window() if front == 0 else None)
        copies[-1].wait()
        inner_start, outer_start = side_starts(rows_dev)
        half = tile_size // 2
        for r in range(blocks):
            own = sums[pl.ds(rows_dev + r * tile_size, tile_size), :]
            own = own + source_v[pl.ds(r * tile_size, tile_size), :].astype(jnp.float32)
            inner = read_block(sums, inner_start, r, tile_size)
            for part in range(PARTS):
                rows = pl.ds(r * half, half)
                own_refs[part][rows, :] = pack(own, part)
                inner_ref[pl.ds(part * packed + r * half, half), :] = pack(inner, part).astype(jnp.bfloat16)
            if front > 0:
                outer = read_block(sums, outer_start, r, tile_size)
                for part in range(PARTS):
                    outer_refs[part][pl.ds(r * half, half), :] = pack(outer, part).astype(jnp.bfloat16)


def kernel_options(name, flops, moved, limit=20):
    return dict(
        compiler_params=pltpu.CompilerParams(vmem_limit_bytes=limit * MIB),
        cost_estimate=pl.CostEstimate(flops=flops, bytes_accessed=moved, transcendentals=0),
        name=name,
    )


def front_products(front, operand, sources, tiles, index, blocks):
    rows_dev, width = sources.shape[-2:]
    tile_size = tiles.shape[-1]
    outer = pltpu.VMEM((rows_dev // 2, width), jnp.bfloat16)
    own = pltpu.VMEM((rows_dev // 2, width), jnp.float32)
    outs = [pltpu.VMEM((rows_dev, width), jnp.bfloat16), own, own] + ([outer, outer] if front else [])
    scratch = [
        pltpu.VMEM((rows_dev, width), jnp.bfloat16),
        pltpu.VMEM((3 * rows_dev + tile_size, width), jnp.float32),
        pltpu.SemaphoreType.DMA((2,)),
    ]
    if front:
        scratch.append(pltpu.VMEM((2, rows_dev, width), jnp.bfloat16))
    return pl.pallas_call(
        functools.partial(front_kernel, front, blocks),
        out_shape=outs,
        in_specs=[SMEM, SMEM, SMEM, HBM, VMEM, HBM if front else VMEM],
        out_specs=[VMEM] * len(outs),
        scratch_shapes=scratch,
        **kernel_options(f"front_{front}", 10**9, 5 * 10**6, 6),
    )(*index, sources, tiles, operand)


def prepare_kernel(wave, front, part, blocks, sources, sums, source_v, sem):
    rows_dev, width = source_v.shape
    tile_size, packed = rows_dev // blocks, rows_dev // 2
    half = tile_size // 2

    @pl.when(lax.axis_index("layer") == wave)
    def _():
        copy = pltpu.make_async_copy(sources.at[0, front], source_v, sem)
        copy.start()
        rest = sums.shape[0] - 2 * packed
        sums[pl.ds(0, packed), :] = jnp.zeros((packed, width), jnp.float32)
        sums[pl.ds(2 * packed, rest), :] = jnp.zeros((rest, width), jnp.float32)
        copy.wait()
        for r in range(blocks):
            source = source_v[pl.ds(r * tile_size, tile_size), :].astype(jnp.float32)
            sums[pl.ds(packed + r * half, half), :] = pack(source, part)


def prepare(wave, front, part, sources, tile_size):
    rows_dev, width = sources.shape[-2:]
    return pl.pallas_call(
        functools.partial(prepare_kernel, wave, front, part, rows_dev // tile_size),
        out_shape=pltpu.VMEM(((3 * rows_dev + tile_size) // 2, width), jnp.float32),
        in_specs=[HBM],
        out_specs=VMEM,
        scratch_shapes=[pltpu.VMEM((rows_dev, width), jnp.bfloat16), pltpu.SemaphoreType.DMA(())],
        **kernel_options(f"prepare_{wave}_{front}_{part}", 10**6, 10**6, 4),
    )(sources)


def chunk_kernel(wave, blocks, *refs):
    rows_s, cols_s, count_s, inbound, tiles, _, outer_ref, inner_ref, sums, operand = refs
    tile_size = tiles.shape[-1]
    packed, width = inbound.shape
    half = tile_size // 2
    first = quarters((half, width))

    @pl.when(lax.axis_index("layer") == wave)
    def _():
        for r in range(blocks):
            value = inbound[pl.ds(r * half, half), :].astype(jnp.float32)
            for j, given in enumerate((value, turn(value))):
                upper = jnp.where(first, given, 0.0)
                lower = jnp.where(first, 0.0, given)
                parts = (
                    upper,
                    pltpu.roll(lower, width - width // 4, 1),
                    pltpu.roll(upper, width // 4, 1),
                    lower,
                )
                for k, part in enumerate(parts):
                    rows = pl.ds((8 * r + 4 * j + k) * half, half)
                    operand[rows, :] = part.astype(jnp.bfloat16)
        start = (lax.axis_index("tile") - 1) * blocks
        count = count_s[0, 0]
        for i in range(tiles.shape[0]):
            live = i < count
            row = jnp.where(live, rows_s[0, i] - start, 3 * blocks)
            column = jnp.where(live, cols_s[0, i], 0)
            rows = pl.ds(pl.multiple_of(column * 4 * tile_size, tile_size), 4 * tile_size)
            target = pl.ds(pl.multiple_of(row * half, half), half)
            left = jnp.concatenate(
                [tiles[i, j, pl.ds(k * half, half), :] for j in range(2) for k in range(2)], axis=1
            )
            sums[target, :] += jnp.dot(left, operand[rows, :], preferred_element_type=jnp.float32)
        inner_start, outer_start = side_starts(packed)
        for ref, begin in ((outer_ref, outer_start), (inner_ref, inner_start)):
            for r in range(blocks):
                ref[pl.ds(r * half, half), :] = read_block(sums, begin, r, half).astype(jnp.bfloat16)


def chunk_products(wave, front, part, inbound, tiles, sums, index, blocks):
    tile_size = tiles.shape[-1]
    packed, width = inbound.shape
    payload = pltpu.VMEM((packed, width), jnp.bfloat16)
    return pl.pallas_call(
        functools.partial(chunk_kernel, wave, blocks),
        out_shape=[payload, payload, pltpu.VMEM(sums.shape, sums.dtype)],
        in_specs=[SMEM, SMEM, SMEM, VMEM, VMEM, VMEM],
        out_specs=[VMEM] * 3,
        scratch_shapes=[pltpu.VMEM((4 * blocks * tile_size, width), jnp.bfloat16)],
        input_output_aliases={5: 2},
        **kernel_options(f"chunk_{wave}_{front}_{part}", 10**9, 5 * 10**6, 4),
    )(*index, inbound, tiles, sums)


def combine_kernel(wave, part, has_through, final, devices, *refs):
    own_ref, inner_ref, outer_ref = refs[:3]
    partner = lax.axis_index("tile") + outer_window() - 1
    outer = jnp.where((partner >= 0) & (partner < devices), outer_ref[...].astype(jnp.float32), 0.0)
    packed, width = outer_ref.shape
    own_rows = pl.ds(packed if own_ref.shape[0] > packed else 0, packed)
    inner_rows = pl.ds(part * packed if inner_ref.shape[0] > packed else 0, packed)
    total = own_ref[own_rows, :] + inner_ref[inner_rows, :].astype(jnp.float32) + outer
    if wave > 0:
        active = lax.axis_index("layer") == wave
        total = jnp.where(active, total, refs[3][...].astype(jnp.float32))
    if not (final and part == PARTS - 1):
        out_ref = refs[-2] if has_through else refs[-1]
        out_ref[...] = total.astype(jnp.bfloat16)
        return
    front, blocks, half = final
    out_ref, staged, sems = refs[-3:]
    low, high = refs[4][...].astype(jnp.float32), total
    first = quarters((half, width))
    copies = []
    for r in range(blocks):
        a, b = low[r * half : (r + 1) * half], high[r * half : (r + 1) * half]
        upper = jnp.where(first, a, pltpu.roll(b, width // 4, 1))
        lower = jnp.where(first, pltpu.roll(a, width - width // 4, 1), b)
        staged[pl.ds(2 * r * half, half), :] = upper.astype(jnp.bfloat16)
        staged[pl.ds((2 * r + 1) * half, half), :] = lower.astype(jnp.bfloat16)
        rows = pl.ds(2 * r * half, 2 * half)
        copies.append(pltpu.make_async_copy(staged.at[rows, :], out_ref.at[0, front, rows, :], sems.at[r]))
        copies[-1].start()
    for copy in copies:
        copy.wait()


def combine(wave, front, part, own, inner, outer, earlier=None, through=None, final=None, partner=None, result=None, fronts=0):
    packed, width = outer.shape
    args, specs, aliases, scratch = [own, inner, outer], [VMEM] * 3, {}, []
    if wave > 0:
        args.append(earlier)
        specs.append(VMEM)
    outs, out_specs = [pltpu.VMEM((packed, width), jnp.bfloat16)], [VMEM]
    if through is not None:
        aliases = {len(args): 1}
        args.append(through)
        specs.append(VMEM)
        outs.append(pltpu.VMEM(through.shape, through.dtype))
        out_specs.append(VMEM)
    if final and part == PARTS - 1:
        final = (front, *final)
        args.append(partner)
        specs.append(VMEM)
        outs = [jax.ShapeDtypeStruct((1, fronts, 2 * packed, width), jnp.bfloat16)]
        out_specs = [HBM]
        scratch = [pltpu.VMEM((2 * packed, width), jnp.bfloat16), pltpu.SemaphoreType.DMA((final[1],))]
        if result is not None:
            aliases = {len(args): 0}
            args.append(result)
            specs.append(HBM)
    return pl.pallas_call(
        functools.partial(combine_kernel, wave, part, through is not None, final, lax.axis_size("tile")),
        out_shape=outs,
        in_specs=specs,
        out_specs=out_specs,
        scratch_shapes=scratch,
        input_output_aliases=aliases,
        **kernel_options(f"combine_{wave}_{front}_{part}", 10**6, 10**6, 8),
    )(*args)


def shards(incident, sources, green_tiles, tile_rows, tile_cols, tile_count):
    depth, devices = lax.axis_size("layer"), lax.axis_size("tile")
    layer_route = down_route(depth)
    fronts, rows_dev, _ = incident.shape
    tile_size = green_tiles.shape[-1]
    blocks = rows_dev // tile_size
    index = (in_hbm(tile_rows), in_hbm(tile_cols), tile_count)
    incident, sources, green_tiles = map(in_hbm, (incident, sources, green_tiles))

    def across(payload, wave, chunk):
        return lax.ppermute(payload, ("layer", "tile"), outer_route(wave, depth, devices, wave == 0 and chunk < PARTS))

    def beside(payload):
        return lax.ppermute(payload, "tile", inner_route(devices))

    def down(payload):
        return lax.ppermute(payload, "layer", layer_route)

    def total(wave, chunk, *args, **kwargs):
        return combine(wave, chunk // PARTS, chunk % PARTS, *args, **kwargs)

    first = open_products(incident, green_tiles, index, blocks)
    payloads, held = list(first[:PARTS]), first[3]
    index = (*first[4:], tile_count)
    chunks = []
    for front in range(fronts):
        made = front_products(front, incident if front else first[2], sources, held, index, blocks)
        inner = beside(made[0])
        payloads += made[3:]
        chunks += [[made[1 + part], inner, None] for part in range(PARTS)]
    for c in range(min(PARTS + 1, len(chunks))):
        chunks[c][2] = across(payloads[c], 0, c)
    passed, leaving = [], []
    for c in range(len(chunks)):
        behind = c + PARTS
        through = payloads[behind] if PARTS < behind < len(chunks) else None
        made = total(0, c, *chunks[c], through=through)
        if through is not None:
            chunks[behind][2] = across(made[1], 0, behind)
        leaving.append(made[0])
        if depth > 1:
            passed.append(down(made[0]))
    for wave in range(1, depth):
        final = wave == depth - 1
        chunks = []
        for c, inbound in enumerate(passed):
            sums = prepare(wave, c // PARTS, c % PARTS, sources, tile_size)
            outer, inner, own = chunk_products(
                wave, c // PARTS, c % PARTS, inbound, held, sums, index, blocks
            )
            chunks.append((own, beside(inner), across(outer, wave, c)))
        if final:
            break
        leaving = [total(wave, c, *chunk, leaving[c])[0] for c, chunk in enumerate(chunks)]
        passed = [down(chunk) for chunk in leaving]
    result = partner = None
    for c, chunk in enumerate(chunks):
        (out,) = total(
            depth - 1, c, *chunk, leaving[c],
            final=(blocks, tile_size // 2), partner=partner, result=result, fronts=fronts,
        )
        partner = out
        if c % PARTS == PARTS - 1:
            result = out
    return result


def solution(mesh):
    return jax.shard_map(
        shards,
        mesh=mesh,
        in_specs=(
            P(None, "tile", None),
            P("layer", None, "tile", None),
            P("layer", "tile", None, None, None),
            P("layer", "tile"),
            P("layer", "tile"),
            P("layer", "tile"),
        ),
        out_specs=P("layer", None, "tile", None),
        check_vma=False,
    )
```

```python
import functools

import jax
import jax.numpy as jnp
from jax import lax
from jax.experimental import pallas as pl
from jax.experimental.pallas import tpu as pltpu
from jax.sharding import PartitionSpec as P


MIB = 1 << 20
VMEM = pl.BlockSpec(memory_space=pltpu.VMEM)
HBM = pl.BlockSpec(memory_space=pltpu.HBM)
SMEM = pl.BlockSpec(memory_space=pltpu.SMEM)
PARTS = 2


def inner_route(devices):
    return [(i, i ^ 1) for i in range(devices)]


def outer_route(wave, depth, devices):
    pairs = []
    for layer in range(depth):
        for i in range(devices):
            other = (i + 1 if i % 2 else i - 1) % devices if layer == wave else i ^ 1
            pairs.append((layer * devices + i, layer * devices + other))
    return pairs


def down_route(depth):
    return [(i, (i + 1) % depth) for i in range(depth)]


def in_hbm(array):
    return pltpu.with_memory_space_constraint(array, pltpu.HBM)


def quarters(shape):
    return lax.rem(lax.broadcasted_iota(jnp.int32, shape, 1), shape[1] // 2) < shape[1] // 4


def pack(block, part):
    rows, width = block.shape
    upper, lower = block[: rows // 2], block[rows // 2 :]
    if part == 0:
        lower = pltpu.roll(lower, width // 4, 1)
    else:
        upper = pltpu.roll(upper, width - width // 4, 1)
    return jnp.where(quarters(upper.shape), upper, lower)


def turn(value):
    half = value.shape[1] // 2
    moved = pltpu.roll(value, half, 1)
    lane = lax.broadcasted_iota(jnp.int32, value.shape, 1)
    return jnp.where(lane < half, -moved, moved)


def accumulate(index_refs, tiles, pair, sums, blocks, skipped=None):
    rows_s, cols_s, count_s = index_refs
    tile_size = tiles.shape[-1]
    first = (lax.axis_index("tile") - 1) * blocks
    count = count_s[0, 0]
    for i in range(tiles.shape[0]):
        live = i < count
        window = rows_s[0, i] - first
        if skipped is not None:
            live = live & (lax.div(window, blocks) != skipped)
        row = jnp.where(live, window, 3 * blocks)
        column = jnp.where(live, cols_s[0, i], 0)
        rows = pl.ds(pl.multiple_of(column * tile_size, tile_size), tile_size)
        target = pl.ds(pl.multiple_of(row * tile_size, tile_size), tile_size)
        term = jnp.dot(tiles[i, 0], pair[0, rows, :], preferred_element_type=jnp.float32)
        term += jnp.dot(tiles[i, 1], pair[1, rows, :], preferred_element_type=jnp.float32)
        sums[target, :] += term


def side_starts(rows_dev):
    odd = lax.rem(lax.axis_index("tile"), 2)
    return (1 - odd) * 2 * rows_dev, odd * 2 * rows_dev


def read_block(sums, start, r, tile_size):
    return sums[pl.ds(pl.multiple_of(start + r * tile_size, tile_size), tile_size), :]


def outer_window():
    return 2 * lax.rem(lax.axis_index("tile"), 2)


def open_kernel(blocks, *refs):
    index_refs, (incident, stored, *outer_refs), (pair, tiles) = refs[:3], refs[3:7], refs[7:9]
    rows_s, cols_s, sums, sems, tile_sems = refs[9:]
    slots, tile_size = tiles.shape[0], tiles.shape[-1]
    half = tile_size // 2
    active = lax.axis_index("layer") == 0
    copies = [
        pltpu.make_async_copy(index_refs[0], rows_s, sems.at[0]),
        pltpu.make_async_copy(index_refs[1], cols_s, sems.at[1]),
        pltpu.make_async_copy(incident.at[0], pair.at[0], sems.at[2]),
    ]

    def tile_copy(i):
        return pltpu.make_async_copy(stored.at[0, i], tiles.at[i], tile_sems.at[i])

    for copy in copies:
        copy.start()
    early = slots // 4
    for i in range(early):
        tile_copy(i).start()

    @pl.when(active)
    def _():
        sums[...] = jnp.zeros(sums.shape, jnp.float32)

    for copy in copies:
        copy.wait()
    for i in range(early, slots):
        tile_copy(i).start()

    @pl.when(active)
    def _():
        for r in range(blocks):
            rows = pl.ds(r * tile_size, tile_size)
            pair[1, rows, :] = turn(pair[0, rows, :].astype(jnp.float32)).astype(jnp.bfloat16)

    count = index_refs[2][0, 0]
    first = (lax.axis_index("tile") - 1) * blocks

    @pl.loop(0, slots)
    def _(i):
        tile_copy(i).wait()
        window = rows_s[0, i] - first

        @pl.when(active & (i < count) & (lax.div(window, blocks) == outer_window()))
        def _():
            rows = pl.ds(pl.multiple_of(cols_s[0, i] * tile_size, tile_size), tile_size)
            target = pl.ds(pl.multiple_of(lax.rem(window, blocks) * tile_size, tile_size), tile_size)
            term = jnp.dot(tiles[i, 0], pair[0, rows, :], preferred_element_type=jnp.float32)
            term += jnp.dot(tiles[i, 1], pair[1, rows, :], preferred_element_type=jnp.float32)
            sums[target, :] += term

    @pl.when(active)
    def _():
        for r in range(blocks):
            block = sums[pl.ds(r * tile_size, tile_size), :]
            for part in range(PARTS):
                outer_refs[part][pl.ds(r * half, half), :] = pack(block, part).astype(jnp.bfloat16)


def open_products(incident, tiles, index, blocks):
    rows_dev, width = incident.shape[-2:]
    slots, _, tile_size, _ = tiles.shape[-4:]
    outer = pltpu.VMEM((rows_dev // 2, width), jnp.bfloat16)
    return pl.pallas_call(
        functools.partial(open_kernel, blocks),
        out_shape=[
            outer,
            outer,
            pltpu.VMEM((2, rows_dev, width), jnp.bfloat16),
            pltpu.VMEM((slots, 2, tile_size, tile_size), jnp.bfloat16),
            pltpu.SMEM((1, slots), jnp.int32),
            pltpu.SMEM((1, slots), jnp.int32),
        ],
        in_specs=[HBM, HBM, SMEM, HBM, HBM],
        out_specs=[VMEM] * 4 + [SMEM] * 2,
        scratch_shapes=[
            pltpu.VMEM((rows_dev, width), jnp.float32),
            pltpu.SemaphoreType.DMA((3,)),
            pltpu.SemaphoreType.DMA((slots,)),
        ],
        **kernel_options("open", 5 * 10**8, 4 * 10**6, 4),
    )(*index, incident, tiles)


def front_kernel(front, blocks, *refs):
    index_refs, sources, tiles, operand = refs[:3], refs[3], refs[4], refs[5]
    own = 3 if front == 0 else 4
    outs, (source_v, sums, sems, *rest) = refs[6:-own], refs[-own:]
    inner_ref, own_refs, outer_refs = outs[0], outs[1:3], outs[3:]
    pair = operand if front == 0 else rest[0]
    tile_size = tiles.shape[-1]
    rows_dev = pair.shape[1]
    packed = rows_dev // 2

    @pl.when(lax.axis_index("layer") == 0)
    def _():
        copies = [pltpu.make_async_copy(sources.at[0, front], source_v, sems.at[0])]
        if front > 0:
            copies.insert(0, pltpu.make_async_copy(operand.at[front], pair.at[0], sems.at[1]))
        for copy in copies:
            copy.start()
        sums[...] = jnp.zeros(sums.shape, jnp.float32)
        if front > 0:
            copies[0].wait()
            for r in range(blocks):
                rows = pl.ds(r * tile_size, tile_size)
                pair[1, rows, :] = turn(pair[0, rows, :].astype(jnp.float32)).astype(jnp.bfloat16)
        accumulate(index_refs, tiles, pair, sums, blocks, outer_window() if front == 0 else None)
        copies[-1].wait()
        inner_start, outer_start = side_starts(rows_dev)
        half = tile_size // 2
        for r in range(blocks):
            own = sums[pl.ds(rows_dev + r * tile_size, tile_size), :]
            own = own + source_v[pl.ds(r * tile_size, tile_size), :].astype(jnp.float32)
            inner = read_block(sums, inner_start, r, tile_size)
            for part in range(PARTS):
                rows = pl.ds(r * half, half)
                own_refs[part][rows, :] = pack(own, part)
                inner_ref[pl.ds(part * packed + r * half, half), :] = pack(inner, part).astype(jnp.bfloat16)
            if front > 0:
                outer = read_block(sums, outer_start, r, tile_size)
                for part in range(PARTS):
                    outer_refs[part][pl.ds(r * half, half), :] = pack(outer, part).astype(jnp.bfloat16)


def kernel_options(name, flops, moved, limit=20):
    return dict(
        compiler_params=pltpu.CompilerParams(vmem_limit_bytes=limit * MIB),
        cost_estimate=pl.CostEstimate(flops=flops, bytes_accessed=moved, transcendentals=0),
        name=name,
    )


def front_products(front, operand, sources, tiles, index, blocks):
    rows_dev, width = sources.shape[-2:]
    tile_size = tiles.shape[-1]
    outer = pltpu.VMEM((rows_dev // 2, width), jnp.bfloat16)
    own = pltpu.VMEM((rows_dev // 2, width), jnp.float32)
    outs = [pltpu.VMEM((rows_dev, width), jnp.bfloat16), own, own] + ([outer, outer] if front else [])
    scratch = [
        pltpu.VMEM((rows_dev, width), jnp.bfloat16),
        pltpu.VMEM((3 * rows_dev + tile_size, width), jnp.float32),
        pltpu.SemaphoreType.DMA((2,)),
    ]
    if front:
        scratch.append(pltpu.VMEM((2, rows_dev, width), jnp.bfloat16))
    return pl.pallas_call(
        functools.partial(front_kernel, front, blocks),
        out_shape=outs,
        in_specs=[SMEM, SMEM, SMEM, HBM, VMEM, HBM if front else VMEM],
        out_specs=[VMEM] * len(outs),
        scratch_shapes=scratch,
        **kernel_options(f"front_{front}", 10**9, 5 * 10**6, 6),
    )(*index, sources, tiles, operand)


def prepare_kernel(wave, front, part, blocks, sources, sums, source_v, sem):
    rows_dev, width = source_v.shape
    tile_size, packed = rows_dev // blocks, rows_dev // 2
    half = tile_size // 2

    @pl.when(lax.axis_index("layer") == wave)
    def _():
        copy = pltpu.make_async_copy(sources.at[0, front], source_v, sem)
        copy.start()
        rest = sums.shape[0] - 2 * packed
        sums[pl.ds(0, packed), :] = jnp.zeros((packed, width), jnp.float32)
        sums[pl.ds(2 * packed, rest), :] = jnp.zeros((rest, width), jnp.float32)
        copy.wait()
        for r in range(blocks):
            source = source_v[pl.ds(r * tile_size, tile_size), :].astype(jnp.float32)
            sums[pl.ds(packed + r * half, half), :] = pack(source, part)


def prepare(wave, front, part, sources, tile_size):
    rows_dev, width = sources.shape[-2:]
    return pl.pallas_call(
        functools.partial(prepare_kernel, wave, front, part, rows_dev // tile_size),
        out_shape=pltpu.VMEM(((3 * rows_dev + tile_size) // 2, width), jnp.float32),
        in_specs=[HBM],
        out_specs=VMEM,
        scratch_shapes=[pltpu.VMEM((rows_dev, width), jnp.bfloat16), pltpu.SemaphoreType.DMA(())],
        **kernel_options(f"prepare_{wave}_{front}_{part}", 10**6, 10**6, 4),
    )(sources)


def chunk_kernel(wave, blocks, *refs):
    rows_s, cols_s, count_s, inbound, tiles, _, outer_ref, inner_ref, sums, operand = refs
    tile_size = tiles.shape[-1]
    packed, width = inbound.shape
    half = tile_size // 2
    first = quarters((half, width))

    @pl.when(lax.axis_index("layer") == wave)
    def _():
        for r in range(blocks):
            value = inbound[pl.ds(r * half, half), :].astype(jnp.float32)
            for j, given in enumerate((value, turn(value))):
                upper = jnp.where(first, given, 0.0)
                lower = jnp.where(first, 0.0, given)
                parts = (
                    upper,
                    pltpu.roll(lower, width - width // 4, 1),
                    pltpu.roll(upper, width // 4, 1),
                    lower,
                )
                for k, part in enumerate(parts):
                    rows = pl.ds((8 * r + 4 * j + k) * half, half)
                    operand[rows, :] = part.astype(jnp.bfloat16)
        start = (lax.axis_index("tile") - 1) * blocks
        count = count_s[0, 0]
        for i in range(tiles.shape[0]):
            live = i < count
            row = jnp.where(live, rows_s[0, i] - start, 3 * blocks)
            column = jnp.where(live, cols_s[0, i], 0)
            rows = pl.ds(pl.multiple_of(column * 4 * tile_size, tile_size), 4 * tile_size)
            target = pl.ds(pl.multiple_of(row * half, half), half)
            left = jnp.concatenate(
                [tiles[i, j, pl.ds(k * half, half), :] for j in range(2) for k in range(2)], axis=1
            )
            sums[target, :] += jnp.dot(left, operand[rows, :], preferred_element_type=jnp.float32)
        inner_start, outer_start = side_starts(packed)
        for ref, begin in ((outer_ref, outer_start), (inner_ref, inner_start)):
            for r in range(blocks):
                ref[pl.ds(r * half, half), :] = read_block(sums, begin, r, half).astype(jnp.bfloat16)


def chunk_products(wave, front, part, inbound, tiles, sums, index, blocks):
    tile_size = tiles.shape[-1]
    packed, width = inbound.shape
    payload = pltpu.VMEM((packed, width), jnp.bfloat16)
    return pl.pallas_call(
        functools.partial(chunk_kernel, wave, blocks),
        out_shape=[payload, payload, pltpu.VMEM(sums.shape, sums.dtype)],
        in_specs=[SMEM, SMEM, SMEM, VMEM, VMEM, VMEM],
        out_specs=[VMEM] * 3,
        scratch_shapes=[pltpu.VMEM((4 * blocks * tile_size, width), jnp.bfloat16)],
        input_output_aliases={5: 2},
        **kernel_options(f"chunk_{wave}_{front}_{part}", 10**9, 5 * 10**6, 4),
    )(*index, inbound, tiles, sums)


def combine_kernel(wave, part, has_through, final, devices, *refs):
    own_ref, inner_ref, outer_ref = refs[:3]
    partner = lax.axis_index("tile") + outer_window() - 1
    outer = jnp.where((partner >= 0) & (partner < devices), outer_ref[...].astype(jnp.float32), 0.0)
    packed, width = outer_ref.shape
    own_rows = pl.ds(packed if own_ref.shape[0] > packed else 0, packed)
    inner_rows = pl.ds(part * packed if inner_ref.shape[0] > packed else 0, packed)
    total = own_ref[own_rows, :] + inner_ref[inner_rows, :].astype(jnp.float32) + outer
    if wave > 0:
        active = lax.axis_index("layer") == wave
        total = jnp.where(active, total, refs[3][...].astype(jnp.float32))
    if not (final and part == PARTS - 1):
        out_ref = refs[-2] if has_through else refs[-1]
        out_ref[...] = total.astype(jnp.bfloat16)
        return
    front, blocks, half = final
    out_ref, staged, sems = refs[-3:]
    low, high = refs[4][...].astype(jnp.float32), total
    first = quarters((half, width))
    copies = []
    for r in range(blocks):
        a, b = low[r * half : (r + 1) * half], high[r * half : (r + 1) * half]
        upper = jnp.where(first, a, pltpu.roll(b, width // 4, 1))
        lower = jnp.where(first, pltpu.roll(a, width - width // 4, 1), b)
        staged[pl.ds(2 * r * half, half), :] = upper.astype(jnp.bfloat16)
        staged[pl.ds((2 * r + 1) * half, half), :] = lower.astype(jnp.bfloat16)
        rows = pl.ds(2 * r * half, 2 * half)
        copies.append(pltpu.make_async_copy(staged.at[rows, :], out_ref.at[0, front, rows, :], sems.at[r]))
        copies[-1].start()
    for copy in copies:
        copy.wait()


def combine(wave, front, part, own, inner, outer, earlier=None, through=None, final=None, partner=None, result=None, fronts=0):
    packed, width = outer.shape
    args, specs, aliases, scratch = [own, inner, outer], [VMEM] * 3, {}, []
    if wave > 0:
        args.append(earlier)
        specs.append(VMEM)
    outs, out_specs = [pltpu.VMEM((packed, width), jnp.bfloat16)], [VMEM]
    if through is not None:
        aliases = {len(args): 1}
        args.append(through)
        specs.append(VMEM)
        outs.append(pltpu.VMEM(through.shape, through.dtype))
        out_specs.append(VMEM)
    if final and part == PARTS - 1:
        final = (front, *final)
        args.append(partner)
        specs.append(VMEM)
        outs = [jax.ShapeDtypeStruct((1, fronts, 2 * packed, width), jnp.bfloat16)]
        out_specs = [HBM]
        scratch = [pltpu.VMEM((2 * packed, width), jnp.bfloat16), pltpu.SemaphoreType.DMA((final[1],))]
        if result is not None:
            aliases = {len(args): 0}
            args.append(result)
            specs.append(HBM)
    return pl.pallas_call(
        functools.partial(combine_kernel, wave, part, through is not None, final, lax.axis_size("tile")),
        out_shape=outs,
        in_specs=specs,
        out_specs=out_specs,
        scratch_shapes=scratch,
        input_output_aliases=aliases,
        **kernel_options(f"combine_{wave}_{front}_{part}", 10**6, 10**6, 8),
    )(*args)


def shards(incident, sources, green_tiles, tile_rows, tile_cols, tile_count):
    depth, devices = lax.axis_size("layer"), lax.axis_size("tile")
    layer_route = down_route(depth)
    fronts, rows_dev, _ = incident.shape
    tile_size = green_tiles.shape[-1]
    blocks = rows_dev // tile_size
    index = (in_hbm(tile_rows), in_hbm(tile_cols), tile_count)
    incident, sources, green_tiles = map(in_hbm, (incident, sources, green_tiles))

    def across(payload, wave):
        return lax.ppermute(payload, ("layer", "tile"), outer_route(wave, depth, devices))

    def beside(payload):
        return lax.ppermute(payload, "tile", inner_route(devices))

    def down(payload):
        return lax.ppermute(payload, "layer", layer_route)

    def total(wave, chunk, *args, **kwargs):
        return combine(wave, chunk // PARTS, chunk % PARTS, *args, **kwargs)

    first = open_products(incident, green_tiles, index, blocks)
    payloads, held = list(first[:PARTS]), first[3]
    index = (*first[4:], tile_count)
    chunks = []
    for front in range(fronts):
        made = front_products(front, incident if front else first[2], sources, held, index, blocks)
        inner = beside(made[0])
        payloads += made[3:]
        chunks += [[made[1 + part], inner, None] for part in range(PARTS)]
    for c in range(min(PARTS + 1, len(chunks))):
        chunks[c][2] = across(payloads[c], 0)
    passed, leaving = [], []
    for c in range(len(chunks)):
        behind = c + PARTS
        through = payloads[behind] if PARTS < behind < len(chunks) else None
        made = total(0, c, *chunks[c], through=through)
        if through is not None:
            chunks[behind][2] = across(made[1], 0)
        leaving.append(made[0])
        if depth > 1:
            passed.append(down(made[0]))
    for wave in range(1, depth):
        final = wave == depth - 1
        chunks = []
        for c, inbound in enumerate(passed):
            sums = prepare(wave, c // PARTS, c % PARTS, sources, tile_size)
            outer, inner, own = chunk_products(
                wave, c // PARTS, c % PARTS, inbound, held, sums, index, blocks
            )
            chunks.append((own, beside(inner), across(outer, wave)))
        if final:
            break
        leaving = [total(wave, c, *chunk, leaving[c])[0] for c, chunk in enumerate(chunks)]
        passed = [down(chunk) for chunk in leaving]
    result = partner = None
    for c, chunk in enumerate(chunks):
        (out,) = total(
            depth - 1, c, *chunk, leaving[c],
            final=(blocks, tile_size // 2), partner=partner, result=result, fronts=fronts,
        )
        partner = out
        if c % PARTS == PARTS - 1:
            result = out
    return result


def solution(mesh):
    return jax.shard_map(
        shards,
        mesh=mesh,
        in_specs=(
            P(None, "tile", None),
            P("layer", None, "tile", None),
            P("layer", "tile", None, None, None),
            P("layer", "tile"),
            P("layer", "tile"),
            P("layer", "tile"),
        ),
        out_specs=P("layer", None, "tile", None),
        check_vma=False,
    )
```

```python
import functools

import jax
import jax.numpy as jnp
from jax import lax
from jax.experimental import pallas as pl
from jax.experimental.pallas import tpu as pltpu
from jax.sharding import PartitionSpec as P


MIB = 1 << 20
VMEM = pl.BlockSpec(memory_space=pltpu.VMEM)
HBM = pl.BlockSpec(memory_space=pltpu.HBM)
SMEM = pl.BlockSpec(memory_space=pltpu.SMEM)
PARTS = 2


def inner_route(devices):
    return [(i, i ^ 1) for i in range(devices)]


def outer_route(wave, depth, devices):
    pairs = []
    for layer in range(depth):
        for i in range(devices):
            other = (i + 1 if i % 2 else i - 1) % devices if layer == wave else i ^ 1
            pairs.append((layer * devices + i, layer * devices + other))
    return pairs


def down_route(depth):
    return [(i, (i + 1) % depth) for i in range(depth)]


def in_hbm(array):
    return pltpu.with_memory_space_constraint(array, pltpu.HBM)


def quarters(shape):
    return lax.rem(lax.broadcasted_iota(jnp.int32, shape, 1), shape[1] // 2) < shape[1] // 4


def pack(block, part):
    rows, width = block.shape
    upper, lower = block[: rows // 2], block[rows // 2 :]
    if part == 0:
        lower = pltpu.roll(lower, width // 4, 1)
    else:
        upper = pltpu.roll(upper, width - width // 4, 1)
    return jnp.where(quarters(upper.shape), upper, lower)


def turn(value):
    half = value.shape[1] // 2
    moved = pltpu.roll(value, half, 1)
    lane = lax.broadcasted_iota(jnp.int32, value.shape, 1)
    return jnp.where(lane < half, -moved, moved)


def accumulate(index_refs, tiles, pair, sums, blocks, skipped=None):
    rows_s, cols_s, count_s = index_refs
    tile_size = tiles.shape[-1]
    first = (lax.axis_index("tile") - 1) * blocks
    count = count_s[0, 0]
    for i in range(tiles.shape[0]):
        live = i < count
        window = rows_s[0, i] - first
        if skipped is not None:
            live = live & (lax.div(window, blocks) != skipped)
        row = jnp.where(live, window, 3 * blocks)
        column = jnp.where(live, cols_s[0, i], 0)
        rows = pl.ds(pl.multiple_of(column * tile_size, tile_size), tile_size)
        target = pl.ds(pl.multiple_of(row * tile_size, tile_size), tile_size)
        term = jnp.dot(tiles[i, 0], pair[0, rows, :], preferred_element_type=jnp.float32)
        term += jnp.dot(tiles[i, 1], pair[1, rows, :], preferred_element_type=jnp.float32)
        sums[target, :] += term


def side_starts(rows_dev):
    odd = lax.rem(lax.axis_index("tile"), 2)
    return (1 - odd) * 2 * rows_dev, odd * 2 * rows_dev


def read_block(sums, start, r, tile_size):
    return sums[pl.ds(pl.multiple_of(start + r * tile_size, tile_size), tile_size), :]


def outer_window():
    return 2 * lax.rem(lax.axis_index("tile"), 2)


def fetched_first(i, active, count_s, rows_s, blocks):
    window = rows_s[0, i] - (lax.axis_index("tile") - 1) * blocks
    return active & (i < count_s[0, 0]) & (lax.div(window, blocks) == outer_window())


def open_kernel(blocks, *refs):
    index_refs, (incident, stored, *outer_refs), (pair, tiles) = refs[:3], refs[3:7], refs[7:9]
    rows_s, cols_s, sums, sems, tile_sems = refs[9:]
    slots, tile_size = tiles.shape[0], tiles.shape[-1]
    half = tile_size // 2
    active = lax.axis_index("layer") == 0
    copies = [
        pltpu.make_async_copy(index_refs[0], rows_s, sems.at[0]),
        pltpu.make_async_copy(index_refs[1], cols_s, sems.at[1]),
        pltpu.make_async_copy(incident.at[0], pair.at[0], sems.at[2]),
    ]

    def tile_copy(i):
        return pltpu.make_async_copy(stored.at[0, i], tiles.at[i], tile_sems.at[i])

    for copy in copies:
        copy.start()
    copies[0].wait()
    copies[1].wait()
    first = (lax.axis_index("tile") - 1) * blocks

    @pl.loop(0, slots)
    def _(i):
        pl.when(fetched_first(i, active, index_refs[2], rows_s, blocks))(lambda: tile_copy(i).start())

    @pl.when(active)
    def _():
        sums[...] = jnp.zeros(sums.shape, jnp.float32)

    copies[2].wait()

    @pl.when(active)
    def _():
        for r in range(blocks):
            rows = pl.ds(r * tile_size, tile_size)
            pair[1, rows, :] = turn(pair[0, rows, :].astype(jnp.float32)).astype(jnp.bfloat16)

    @pl.loop(0, slots)
    def _(i):
        @pl.when(fetched_first(i, active, index_refs[2], rows_s, blocks))
        def _():
            tile_copy(i).wait()
            rows = pl.ds(pl.multiple_of(cols_s[0, i] * tile_size, tile_size), tile_size)
            place = lax.rem(rows_s[0, i] - first, blocks)
            target = pl.ds(pl.multiple_of(place * tile_size, tile_size), tile_size)
            term = jnp.dot(tiles[i, 0], pair[0, rows, :], preferred_element_type=jnp.float32)
            term += jnp.dot(tiles[i, 1], pair[1, rows, :], preferred_element_type=jnp.float32)
            sums[target, :] += term

    @pl.when(active)
    def _():
        for r in range(blocks):
            block = sums[pl.ds(r * tile_size, tile_size), :]
            for part in range(PARTS):
                outer_refs[part][pl.ds(r * half, half), :] = pack(block, part).astype(jnp.bfloat16)


def open_products(incident, tiles, index, blocks):
    rows_dev, width = incident.shape[-2:]
    slots, _, tile_size, _ = tiles.shape[-4:]
    outer = pltpu.VMEM((rows_dev // 2, width), jnp.bfloat16)
    return pl.pallas_call(
        functools.partial(open_kernel, blocks),
        out_shape=[
            outer,
            outer,
            pltpu.VMEM((2, rows_dev, width), jnp.bfloat16),
            pltpu.VMEM((slots, 2, tile_size, tile_size), jnp.bfloat16),
            pltpu.SMEM((1, slots), jnp.int32),
            pltpu.SMEM((1, slots), jnp.int32),
        ],
        in_specs=[HBM, HBM, SMEM, HBM, HBM],
        out_specs=[VMEM] * 4 + [SMEM] * 2,
        scratch_shapes=[
            pltpu.VMEM((rows_dev, width), jnp.float32),
            pltpu.SemaphoreType.DMA((3,)),
            pltpu.SemaphoreType.DMA((slots,)),
        ],
        **kernel_options("open", 5 * 10**8, 4 * 10**6, 4),
    )(*index, incident, tiles)


def front_kernel(front, blocks, *refs):
    index_refs, sources, tiles, operand = refs[:3], refs[3], refs[4], refs[5]
    outs, (source_v, sums, sems, *rest) = refs[6 if front else 7 : -4], refs[-4:]
    inner_ref, own_refs, outer_refs = outs[0], outs[1:3], outs[3:]
    active = lax.axis_index("layer") == 0
    if front == 0:
        stored, tiles = refs[6], outs[3]

        @pl.loop(0, tiles.shape[0])
        def _(i):
            done = fetched_first(i, active, index_refs[2], index_refs[0], blocks)
            copy = pltpu.make_async_copy(stored.at[0, i], tiles.at[i], rest[0].at[i])
            pl.when(jnp.logical_not(done))(copy.start)

    pair = operand if front == 0 else rest[0]
    tile_size = tiles.shape[-1]
    rows_dev = pair.shape[1]
    packed = rows_dev // 2
    copies = [pltpu.make_async_copy(sources.at[0, front], source_v, sems.at[0])]
    if front > 0:
        copies.insert(0, pltpu.make_async_copy(operand.at[front], pair.at[0], sems.at[1]))

    @pl.when(active)
    def _():
        for copy in copies:
            copy.start()
        sums[...] = jnp.zeros(sums.shape, jnp.float32)

    if front == 0:

        @pl.loop(0, tiles.shape[0])
        def _(i):
            done = fetched_first(i, active, index_refs[2], index_refs[0], blocks)
            copy = pltpu.make_async_copy(stored.at[0, i], tiles.at[i], rest[0].at[i])
            pl.when(jnp.logical_not(done))(copy.wait)

    @pl.when(active)
    def _():
        if front > 0:
            copies[0].wait()
            for r in range(blocks):
                rows = pl.ds(r * tile_size, tile_size)
                pair[1, rows, :] = turn(pair[0, rows, :].astype(jnp.float32)).astype(jnp.bfloat16)
        accumulate(index_refs, tiles, pair, sums, blocks, outer_window() if front == 0 else None)
        copies[-1].wait()
        inner_start, outer_start = side_starts(rows_dev)
        half = tile_size // 2
        for r in range(blocks):
            own = sums[pl.ds(rows_dev + r * tile_size, tile_size), :]
            own = own + source_v[pl.ds(r * tile_size, tile_size), :].astype(jnp.float32)
            inner = read_block(sums, inner_start, r, tile_size)
            for part in range(PARTS):
                rows = pl.ds(r * half, half)
                own_refs[part][rows, :] = pack(own, part)
                inner_ref[pl.ds(part * packed + r * half, half), :] = pack(inner, part).astype(jnp.bfloat16)
            if front > 0:
                outer = read_block(sums, outer_start, r, tile_size)
                for part in range(PARTS):
                    outer_refs[part][pl.ds(r * half, half), :] = pack(outer, part).astype(jnp.bfloat16)


def kernel_options(name, flops, moved, limit=20):
    return dict(
        compiler_params=pltpu.CompilerParams(vmem_limit_bytes=limit * MIB),
        cost_estimate=pl.CostEstimate(flops=flops, bytes_accessed=moved, transcendentals=0),
        name=name,
    )


def front_products(front, operand, sources, tiles, index, blocks, stored=None):
    rows_dev, width = sources.shape[-2:]
    tile_size = tiles.shape[-1]
    outer = pltpu.VMEM((rows_dev // 2, width), jnp.bfloat16)
    own = pltpu.VMEM((rows_dev // 2, width), jnp.float32)
    outs = [pltpu.VMEM((rows_dev, width), jnp.bfloat16), own, own] + ([outer, outer] if front else [])
    scratch = [
        pltpu.VMEM((rows_dev, width), jnp.bfloat16),
        pltpu.VMEM((3 * rows_dev + tile_size, width), jnp.float32),
        pltpu.SemaphoreType.DMA((2,)),
    ]
    args, specs, aliases = [*index, sources, tiles, operand], [SMEM, SMEM, SMEM, HBM, VMEM], {}
    specs.append(HBM if front else VMEM)
    if front:
        scratch.append(pltpu.VMEM((2, rows_dev, width), jnp.bfloat16))
    else:
        scratch.append(pltpu.SemaphoreType.DMA((tiles.shape[0],)))
        outs.append(pltpu.VMEM(tiles.shape, tiles.dtype))
        args.append(stored)
        specs.append(HBM)
        aliases = {4: 3}
    return pl.pallas_call(
        functools.partial(front_kernel, front, blocks),
        out_shape=outs,
        in_specs=specs,
        input_output_aliases=aliases,
        out_specs=[VMEM] * len(outs),
        scratch_shapes=scratch,
        **kernel_options(f"front_{front}", 10**9, 5 * 10**6, 6),
    )(*args)


def prepare_kernel(wave, front, part, blocks, sources, sums, source_v, sem):
    rows_dev, width = source_v.shape
    tile_size, packed = rows_dev // blocks, rows_dev // 2
    half = tile_size // 2

    @pl.when(lax.axis_index("layer") == wave)
    def _():
        copy = pltpu.make_async_copy(sources.at[0, front], source_v, sem)
        copy.start()
        rest = sums.shape[0] - 2 * packed
        sums[pl.ds(0, packed), :] = jnp.zeros((packed, width), jnp.float32)
        sums[pl.ds(2 * packed, rest), :] = jnp.zeros((rest, width), jnp.float32)
        copy.wait()
        for r in range(blocks):
            source = source_v[pl.ds(r * tile_size, tile_size), :].astype(jnp.float32)
            sums[pl.ds(packed + r * half, half), :] = pack(source, part)


def prepare(wave, front, part, sources, tile_size):
    rows_dev, width = sources.shape[-2:]
    return pl.pallas_call(
        functools.partial(prepare_kernel, wave, front, part, rows_dev // tile_size),
        out_shape=pltpu.VMEM(((3 * rows_dev + tile_size) // 2, width), jnp.float32),
        in_specs=[HBM],
        out_specs=VMEM,
        scratch_shapes=[pltpu.VMEM((rows_dev, width), jnp.bfloat16), pltpu.SemaphoreType.DMA(())],
        **kernel_options(f"prepare_{wave}_{front}_{part}", 10**6, 10**6, 4),
    )(sources)


def chunk_kernel(wave, blocks, *refs):
    rows_s, cols_s, count_s, inbound, tiles, _, outer_ref, inner_ref, sums, operand = refs
    tile_size = tiles.shape[-1]
    packed, width = inbound.shape
    half = tile_size // 2
    first = quarters((half, width))

    @pl.when(lax.axis_index("layer") == wave)
    def _():
        for r in range(blocks):
            value = inbound[pl.ds(r * half, half), :].astype(jnp.float32)
            for j, given in enumerate((value, turn(value))):
                upper = jnp.where(first, given, 0.0)
                lower = jnp.where(first, 0.0, given)
                parts = (
                    upper,
                    pltpu.roll(lower, width - width // 4, 1),
                    pltpu.roll(upper, width // 4, 1),
                    lower,
                )
                for k, part in enumerate(parts):
                    rows = pl.ds((8 * r + 4 * j + k) * half, half)
                    operand[rows, :] = part.astype(jnp.bfloat16)
        start = (lax.axis_index("tile") - 1) * blocks
        count = count_s[0, 0]
        for i in range(tiles.shape[0]):
            live = i < count
            row = jnp.where(live, rows_s[0, i] - start, 3 * blocks)
            column = jnp.where(live, cols_s[0, i], 0)
            rows = pl.ds(pl.multiple_of(column * 4 * tile_size, tile_size), 4 * tile_size)
            target = pl.ds(pl.multiple_of(row * half, half), half)
            left = jnp.concatenate(
                [tiles[i, j, pl.ds(k * half, half), :] for j in range(2) for k in range(2)], axis=1
            )
            sums[target, :] += jnp.dot(left, operand[rows, :], preferred_element_type=jnp.float32)
        inner_start, outer_start = side_starts(packed)
        for ref, begin in ((outer_ref, outer_start), (inner_ref, inner_start)):
            for r in range(blocks):
                ref[pl.ds(r * half, half), :] = read_block(sums, begin, r, half).astype(jnp.bfloat16)


def chunk_products(wave, front, part, inbound, tiles, sums, index, blocks):
    tile_size = tiles.shape[-1]
    packed, width = inbound.shape
    payload = pltpu.VMEM((packed, width), jnp.bfloat16)
    return pl.pallas_call(
        functools.partial(chunk_kernel, wave, blocks),
        out_shape=[payload, payload, pltpu.VMEM(sums.shape, sums.dtype)],
        in_specs=[SMEM, SMEM, SMEM, VMEM, VMEM, VMEM],
        out_specs=[VMEM] * 3,
        scratch_shapes=[pltpu.VMEM((4 * blocks * tile_size, width), jnp.bfloat16)],
        input_output_aliases={5: 2},
        **kernel_options(f"chunk_{wave}_{front}_{part}", 10**9, 5 * 10**6, 4),
    )(*index, inbound, tiles, sums)


def combine_kernel(wave, part, has_through, final, *refs):
    own_ref, inner_ref, outer_ref = refs[:3]
    packed, width = outer_ref.shape
    own_rows = pl.ds(packed if own_ref.shape[0] > packed else 0, packed)
    inner_rows = pl.ds(part * packed if inner_ref.shape[0] > packed else 0, packed)
    total = own_ref[own_rows, :] + inner_ref[inner_rows, :].astype(jnp.float32) + outer_ref[...].astype(jnp.float32)
    if wave > 0:
        active = lax.axis_index("layer") == wave
        total = jnp.where(active, total, refs[3][...].astype(jnp.float32))
    if not (final and part == PARTS - 1):
        out_ref = refs[-2] if has_through else refs[-1]
        out_ref[...] = total.astype(jnp.bfloat16)
        return
    front, blocks, half = final
    out_ref, staged, sems = refs[-3:]
    low, high = refs[4][...].astype(jnp.float32), total
    first = quarters((half, width))
    copies = []
    for r in range(blocks):
        a, b = low[r * half : (r + 1) * half], high[r * half : (r + 1) * half]
        upper = jnp.where(first, a, pltpu.roll(b, width // 4, 1))
        lower = jnp.where(first, pltpu.roll(a, width - width // 4, 1), b)
        staged[pl.ds(2 * r * half, half), :] = upper.astype(jnp.bfloat16)
        staged[pl.ds((2 * r + 1) * half, half), :] = lower.astype(jnp.bfloat16)
        rows = pl.ds(2 * r * half, 2 * half)
        copies.append(pltpu.make_async_copy(staged.at[rows, :], out_ref.at[0, front, rows, :], sems.at[r]))
        copies[-1].start()
    for copy in copies:
        copy.wait()


def combine(wave, front, part, own, inner, outer, earlier=None, through=None, final=None, partner=None, result=None, fronts=0):
    packed, width = outer.shape
    args, specs, aliases, scratch = [own, inner, outer], [VMEM] * 3, {}, []
    if wave > 0:
        args.append(earlier)
        specs.append(VMEM)
    outs, out_specs = [pltpu.VMEM((packed, width), jnp.bfloat16)], [VMEM]
    if through is not None:
        aliases = {len(args): 1}
        args.append(through)
        specs.append(VMEM)
        outs.append(pltpu.VMEM(through.shape, through.dtype))
        out_specs.append(VMEM)
    if final and part == PARTS - 1:
        final = (front, *final)
        args.append(partner)
        specs.append(VMEM)
        outs = [jax.ShapeDtypeStruct((1, fronts, 2 * packed, width), jnp.bfloat16)]
        out_specs = [HBM]
        scratch = [pltpu.VMEM((2 * packed, width), jnp.bfloat16), pltpu.SemaphoreType.DMA((final[1],))]
        if result is not None:
            aliases = {len(args): 0}
            args.append(result)
            specs.append(HBM)
    return pl.pallas_call(
        functools.partial(combine_kernel, wave, part, through is not None, final),
        out_shape=outs,
        in_specs=specs,
        out_specs=out_specs,
        scratch_shapes=scratch,
        input_output_aliases=aliases,
        **kernel_options(f"combine_{wave}_{front}_{part}", 10**6, 10**6, 8),
    )(*args)


def shards(incident, sources, green_tiles, tile_rows, tile_cols, tile_count):
    depth, devices = lax.axis_size("layer"), lax.axis_size("tile")
    layer_route = down_route(depth)
    fronts, rows_dev, _ = incident.shape
    tile_size = green_tiles.shape[-1]
    blocks = rows_dev // tile_size
    index = (in_hbm(tile_rows), in_hbm(tile_cols), tile_count)
    incident, sources, green_tiles = map(in_hbm, (incident, sources, green_tiles))

    def across(payload, wave):
        return lax.ppermute(payload, ("layer", "tile"), outer_route(wave, depth, devices))

    def beside(payload):
        return lax.ppermute(payload, "tile", inner_route(devices))

    def down(payload):
        return lax.ppermute(payload, "layer", layer_route)

    def total(wave, chunk, *args, **kwargs):
        return combine(wave, chunk // PARTS, chunk % PARTS, *args, **kwargs)

    first = open_products(incident, green_tiles, index, blocks)
    payloads, held = list(first[:PARTS]), first[3]
    index = (*first[4:], tile_count)
    chunks = []
    for front in range(fronts):
        operand = incident if front else first[2]
        made = front_products(front, operand, sources, held, index, blocks, green_tiles)
        if front == 0:
            held, made = made[3], made[:3]
        inner = beside(made[0])
        payloads += made[3:]
        chunks += [[made[1 + part], inner, None] for part in range(PARTS)]
    for c in range(min(PARTS + 1, len(chunks))):
        chunks[c][2] = across(payloads[c], 0)
    passed, leaving = [], []
    for c in range(len(chunks)):
        behind = c + PARTS
        through = payloads[behind] if PARTS < behind < len(chunks) else None
        made = total(0, c, *chunks[c], through=through)
        if through is not None:
            chunks[behind][2] = across(made[1], 0)
        leaving.append(made[0])
        if depth > 1:
            passed.append(down(made[0]))
    for wave in range(1, depth):
        final = wave == depth - 1
        chunks = []
        for c, inbound in enumerate(passed):
            sums = prepare(wave, c // PARTS, c % PARTS, sources, tile_size)
            outer, inner, own = chunk_products(
                wave, c // PARTS, c % PARTS, inbound, held, sums, index, blocks
            )
            chunks.append((own, beside(inner), across(outer, wave)))
        if final:
            break
        leaving = [total(wave, c, *chunk, leaving[c])[0] for c, chunk in enumerate(chunks)]
        passed = [down(chunk) for chunk in leaving]
    result = partner = None
    for c, chunk in enumerate(chunks):
        (out,) = total(
            depth - 1, c, *chunk, leaving[c],
            final=(blocks, tile_size // 2), partner=partner, result=result, fronts=fronts,
        )
        partner = out
        if c % PARTS == PARTS - 1:
            result = out
    return result


def solution(mesh):
    return jax.shard_map(
        shards,
        mesh=mesh,
        in_specs=(
            P(None, "tile", None),
            P("layer", None, "tile", None),
            P("layer", "tile", None, None, None),
            P("layer", "tile"),
            P("layer", "tile"),
            P("layer", "tile"),
        ),
        out_specs=P("layer", None, "tile", None),
        check_vma=False,
    )
```
